128 devices in a mesh: gx: 8 (over x, core), gy: 16 (over z, y).
Axes of the slice: x: 4, y: 4, z: 4, core: 2. Of those that a mesh axis runs over, the one named last changes fastest.
Arguments:
- parent_fields: float32 [5, 4, 384, 6144], P(None, None, 'gx', 'gy'), may hold values from -6 to 6
- parent_velocity: float32 [2, 4, 384, 6144], P(None, None, 'gx', 'gy'), may hold values from -0.3 to 0.3
- parent_mixing: float32 [4, 384, 6144], P(None, 'gx', 'gy'), may hold values from 0.01 to 0.1
- nest_fields: float32 [5, 4, 384, 6144], P(None, None, 'gx', 'gy'), may hold values from -6 to 6
- nest_velocity: float32 [2, 4, 384, 6144], P(None, None, 'gx', 'gy'), may hold values from -0.3 to 0.3
- nest_mixing: float32 [4, 384, 6144], P(None, 'gx', 'gy'), may hold values from 0.01 to 0.1
- nest_anchor: int32 [2], replicated, may hold values from 1 to 3327, as said below
Outputs:
- parent_result: float32 [5, 4, 384, 6144], P(None, None, 'gx', 'gy')
- nest_result: float32 [5, 4, 384, 6144], P(None, None, 'gx', 'gy')
The draws below stay inside these ranges and needn't reach their ends.
Inputs may be any that keep to these rules, and one draw needn't show every extreme that they name: `nest_anchor`: the row anchor is 1 to 254; the column anchor is 3073 to 3327, so the nest with a rim of one parent cell lies inside the parent grid.
All inputs are finite; a program needn't handle non-finite values.
Results may differ from the reference program's by a relative error of at most 0.00002.
Values sent between devices are 32-bit elements; how exact they have to be, the bound alone decides.
A program may use at most 192 MiB of HBM per device.

```python
import math
import jax
import jax.numpy as jnp
from jax import lax

FIELDS = 5
LEVELS = 4
SUBSTEPS = 3
FY = 128
PY = 384
PARENT_ROWS = 384
PARENT_COLS = 6144
NEST_ROWS = 384
NEST_COLS = 6144


def draw_nest_anchor(key, part):
    row_key = jax.random.fold_in(key, 11)
    column_key = jax.random.fold_in(key, 23)
    row_limit = PARENT_ROWS - NEST_ROWS // 3 - 1
    column_start = PARENT_COLS // 2 + 1
    column_limit = PARENT_COLS // 2 + PY - FY
    row_anchor = jax.random.randint(row_key, (1,), 1, row_limit, dtype=jnp.int32)
    column_anchor = jax.random.randint(column_key, (1,), column_start, column_limit, dtype=jnp.int32)
    return jnp.concatenate((row_anchor, column_anchor)).astype(jnp.int32)


def block_scale(rng, shape, shards, least, largest):
    factor_of = 1.0
    for axis_at, blocks in shards:
        draws = jax.random.uniform(jax.random.fold_in(jax.random.fold_in(rng, 6), axis_at), (blocks,), jnp.float32, least / len(shards), largest / len(shards))
        factor_of = factor_of * jnp.repeat(jnp.exp(draws), shape[axis_at] // blocks).reshape((-1,) + (1,) * (len(shape) - 1 - axis_at))
    return factor_of


def gaussian(own_key, shape, spread, most, shards=(), held_as=jnp.bfloat16):
    values = jax.random.normal(own_key, shape, jnp.float32) * spread
    if len(shards) > 0:
        values = block_scale(own_key, shape, shards, -0.22, 0.18) * values
    return jnp.clip(values, min=-most, max=most).astype(held_as)


def setup_inputs(seed: int = 0) -> dict:
    keys = jax.random.split(jax.random.key(seed), 8)
    parent_fields = gaussian(keys[0], (FIELDS, LEVELS, PARENT_ROWS, PARENT_COLS), 1.0, 6.0, ((2, 8), (3, 16)), jnp.float32)
    parent_velocity = jnp.clip(jax.random.uniform(keys[1], (2, LEVELS, PARENT_ROWS, PARENT_COLS), jnp.float32, -0.3, 0.3) * block_scale(keys[1], (2, LEVELS, PARENT_ROWS, PARENT_COLS), ((2, 8), (3, 16)), -0.4, 0.0), -0.3, 0.3)
    parent_mixing = jnp.clip(jnp.exp(math.log(0.1) - 2.3025851 * jax.random.uniform(keys[2], (LEVELS, PARENT_ROWS, PARENT_COLS), jnp.float32) ** block_scale(keys[2], (LEVELS, PARENT_ROWS, PARENT_COLS), ((1, 8), (2, 16)), -0.2, 0.2)), 0.01, 0.1)
    nest_fields = gaussian(keys[3], (FIELDS, LEVELS, NEST_ROWS, NEST_COLS), 1.0, 6.0, ((2, 8), (3, 16)), jnp.float32)
    nest_velocity = jnp.clip(jax.random.uniform(keys[4], (2, LEVELS, NEST_ROWS, NEST_COLS), jnp.float32, -0.3, 0.3) * block_scale(keys[4], (2, LEVELS, NEST_ROWS, NEST_COLS), ((2, 8), (3, 16)), -0.4, 0.0), -0.3, 0.3)
    nest_mixing = jnp.clip(jnp.exp(math.log(0.1) - 2.3025851 * jax.random.uniform(keys[5], (LEVELS, NEST_ROWS, NEST_COLS), jnp.float32) ** block_scale(keys[5], (LEVELS, NEST_ROWS, NEST_COLS), ((1, 8), (2, 16)), -0.2, 0.2)), 0.01, 0.1)
    nest_anchor = draw_nest_anchor(jax.random.fold_in(keys[7], 71), 0)
    return {"parent_fields": parent_fields, "parent_velocity": parent_velocity, "parent_mixing": parent_mixing, "nest_fields": nest_fields, "nest_velocity": nest_velocity, "nest_mixing": nest_mixing, "nest_anchor": nest_anchor}


third = 1.0 / 3.0
two_thirds = 2.0 / 3.0
nudge_floor = 0.1
relax_width = 4.0


def update(values, padded, velocity, mixing):
    western = padded[:, :, :-2, 1:-1]
    eastern = padded[:, :, 2:, 1:-1]
    southern = padded[:, :, 1:-1, :-2]
    northern = padded[:, :, 1:-1, 2:]
    along_rows = velocity[0]
    along_columns = velocity[1]
    upwind = (jnp.maximum(along_rows, 0.0) * (values - western)
              + jnp.minimum(along_rows, 0.0) * (eastern - values)
              + jnp.maximum(along_columns, 0.0) * (values - southern)
              + jnp.minimum(along_columns, 0.0) * (northern - values))
    return values - upwind + mixing * (eastern + western + northern + southern - 4.0 * values)


def advance(values, velocity, mixing):
    padded = jnp.pad(values, ((0, 0), (0, 0), (1, 1), (1, 1)))
    return update(values, padded, velocity, mixing)


def refine_rows(block):
    lower = block[:, :, :-2]
    centre = block[:, :, 1:-1]
    upper = block[:, :, 2:]
    stacked = jnp.stack((third * lower + two_thirds * centre, centre, two_thirds * centre + third * upper), axis=3)
    extent = centre.shape
    return stacked.reshape(extent[0], extent[1], 3 * extent[2], extent[3])


def refine_columns(block):
    lower = block[:, :, :, :-2]
    centre = block[:, :, :, 1:-1]
    upper = block[:, :, :, 2:]
    stacked = jnp.stack((third * lower + two_thirds * centre, centre, two_thirds * centre + third * upper), axis=4)
    extent = centre.shape
    return stacked.reshape(extent[0], extent[1], extent[2], 3 * extent[3])


def block_mean(state):
    extent = state.shape
    grouped = state.reshape(extent[0], extent[1], extent[2] // 3, 3, extent[3] // 3, 3)
    return jnp.sum(grouped, axis=(3, 5)) / 9.0


def relax_weight(row_global, column_global, total_rows, total_columns):
    row_distance = jnp.minimum(row_global, total_rows - 1 - row_global)
    column_distance = jnp.minimum(column_global, total_columns - 1 - column_global)
    distance = jnp.minimum(row_distance[:, None], column_distance[None, :]).astype(jnp.float32)
    return nudge_floor + (1.0 - nudge_floor) * jnp.exp(-distance / relax_width)


def reference(parent_fields, parent_velocity, parent_mixing, nest_fields, nest_velocity, nest_mixing, nest_anchor):
    parent_next = advance(parent_fields, parent_velocity, parent_mixing)
    fields_count = parent_fields.shape[0]
    levels_count = parent_fields.shape[1]
    nest_rows = nest_fields.shape[2]
    nest_columns = nest_fields.shape[3]
    span_rows = nest_rows // 3
    span_columns = nest_columns // 3
    zero_index = jnp.zeros((), jnp.int32)
    row_anchor = nest_anchor[0].astype(jnp.int32)
    column_anchor = nest_anchor[1].astype(jnp.int32)
    relay = lax.dynamic_slice(parent_next, (zero_index, zero_index, (row_anchor - 1).astype(jnp.int32), (column_anchor - 1).astype(jnp.int32)),
                              (fields_count, levels_count, span_rows + 2, span_columns + 2))
    forcing = refine_columns(refine_rows(relay))
    weight = relax_weight(jnp.arange(nest_rows, dtype=jnp.int32), jnp.arange(nest_columns, dtype=jnp.int32), nest_rows, nest_columns)
    state = nest_fields
    for substep in range(SUBSTEPS):
        moved = advance(state, nest_velocity, nest_mixing)
        state = moved + weight * (forcing - moved)
    coarse = block_mean(state)
    parent_result = lax.dynamic_update_slice(parent_next, coarse, (zero_index, zero_index, row_anchor, column_anchor))
    return parent_result, state
```

```python
import jax
import jax.numpy as jnp
from jax import lax
from jax.sharding import PartitionSpec as P

SUBSTEPS = 3


third = 1.0 / 3.0
two_thirds = 2.0 / 3.0
nudge_floor = 0.1
relax_width = 4.0


def shift_pairs(count, step):
    return [(i, i + step) for i in range(count) if 0 <= i + step < count]


def neighbours(cells):
    rows = lax.axis_size("gx")
    cols = lax.axis_size("gy")
    western = lax.ppermute(cells[:, :, -1:, :], "gx", shift_pairs(rows, 1))
    eastern = lax.ppermute(cells[:, :, :1, :], "gx", shift_pairs(rows, -1))
    southern = lax.ppermute(cells[:, :, :, -1:], "gy", shift_pairs(cols, 1))
    northern = lax.ppermute(cells[:, :, :, :1], "gy", shift_pairs(cols, -1))
    return western, eastern, southern, northern


def update(values, halo, velocity, mixing):
    west_row, east_row, south_col, north_col = halo
    western = jnp.concatenate([west_row, values[:, :, :-1, :]], axis=2)
    eastern = jnp.concatenate([values[:, :, 1:, :], east_row], axis=2)
    southern = jnp.concatenate([south_col, values[:, :, :, :-1]], axis=3)
    northern = jnp.concatenate([values[:, :, :, 1:], north_col], axis=3)
    along_rows = velocity[0]
    along_columns = velocity[1]
    upwind = (
        jnp.maximum(along_rows, 0.0) * (values - western)
        + jnp.minimum(along_rows, 0.0) * (eastern - values)
        + jnp.maximum(along_columns, 0.0) * (values - southern)
        + jnp.minimum(along_columns, 0.0) * (northern - values)
    )
    return values - upwind + mixing * (eastern + western + northern + southern - 4.0 * values)


def refine_rows(block):
    lower = block[:, :, :-2]
    centre = block[:, :, 1:-1]
    upper = block[:, :, 2:]
    stacked = jnp.stack(
        (third * lower + two_thirds * centre, centre, two_thirds * centre + third * upper), axis=3
    )
    extent = centre.shape
    return stacked.reshape(extent[0], extent[1], 3 * extent[2], extent[3])


def refine_columns(block):
    lower = block[:, :, :, :-2]
    centre = block[:, :, :, 1:-1]
    upper = block[:, :, :, 2:]
    stacked = jnp.stack(
        (third * lower + two_thirds * centre, centre, two_thirds * centre + third * upper), axis=4
    )
    extent = centre.shape
    return stacked.reshape(extent[0], extent[1], extent[2], 3 * extent[3])


def block_mean(state):
    extent = state.shape
    grouped = state.reshape(extent[0], extent[1], extent[2] // 3, 3, extent[3] // 3, 3)
    return jnp.sum(grouped, axis=(3, 5)) / 9.0


def relax_weight(row_global, column_global, total_rows, total_columns):
    row_distance = jnp.minimum(row_global, total_rows - 1 - row_global)
    column_distance = jnp.minimum(column_global, total_columns - 1 - column_global)
    distance = jnp.minimum(row_distance[:, None], column_distance[None, :]).astype(jnp.float32)
    return nudge_floor + (1.0 - nudge_floor) * jnp.exp(-distance / relax_width)


def within(positions, limit):
    return (positions >= 0) & (positions < limit)


def column_pairs(count, base, ratio, k, extra):
    pairs = []
    for m in range(count):
        j = ratio * m + k
        p = base + m + extra
        if j < count and p < count:
            pairs.append((p, j))
    return pairs


def per_device(
    parent_fields,
    parent_velocity,
    parent_mixing,
    nest_fields,
    nest_velocity,
    nest_mixing,
    nest_anchor,
):
    row_rank = lax.axis_index("gx")
    column_rank = lax.axis_index("gy")
    row_devices = lax.axis_size("gx")
    column_devices = lax.axis_size("gy")
    parent_rows = parent_fields.shape[2]
    parent_columns = parent_fields.shape[3]
    nest_rows = nest_fields.shape[2]
    nest_columns = nest_fields.shape[3]
    span_rows = nest_rows // 3
    span_columns = nest_columns // 3
    ratio = parent_columns // span_columns
    base = column_devices // 2
    base_column = base * parent_columns
    relay_rows = span_rows + 2
    relay_columns = span_columns + 2
    row_anchor = nest_anchor[0]
    column_anchor = nest_anchor[1]
    offset = column_anchor - 1 - base_column

    parent_next = update(
        parent_fields, neighbours(parent_fields), parent_velocity, parent_mixing
    )

    margin = parent_columns - span_columns
    wide = jnp.pad(parent_next, ((0, 0), (0, 0), (0, 0), (margin, margin)))
    relay_cols = None
    for k in range(ratio):
        for extra in (0, 1):
            if extra == 1 and k == 0:
                continue
            start = margin + span_columns * k + offset - extra * parent_columns
            piece = lax.dynamic_slice_in_dim(wide, start, relay_columns, axis=3)
            moved = lax.ppermute(
                piece, "gy", column_pairs(column_devices, base, ratio, k, extra)
            )
            relay_cols = moved if relay_cols is None else relay_cols + moved

    padded = jnp.pad(relay_cols, ((0, 0), (0, 0), (relay_rows, relay_rows), (0, 0)))
    slots = []
    for target in range(row_devices):
        first = row_anchor - 1 + span_rows * target - parent_rows * row_rank
        first = jnp.clip(first, -relay_rows, parent_rows) + relay_rows
        slots.append(lax.dynamic_slice_in_dim(padded, first, relay_rows, axis=2))
    stacked = jnp.stack(slots, axis=0)
    relay = lax.psum_scatter(stacked, "gx", scatter_dimension=0, tiled=True)[0]

    forcing = refine_columns(refine_rows(relay))
    row_global = row_rank * nest_rows + jnp.arange(nest_rows, dtype=jnp.int32)
    column_global = column_rank * nest_columns + jnp.arange(nest_columns, dtype=jnp.int32)
    weight = relax_weight(
        row_global, column_global, row_devices * nest_rows, column_devices * nest_columns
    )
    state = nest_fields
    for substep in range(SUBSTEPS):
        moved = update(state, neighbours(state), nest_velocity, nest_mixing)
        state = moved + weight * (forcing - moved)

    coarse = block_mean(state)
    gathered = lax.all_gather(coarse, "gx", axis=2, tiled=True)
    total_span = row_devices * span_rows
    gathered = jnp.pad(gathered, ((0, 0), (0, 0), (parent_rows, parent_rows), (0, 0)))
    first = jnp.clip(parent_rows * row_rank - row_anchor, -parent_rows, total_span)
    strip = lax.dynamic_slice_in_dim(gathered, first + parent_rows, parent_rows, axis=2)

    pieces = []
    for extra in (1, 0):
        for k in range(ratio):
            if extra == 1 and k == 0:
                continue
            pairs = [(j, p) for (p, j) in column_pairs(column_devices, base, ratio, k, extra)]
            pieces.append(lax.ppermute(strip, "gy", pairs))
    joined = jnp.concatenate(pieces, axis=3)
    start = (ratio - 1) * span_columns - 1 - offset
    fed_back = lax.dynamic_slice_in_dim(joined, start, parent_columns, axis=3)

    relative_rows = row_rank * parent_rows + jnp.arange(parent_rows, dtype=jnp.int32) - row_anchor
    relative_columns = (
        column_rank * parent_columns + jnp.arange(parent_columns, dtype=jnp.int32) - column_anchor
    )
    rows_valid = within(relative_rows, total_span)
    columns_valid = within(relative_columns, column_devices * span_columns)
    covered = rows_valid[:, None] & columns_valid[None, :]
    parent_result = jnp.where(covered, fed_back, parent_next)
    return (parent_result, state)


def solution(mesh):
    placed = (
        P(None, None, "gx", "gy"),
        P(None, None, "gx", "gy"),
        P(None, "gx", "gy"),
        P(None, None, "gx", "gy"),
        P(None, None, "gx", "gy"),
        P(None, "gx", "gy"),
        P(),
    )
    return jax.shard_map(
        per_device,
        mesh=mesh,
        in_specs=placed,
        out_specs=(P(None, None, "gx", "gy"), P(None, None, "gx", "gy")),
        check_vma=False,
    )
```

```python
import jax
import jax.numpy as jnp
from jax import lax
from jax.sharding import PartitionSpec as P

SUBSTEPS = 3


third = 1.0 / 3.0
two_thirds = 2.0 / 3.0
nudge_floor = 0.1
relax_width = 4.0


def shift_pairs(count, step):
    return [(i, i + step) for i in range(count) if 0 <= i + step < count]


def neighbours(cells):
    rows = lax.axis_size("gx")
    cols = lax.axis_size("gy")
    western = lax.ppermute(cells[:, :, -1:, :], "gx", shift_pairs(rows, 1))
    eastern = lax.ppermute(cells[:, :, :1, :], "gx", shift_pairs(rows, -1))
    southern = lax.ppermute(cells[:, :, :, -1:], "gy", shift_pairs(cols, 1))
    northern = lax.ppermute(cells[:, :, :, :1], "gy", shift_pairs(cols, -1))
    return western, eastern, southern, northern


def update(values, halo, velocity, mixing):
    west_row, east_row, south_col, north_col = halo
    western = jnp.concatenate([west_row, values[:, :, :-1, :]], axis=2)
    eastern = jnp.concatenate([values[:, :, 1:, :], east_row], axis=2)
    southern = jnp.concatenate([south_col, values[:, :, :, :-1]], axis=3)
    northern = jnp.concatenate([values[:, :, :, 1:], north_col], axis=3)
    along_rows = velocity[0]
    along_columns = velocity[1]
    upwind = (
        jnp.maximum(along_rows, 0.0) * (values - western)
        + jnp.minimum(along_rows, 0.0) * (eastern - values)
        + jnp.maximum(along_columns, 0.0) * (values - southern)
        + jnp.minimum(along_columns, 0.0) * (northern - values)
    )
    return values - upwind + mixing * (eastern + western + northern + southern - 4.0 * values)


def refine_rows(block):
    lower = block[:, :, :-2]
    centre = block[:, :, 1:-1]
    upper = block[:, :, 2:]
    stacked = jnp.stack(
        (third * lower + two_thirds * centre, centre, two_thirds * centre + third * upper), axis=3
    )
    extent = centre.shape
    return stacked.reshape(extent[0], extent[1], 3 * extent[2], extent[3])


def refine_columns(block):
    lower = block[:, :, :, :-2]
    centre = block[:, :, :, 1:-1]
    upper = block[:, :, :, 2:]
    stacked = jnp.stack(
        (third * lower + two_thirds * centre, centre, two_thirds * centre + third * upper), axis=4
    )
    extent = centre.shape
    return stacked.reshape(extent[0], extent[1], extent[2], 3 * extent[3])


def grouping(count):
    rows = jnp.arange(count, dtype=jnp.int32)[:, None] // 3
    return (rows == jnp.arange(count // 3, dtype=jnp.int32)[None, :]).astype(jnp.float32)


def block_mean(state):
    extent = state.shape
    exact = lax.Precision.HIGHEST
    across = jnp.einsum("flrc,cb->flrb", state, grouping(extent[3]), precision=exact)
    down = jnp.einsum("ra,flrb->flab", grouping(extent[2]), across, precision=exact)
    return down / 9.0


def relax_weight(row_global, column_global, total_rows, total_columns):
    row_distance = jnp.minimum(row_global, total_rows - 1 - row_global)
    column_distance = jnp.minimum(column_global, total_columns - 1 - column_global)
    distance = jnp.minimum(row_distance[:, None], column_distance[None, :]).astype(jnp.float32)
    return nudge_floor + (1.0 - nudge_floor) * jnp.exp(-distance / relax_width)


def within(positions, limit):
    return (positions >= 0) & (positions < limit)


def column_pairs(count, base, ratio, k, extra):
    pairs = []
    for m in range(count):
        j = ratio * m + k
        p = base + m + extra
        if j < count and p < count:
            pairs.append((p, j))
    return pairs


def per_device(
    parent_fields,
    parent_velocity,
    parent_mixing,
    nest_fields,
    nest_velocity,
    nest_mixing,
    nest_anchor,
):
    row_rank = lax.axis_index("gx")
    column_rank = lax.axis_index("gy")
    row_devices = lax.axis_size("gx")
    column_devices = lax.axis_size("gy")
    parent_rows = parent_fields.shape[2]
    parent_columns = parent_fields.shape[3]
    nest_rows = nest_fields.shape[2]
    nest_columns = nest_fields.shape[3]
    span_rows = nest_rows // 3
    span_columns = nest_columns // 3
    ratio = parent_columns // span_columns
    base = column_devices // 2
    base_column = base * parent_columns
    relay_rows = span_rows + 2
    relay_columns = span_columns + 2
    row_anchor = nest_anchor[0]
    column_anchor = nest_anchor[1]
    offset = column_anchor - 1 - base_column

    parent_next = update(
        parent_fields, neighbours(parent_fields), parent_velocity, parent_mixing
    )

    margin = parent_columns - span_columns
    wide = jnp.pad(parent_next, ((0, 0), (0, 0), (0, 0), (margin, margin)))
    relay_cols = None
    for k in range(ratio):
        for extra in (0, 1):
            if extra == 1 and k == 0:
                continue
            start = margin + span_columns * k + offset - extra * parent_columns
            piece = lax.dynamic_slice_in_dim(wide, start, relay_columns, axis=3)
            moved = lax.ppermute(
                piece, "gy", column_pairs(column_devices, base, ratio, k, extra)
            )
            relay_cols = moved if relay_cols is None else relay_cols + moved

    padded = jnp.pad(relay_cols, ((0, 0), (0, 0), (relay_rows, relay_rows), (0, 0)))
    slots = []
    for target in range(row_devices):
        first = row_anchor - 1 + span_rows * target - parent_rows * row_rank
        first = jnp.clip(first, -relay_rows, parent_rows) + relay_rows
        slots.append(lax.dynamic_slice_in_dim(padded, first, relay_rows, axis=2))
    stacked = jnp.stack(slots, axis=0)
    received = lax.all_to_all(stacked, "gx", split_axis=0, concat_axis=0, tiled=True)
    relay = jnp.sum(received, axis=0)

    forcing = refine_columns(refine_rows(relay))
    row_global = row_rank * nest_rows + jnp.arange(nest_rows, dtype=jnp.int32)
    column_global = column_rank * nest_columns + jnp.arange(nest_columns, dtype=jnp.int32)
    weight = relax_weight(
        row_global, column_global, row_devices * nest_rows, column_devices * nest_columns
    )
    state = nest_fields
    for substep in range(SUBSTEPS):
        moved = update(state, neighbours(state), nest_velocity, nest_mixing)
        state = moved + weight * (forcing - moved)

    coarse = block_mean(state)
    gathered = lax.all_gather(coarse, "gx", axis=2, tiled=True)
    total_span = row_devices * span_rows
    gathered = jnp.pad(gathered, ((0, 0), (0, 0), (parent_rows, parent_rows), (0, 0)))
    first = jnp.clip(parent_rows * row_rank - row_anchor, -parent_rows, total_span)
    strip = lax.dynamic_slice_in_dim(gathered, first + parent_rows, parent_rows, axis=2)

    pieces = []
    for extra in (1, 0):
        for k in range(ratio):
            if extra == 1 and k == 0:
                continue
            pairs = [(j, p) for (p, j) in column_pairs(column_devices, base, ratio, k, extra)]
            pieces.append(lax.ppermute(strip, "gy", pairs))
    joined = jnp.concatenate(pieces, axis=3)
    start = (ratio - 1) * span_columns - 1 - offset
    fed_back = lax.dynamic_slice_in_dim(joined, start, parent_columns, axis=3)

    relative_rows = row_rank * parent_rows + jnp.arange(parent_rows, dtype=jnp.int32) - row_anchor
    relative_columns = (
        column_rank * parent_columns + jnp.arange(parent_columns, dtype=jnp.int32) - column_anchor
    )
    rows_valid = within(relative_rows, total_span)
    columns_valid = within(relative_columns, column_devices * span_columns)
    covered = rows_valid[:, None] & columns_valid[None, :]
    parent_result = jnp.where(covered, fed_back, parent_next)
    return (parent_result, state)


def solution(mesh):
    placed = (
        P(None, None, "gx", "gy"),
        P(None, None, "gx", "gy"),
        P(None, "gx", "gy"),
        P(None, None, "gx", "gy"),
        P(None, None, "gx", "gy"),
        P(None, "gx", "gy"),
        P(),
    )
    return jax.shard_map(
        per_device,
        mesh=mesh,
        in_specs=placed,
        out_specs=(P(None, None, "gx", "gy"), P(None, None, "gx", "gy")),
        check_vma=False,
    )
```

```python
import jax
import jax.numpy as jnp
from jax import lax
from jax.experimental import pallas as pl
from jax.experimental.pallas import tpu as pltpu
from jax.sharding import PartitionSpec as P

MESH = pl.DeviceIdType.MESH

SUBSTEPS = 3


third = 1.0 / 3.0
two_thirds = 2.0 / 3.0
nudge_floor = 0.1
relax_width = 4.0


def shift_pairs(count, step):
    return [(i, i + step) for i in range(count) if 0 <= i + step < count]


def neighbours(cells):
    rows = lax.axis_size("gx")
    cols = lax.axis_size("gy")
    western = lax.ppermute(cells[:, :, -1:, :], "gx", shift_pairs(rows, 1))
    eastern = lax.ppermute(cells[:, :, :1, :], "gx", shift_pairs(rows, -1))
    southern = lax.ppermute(cells[:, :, :, -1:], "gy", shift_pairs(cols, 1))
    northern = lax.ppermute(cells[:, :, :, :1], "gy", shift_pairs(cols, -1))
    return western, eastern, southern, northern


def update(values, halo, velocity, mixing):
    west_row, east_row, south_col, north_col = halo
    western = jnp.concatenate([west_row, values[:, :, :-1, :]], axis=2)
    eastern = jnp.concatenate([values[:, :, 1:, :], east_row], axis=2)
    southern = jnp.concatenate([south_col, values[:, :, :, :-1]], axis=3)
    northern = jnp.concatenate([values[:, :, :, 1:], north_col], axis=3)
    along_rows = velocity[0]
    along_columns = velocity[1]
    upwind = (
        jnp.maximum(along_rows, 0.0) * (values - western)
        + jnp.minimum(along_rows, 0.0) * (eastern - values)
        + jnp.maximum(along_columns, 0.0) * (values - southern)
        + jnp.minimum(along_columns, 0.0) * (northern - values)
    )
    return values - upwind + mixing * (eastern + western + northern + southern - 4.0 * values)


def refine_rows(block):
    lower = block[:, :, :-2]
    centre = block[:, :, 1:-1]
    upper = block[:, :, 2:]
    stacked = jnp.stack(
        (third * lower + two_thirds * centre, centre, two_thirds * centre + third * upper), axis=3
    )
    extent = centre.shape
    return stacked.reshape(extent[0], extent[1], 3 * extent[2], extent[3])


def refine_columns(block):
    lower = block[:, :, :, :-2]
    centre = block[:, :, :, 1:-1]
    upper = block[:, :, :, 2:]
    stacked = jnp.stack(
        (third * lower + two_thirds * centre, centre, two_thirds * centre + third * upper), axis=4
    )
    extent = centre.shape
    return stacked.reshape(extent[0], extent[1], extent[2], 3 * extent[3])


def grouping(count):
    rows = jnp.arange(count, dtype=jnp.int32)[:, None] // 3
    return (rows == jnp.arange(count // 3, dtype=jnp.int32)[None, :]).astype(jnp.float32)


def block_mean(state):
    extent = state.shape
    exact = lax.Precision.HIGHEST
    across = jnp.einsum("flrc,cb->flrb", state, grouping(extent[3]), precision=exact)
    down = jnp.einsum("ra,flrb->flab", grouping(extent[2]), across, precision=exact)
    return down / 9.0


def relax_weight(row_global, column_global, total_rows, total_columns):
    row_distance = jnp.minimum(row_global, total_rows - 1 - row_global)
    column_distance = jnp.minimum(column_global, total_columns - 1 - column_global)
    distance = jnp.minimum(row_distance[:, None], column_distance[None, :]).astype(jnp.float32)
    return nudge_floor + (1.0 - nudge_floor) * jnp.exp(-distance / relax_width)


def within(positions, limit):
    return (positions >= 0) & (positions < limit)


def column_pairs(count, base, ratio, k, extra):
    pairs = []
    for m in range(count):
        j = ratio * m + k
        p = base + m + extra
        if j < count and p < count:
            pairs.append((p, j))
    return pairs


def exchange_kernel(axis, patterns, send_ref, recv_ref, send_sems, recv_sems):
    me = lax.axis_index(axis)
    barrier = pltpu.get_barrier_semaphore()
    links = [pair for pairs, _, _ in patterns for pair in pairs]
    for a, b in links:
        @pl.when(me == a)
        def _():
            pl.semaphore_signal(barrier, 1, device_id={axis: b}, device_id_type=MESH)

        @pl.when(me == b)
        def _():
            pl.semaphore_signal(barrier, 1, device_id={axis: a}, device_id_type=MESH)

    peers = {}
    for a, b in links:
        peers[a] = peers.get(a, 0) + 1
        peers[b] = peers.get(b, 0) + 1
    for device, count in sorted(peers.items()):
        @pl.when(me == device)
        def _():
            pl.semaphore_wait(barrier, count)

    copies = []
    for number, (pairs, source, slot) in enumerate(patterns):
        for a, b in pairs:
            copy = pltpu.make_async_remote_copy(
                src_ref=send_ref.at[source],
                dst_ref=recv_ref.at[slot],
                send_sem=send_sems.at[number],
                recv_sem=recv_sems.at[slot],
                device_id={axis: b},
                device_id_type=MESH,
            )
            copies.append((a, b, copy))

            @pl.when(me == a)
            def _():
                copy.start()

    for a, b, copy in copies:
        @pl.when(me == a)
        def _():
            copy.wait_send()

        @pl.when(me == b)
        def _():
            copy.wait_recv()


def exchange(pieces, patterns, slots, axis, identity):
    me = lax.axis_index(axis)
    remote = [([(a, b) for a, b in pairs if a != b], source, slot) for pairs, source, slot in patterns]
    remote = [entry for entry in remote if entry[0]]
    shape = pieces.shape[1:]
    received = pl.pallas_call(
        lambda *refs: exchange_kernel(axis, remote, *refs),
        out_shape=jax.ShapeDtypeStruct((slots,) + shape, pieces.dtype),
        in_specs=[pl.BlockSpec(memory_space=pl.ANY)],
        out_specs=pl.BlockSpec(memory_space=pl.ANY),
        scratch_shapes=[
            pltpu.SemaphoreType.DMA((len(remote),)),
            pltpu.SemaphoreType.DMA((slots,)),
        ],
        compiler_params=pltpu.CompilerParams(collective_id=identity, has_side_effects=True),
    )(pieces)
    parts = [received[slot] for slot in range(slots)]
    for pairs, source, slot in patterns:
        for a, b in pairs:
            if a == b:
                parts[slot] = jnp.where(me == a, pieces[source], parts[slot])
    return parts


def flat(block):
    size = block.size
    return block.reshape(size // 128, 128) if size % 128 == 0 else block.reshape(-1, block.shape[-1])


def per_device(
    parent_fields,
    parent_velocity,
    parent_mixing,
    nest_fields,
    nest_velocity,
    nest_mixing,
    nest_anchor,
):
    row_rank = lax.axis_index("gx")
    column_rank = lax.axis_index("gy")
    row_devices = lax.axis_size("gx")
    column_devices = lax.axis_size("gy")
    parent_rows = parent_fields.shape[2]
    parent_columns = parent_fields.shape[3]
    nest_rows = nest_fields.shape[2]
    nest_columns = nest_fields.shape[3]
    span_rows = nest_rows // 3
    span_columns = nest_columns // 3
    ratio = parent_columns // span_columns
    base = column_devices // 2
    base_column = base * parent_columns
    relay_rows = span_rows + 2
    relay_columns = span_columns + 2
    row_anchor = nest_anchor[0]
    column_anchor = nest_anchor[1]
    offset = column_anchor - 1 - base_column

    parent_next = update(
        parent_fields, neighbours(parent_fields), parent_velocity, parent_mixing
    )

    margin = parent_columns - span_columns
    wide = jnp.pad(parent_next, ((0, 0), (0, 0), (0, 0), (margin, margin)))
    pieces = []
    patterns = []
    for extra in (0, 1):
        for k in range(ratio):
            if extra == 1 and k == 0:
                continue
            start = margin + span_columns * k + offset - extra * parent_columns
            piece = lax.dynamic_slice_in_dim(wide, start, relay_columns, axis=3)
            patterns.append(
                (column_pairs(column_devices, base, ratio, k, extra), len(pieces), extra)
            )
            pieces.append(flat(piece))
    within_part, beyond_part = exchange(jnp.stack(pieces), patterns, 2, "gy", 0)
    piece_shape = parent_next.shape[:3] + (relay_columns,)
    straddles = column_rank % ratio != 0
    relay_cols = within_part.reshape(piece_shape) + jnp.where(
        straddles, beyond_part.reshape(piece_shape), 0.0
    )

    padded = jnp.pad(relay_cols, ((0, 0), (0, 0), (relay_rows, relay_rows), (0, 0)))
    slots = []
    for target in range(row_devices):
        first = row_anchor - 1 + span_rows * target - parent_rows * row_rank
        first = jnp.clip(first, -relay_rows, parent_rows) + relay_rows
        slots.append(lax.dynamic_slice_in_dim(padded, first, relay_rows, axis=2))
    stacked = jnp.stack(slots, axis=0)
    received = lax.all_to_all(stacked, "gx", split_axis=0, concat_axis=0, tiled=True)
    relay = jnp.sum(received, axis=0)

    forcing = refine_columns(refine_rows(relay))
    row_global = row_rank * nest_rows + jnp.arange(nest_rows, dtype=jnp.int32)
    column_global = column_rank * nest_columns + jnp.arange(nest_columns, dtype=jnp.int32)
    weight = relax_weight(
        row_global, column_global, row_devices * nest_rows, column_devices * nest_columns
    )
    state = nest_fields
    for substep in range(SUBSTEPS):
        moved = update(state, neighbours(state), nest_velocity, nest_mixing)
        state = moved + weight * (forcing - moved)

    coarse = block_mean(state)
    gathered = lax.all_gather(coarse, "gx", axis=2, tiled=True)
    total_span = row_devices * span_rows
    gathered = jnp.pad(gathered, ((0, 0), (0, 0), (parent_rows, parent_rows), (0, 0)))
    first = jnp.clip(parent_rows * row_rank - row_anchor, -parent_rows, total_span)
    strip = lax.dynamic_slice_in_dim(gathered, first + parent_rows, parent_rows, axis=2)

    patterns = []
    for extra in (1, 0):
        for k in range(ratio):
            if extra == 1 and k == 0:
                continue
            pairs = [(j, p) for (p, j) in column_pairs(column_devices, base, ratio, k, extra)]
            patterns.append((pairs, 0, len(patterns)))
    parts = exchange(flat(strip)[None], patterns, len(patterns), "gy", 1)
    joined = jnp.concatenate([part.reshape(strip.shape) for part in parts], axis=3)
    start = (ratio - 1) * span_columns - 1 - offset
    fed_back = lax.dynamic_slice_in_dim(joined, start, parent_columns, axis=3)

    relative_rows = row_rank * parent_rows + jnp.arange(parent_rows, dtype=jnp.int32) - row_anchor
    relative_columns = (
        column_rank * parent_columns + jnp.arange(parent_columns, dtype=jnp.int32) - column_anchor
    )
    rows_valid = within(relative_rows, total_span)
    columns_valid = within(relative_columns, column_devices * span_columns)
    covered = rows_valid[:, None] & columns_valid[None, :]
    parent_result = jnp.where(covered, fed_back, parent_next)
    return (parent_result, state)


def solution(mesh):
    placed = (
        P(None, None, "gx", "gy"),
        P(None, None, "gx", "gy"),
        P(None, "gx", "gy"),
        P(None, None, "gx", "gy"),
        P(None, None, "gx", "gy"),
        P(None, "gx", "gy"),
        P(),
    )
    return jax.shard_map(
        per_device,
        mesh=mesh,
        in_specs=placed,
        out_specs=(P(None, None, "gx", "gy"), P(None, None, "gx", "gy")),
        check_vma=False,
    )
```

```python
import jax
import jax.numpy as jnp
from jax import lax
from jax.experimental import pallas as pl
from jax.experimental.pallas import tpu as pltpu
from jax.sharding import PartitionSpec as P

MESH = pl.DeviceIdType.MESH

SUBSTEPS = 3


third = 1.0 / 3.0
two_thirds = 2.0 / 3.0
nudge_floor = 0.1
relax_width = 4.0


def shift_pairs(count, step):
    return [(i, i + step) for i in range(count) if 0 <= i + step < count]


def halo_kernel(rows, cols, *refs):
    sources, targets, send_sems, recv_sems = refs[:4], refs[4:8], refs[8], refs[9]
    x = lax.axis_index("gx")
    y = lax.axis_index("gy")
    routes = (("gx", x, 1, rows), ("gx", x, -1, rows), ("gy", y, 1, cols), ("gy", y, -1, cols))
    barrier = pltpu.get_barrier_semaphore()
    for axis, own, step, count in routes:
        @pl.when((own + step >= 0) & (own + step < count))
        def _():
            pl.semaphore_signal(barrier, 1, device_id={axis: own + step}, device_id_type=MESH)

    peers = (x + rows - 1) // rows + (2 * rows - 2 - x) // rows
    peers = peers + (y + cols - 1) // cols + (2 * cols - 2 - y) // cols
    pl.semaphore_wait(barrier, peers)
    copies = []
    for number, (axis, own, step, count) in enumerate(routes):
        copy = pltpu.make_async_remote_copy(
            src_ref=sources[number],
            dst_ref=targets[number],
            send_sem=send_sems.at[number],
            recv_sem=recv_sems.at[number],
            device_id={axis: own + step},
            device_id_type=MESH,
        )
        copies.append((own, step, count, copy))

        @pl.when((own + step >= 0) & (own + step < count))
        def _():
            copy.start()

    for own, step, count, copy in copies:
        @pl.when((own + step >= 0) & (own + step < count))
        def _():
            copy.wait_send()

        @pl.when((own - step >= 0) & (own - step < count))
        def _():
            copy.wait_recv()


def neighbours(cells, identity):
    rows = lax.axis_size("gx")
    cols = lax.axis_size("gy")
    x = lax.axis_index("gx")
    y = lax.axis_index("gy")
    fields, levels, height, width = cells.shape
    planes = fields * levels
    sources = (
        cells[:, :, -1, :].reshape(planes, width),
        cells[:, :, 0, :].reshape(planes, width),
        cells[:, :, :, -1].reshape(planes, height),
        cells[:, :, :, 0].reshape(planes, height),
    )
    received = pl.pallas_call(
        lambda *refs: halo_kernel(rows, cols, *refs),
        out_shape=tuple(jax.ShapeDtypeStruct(part.shape, part.dtype) for part in sources),
        in_specs=[pl.BlockSpec(memory_space=pltpu.VMEM)] * 4,
        out_specs=tuple(pl.BlockSpec(memory_space=pltpu.VMEM) for _ in range(4)),
        scratch_shapes=[pltpu.SemaphoreType.DMA((4,)), pltpu.SemaphoreType.DMA((4,))],
        compiler_params=pltpu.CompilerParams(collective_id=identity, has_side_effects=True),
    )(*sources)
    western, eastern, southern, northern = received
    western = jnp.where(x > 0, western, 0.0).reshape(fields, levels, 1, width)
    eastern = jnp.where(x < rows - 1, eastern, 0.0).reshape(fields, levels, 1, width)
    southern = jnp.where(y > 0, southern, 0.0).reshape(fields, levels, height, 1)
    northern = jnp.where(y < cols - 1, northern, 0.0).reshape(fields, levels, height, 1)
    return western, eastern, southern, northern


def update(values, halo, velocity, mixing):
    west_row, east_row, south_col, north_col = halo
    western = jnp.concatenate([west_row, values[:, :, :-1, :]], axis=2)
    eastern = jnp.concatenate([values[:, :, 1:, :], east_row], axis=2)
    southern = jnp.concatenate([south_col, values[:, :, :, :-1]], axis=3)
    northern = jnp.concatenate([values[:, :, :, 1:], north_col], axis=3)
    along_rows = velocity[0]
    along_columns = velocity[1]
    upwind = (
        jnp.maximum(along_rows, 0.0) * (values - western)
        + jnp.minimum(along_rows, 0.0) * (eastern - values)
        + jnp.maximum(along_columns, 0.0) * (values - southern)
        + jnp.minimum(along_columns, 0.0) * (northern - values)
    )
    return values - upwind + mixing * (eastern + western + northern + southern - 4.0 * values)


def refine_rows(block):
    lower = block[:, :, :-2]
    centre = block[:, :, 1:-1]
    upper = block[:, :, 2:]
    stacked = jnp.stack(
        (third * lower + two_thirds * centre, centre, two_thirds * centre + third * upper), axis=3
    )
    extent = centre.shape
    return stacked.reshape(extent[0], extent[1], 3 * extent[2], extent[3])


def refine_columns(block):
    lower = block[:, :, :, :-2]
    centre = block[:, :, :, 1:-1]
    upper = block[:, :, :, 2:]
    stacked = jnp.stack(
        (third * lower + two_thirds * centre, centre, two_thirds * centre + third * upper), axis=4
    )
    extent = centre.shape
    return stacked.reshape(extent[0], extent[1], extent[2], 3 * extent[3])


def grouping(count):
    rows = jnp.arange(count, dtype=jnp.int32)[:, None] // 3
    return (rows == jnp.arange(count // 3, dtype=jnp.int32)[None, :]).astype(jnp.float32)


def block_mean(state):
    extent = state.shape
    exact = lax.Precision.HIGHEST
    across = jnp.einsum("flrc,cb->flrb", state, grouping(extent[3]), precision=exact)
    down = jnp.einsum("ra,flrb->flab", grouping(extent[2]), across, precision=exact)
    return down / 9.0


def relax_weight(row_global, column_global, total_rows, total_columns):
    row_distance = jnp.minimum(row_global, total_rows - 1 - row_global)
    column_distance = jnp.minimum(column_global, total_columns - 1 - column_global)
    distance = jnp.minimum(row_distance[:, None], column_distance[None, :]).astype(jnp.float32)
    return nudge_floor + (1.0 - nudge_floor) * jnp.exp(-distance / relax_width)


def within(positions, limit):
    return (positions >= 0) & (positions < limit)


def column_pairs(count, base, ratio, k, extra):
    pairs = []
    for m in range(count):
        j = ratio * m + k
        p = base + m + extra
        if j < count and p < count:
            pairs.append((p, j))
    return pairs


def exchange_kernel(axis, patterns, send_ref, recv_ref, send_sems, recv_sems):
    me = lax.axis_index(axis)
    barrier = pltpu.get_barrier_semaphore()
    links = [pair for pairs, _, _ in patterns for pair in pairs]
    for a, b in links:
        @pl.when(me == a)
        def _():
            pl.semaphore_signal(barrier, 1, device_id={axis: b}, device_id_type=MESH)

        @pl.when(me == b)
        def _():
            pl.semaphore_signal(barrier, 1, device_id={axis: a}, device_id_type=MESH)

    peers = {}
    for a, b in links:
        peers[a] = peers.get(a, 0) + 1
        peers[b] = peers.get(b, 0) + 1
    for device, count in sorted(peers.items()):
        @pl.when(me == device)
        def _():
            pl.semaphore_wait(barrier, count)

    copies = []
    for number, (pairs, source, slot) in enumerate(patterns):
        for a, b in pairs:
            copy = pltpu.make_async_remote_copy(
                src_ref=send_ref.at[source],
                dst_ref=recv_ref.at[slot],
                send_sem=send_sems.at[number],
                recv_sem=recv_sems.at[slot],
                device_id={axis: b},
                device_id_type=MESH,
            )
            copies.append((a, b, copy))

            @pl.when(me == a)
            def _():
                copy.start()

    for a, b, copy in copies:
        @pl.when(me == a)
        def _():
            copy.wait_send()

        @pl.when(me == b)
        def _():
            copy.wait_recv()


def exchange(pieces, patterns, slots, axis, identity):
    me = lax.axis_index(axis)
    remote = [([(a, b) for a, b in pairs if a != b], source, slot) for pairs, source, slot in patterns]
    remote = [entry for entry in remote if entry[0]]
    shape = pieces.shape[1:]
    received = pl.pallas_call(
        lambda *refs: exchange_kernel(axis, remote, *refs),
        out_shape=jax.ShapeDtypeStruct((slots,) + shape, pieces.dtype),
        in_specs=[pl.BlockSpec(memory_space=pl.ANY)],
        out_specs=pl.BlockSpec(memory_space=pl.ANY),
        scratch_shapes=[
            pltpu.SemaphoreType.DMA((len(remote),)),
            pltpu.SemaphoreType.DMA((slots,)),
        ],
        compiler_params=pltpu.CompilerParams(collective_id=identity, has_side_effects=True),
    )(pieces)
    parts = [received[slot] for slot in range(slots)]
    for pairs, source, slot in patterns:
        for a, b in pairs:
            if a == b:
                parts[slot] = jnp.where(me == a, pieces[source], parts[slot])
    return parts


def flat(block):
    size = block.size
    return block.reshape(size // 128, 128) if size % 128 == 0 else block.reshape(-1, block.shape[-1])


def per_device(
    parent_fields,
    parent_velocity,
    parent_mixing,
    nest_fields,
    nest_velocity,
    nest_mixing,
    nest_anchor,
):
    row_rank = lax.axis_index("gx")
    column_rank = lax.axis_index("gy")
    row_devices = lax.axis_size("gx")
    column_devices = lax.axis_size("gy")
    parent_rows = parent_fields.shape[2]
    parent_columns = parent_fields.shape[3]
    nest_rows = nest_fields.shape[2]
    nest_columns = nest_fields.shape[3]
    span_rows = nest_rows // 3
    span_columns = nest_columns // 3
    ratio = parent_columns // span_columns
    base = column_devices // 2
    base_column = base * parent_columns
    relay_rows = span_rows + 2
    relay_columns = span_columns + 2
    row_anchor = nest_anchor[0]
    column_anchor = nest_anchor[1]
    offset = column_anchor - 1 - base_column

    parent_next = update(
        parent_fields, neighbours(parent_fields, 2), parent_velocity, parent_mixing
    )

    margin = parent_columns - span_columns
    wide = jnp.pad(parent_next, ((0, 0), (0, 0), (0, 0), (margin, margin)))
    pieces = []
    patterns = []
    for extra in (0, 1):
        for k in range(ratio):
            if extra == 1 and k == 0:
                continue
            start = margin + span_columns * k + offset - extra * parent_columns
            piece = lax.dynamic_slice_in_dim(wide, start, relay_columns, axis=3)
            patterns.append(
                (column_pairs(column_devices, base, ratio, k, extra), len(pieces), extra)
            )
            pieces.append(flat(piece))
    within_part, beyond_part = exchange(jnp.stack(pieces), patterns, 2, "gy", 0)
    piece_shape = parent_next.shape[:3] + (relay_columns,)
    straddles = column_rank % ratio != 0
    relay_cols = within_part.reshape(piece_shape) + jnp.where(
        straddles, beyond_part.reshape(piece_shape), 0.0
    )

    padded = jnp.pad(relay_cols, ((0, 0), (0, 0), (relay_rows, relay_rows), (0, 0)))
    slots = []
    for target in range(row_devices):
        first = row_anchor - 1 + span_rows * target - parent_rows * row_rank
        first = jnp.clip(first, -relay_rows, parent_rows) + relay_rows
        slots.append(lax.dynamic_slice_in_dim(padded, first, relay_rows, axis=2))
    stacked = jnp.stack(slots, axis=0)
    received = lax.all_to_all(stacked, "gx", split_axis=0, concat_axis=0, tiled=True)
    relay = jnp.sum(received, axis=0)

    forcing = refine_columns(refine_rows(relay))
    row_global = row_rank * nest_rows + jnp.arange(nest_rows, dtype=jnp.int32)
    column_global = column_rank * nest_columns + jnp.arange(nest_columns, dtype=jnp.int32)
    weight = relax_weight(
        row_global, column_global, row_devices * nest_rows, column_devices * nest_columns
    )
    state = nest_fields
    for substep in range(SUBSTEPS):
        moved = update(state, neighbours(state, 3 + substep), nest_velocity, nest_mixing)
        state = moved + weight * (forcing - moved)

    coarse = block_mean(state)
    gathered = lax.all_gather(coarse, "gx", axis=2, tiled=True)
    total_span = row_devices * span_rows
    gathered = jnp.pad(gathered, ((0, 0), (0, 0), (parent_rows, parent_rows), (0, 0)))
    first = jnp.clip(parent_rows * row_rank - row_anchor, -parent_rows, total_span)
    strip = lax.dynamic_slice_in_dim(gathered, first + parent_rows, parent_rows, axis=2)

    patterns = []
    for extra in (1, 0):
        for k in range(ratio):
            if extra == 1 and k == 0:
                continue
            pairs = [(j, p) for (p, j) in column_pairs(column_devices, base, ratio, k, extra)]
            patterns.append((pairs, 0, len(patterns)))
    parts = exchange(flat(strip)[None], patterns, len(patterns), "gy", 1)
    joined = jnp.concatenate([part.reshape(strip.shape) for part in parts], axis=3)
    start = (ratio - 1) * span_columns - 1 - offset
    fed_back = lax.dynamic_slice_in_dim(joined, start, parent_columns, axis=3)

    relative_rows = row_rank * parent_rows + jnp.arange(parent_rows, dtype=jnp.int32) - row_anchor
    relative_columns = (
        column_rank * parent_columns + jnp.arange(parent_columns, dtype=jnp.int32) - column_anchor
    )
    rows_valid = within(relative_rows, total_span)
    columns_valid = within(relative_columns, column_devices * span_columns)
    covered = rows_valid[:, None] & columns_valid[None, :]
    parent_result = jnp.where(covered, fed_back, parent_next)
    return (parent_result, state)


def solution(mesh):
    placed = (
        P(None, None, "gx", "gy"),
        P(None, None, "gx", "gy"),
        P(None, "gx", "gy"),
        P(None, None, "gx", "gy"),
        P(None, None, "gx", "gy"),
        P(None, "gx", "gy"),
        P(),
    )
    return jax.shard_map(
        per_device,
        mesh=mesh,
        in_specs=placed,
        out_specs=(P(None, None, "gx", "gy"), P(None, None, "gx", "gy")),
        check_vma=False,
    )
```

```python
import jax
import jax.numpy as jnp
from jax import lax
from jax.experimental import pallas as pl
from jax.experimental.pallas import tpu as pltpu
from jax.sharding import PartitionSpec as P

MESH = pl.DeviceIdType.MESH

SUBSTEPS = 3


third = 1.0 / 3.0
two_thirds = 2.0 / 3.0
nudge_floor = 0.1
relax_width = 4.0


def shift_pairs(count, step):
    return [(i, i + step) for i in range(count) if 0 <= i + step < count]


def halo_kernel(rows, cols, *refs):
    sources, targets, send_sems, recv_sems = refs[:4], refs[4:8], refs[8], refs[9]
    x = lax.axis_index("gx")
    y = lax.axis_index("gy")
    routes = (("gx", x, 1, rows), ("gx", x, -1, rows), ("gy", y, 1, cols), ("gy", y, -1, cols))
    barrier = pltpu.get_barrier_semaphore()
    for axis, own, step, count in routes:
        @pl.when((own + step >= 0) & (own + step < count))
        def _():
            pl.semaphore_signal(barrier, 1, device_id={axis: own + step}, device_id_type=MESH)

    peers = (x + rows - 1) // rows + (2 * rows - 2 - x) // rows
    peers = peers + (y + cols - 1) // cols + (2 * cols - 2 - y) // cols
    pl.semaphore_wait(barrier, peers)
    copies = []
    for number, (axis, own, step, count) in enumerate(routes):
        copy = pltpu.make_async_remote_copy(
            src_ref=sources[number],
            dst_ref=targets[number],
            send_sem=send_sems.at[number],
            recv_sem=recv_sems.at[number],
            device_id={axis: own + step},
            device_id_type=MESH,
        )
        copies.append((own, step, count, copy))

        @pl.when((own + step >= 0) & (own + step < count))
        def _():
            copy.start()

    for own, step, count, copy in copies:
        @pl.when((own + step >= 0) & (own + step < count))
        def _():
            copy.wait_send()

        @pl.when((own - step >= 0) & (own - step < count))
        def _():
            copy.wait_recv()


def neighbours(cells, identity):
    rows = lax.axis_size("gx")
    cols = lax.axis_size("gy")
    x = lax.axis_index("gx")
    y = lax.axis_index("gy")
    fields, levels, height, width = cells.shape
    planes = fields * levels
    sources = (
        cells[:, :, -1, :].reshape(planes, width),
        cells[:, :, 0, :].reshape(planes, width),
        cells[:, :, :, -1].reshape(planes, height),
        cells[:, :, :, 0].reshape(planes, height),
    )
    received = pl.pallas_call(
        lambda *refs: halo_kernel(rows, cols, *refs),
        out_shape=tuple(jax.ShapeDtypeStruct(part.shape, part.dtype) for part in sources),
        in_specs=[pl.BlockSpec(memory_space=pltpu.VMEM)] * 4,
        out_specs=tuple(pl.BlockSpec(memory_space=pltpu.VMEM) for _ in range(4)),
        scratch_shapes=[pltpu.SemaphoreType.DMA((4,)), pltpu.SemaphoreType.DMA((4,))],
        compiler_params=pltpu.CompilerParams(collective_id=identity, has_side_effects=True),
    )(*sources)
    western, eastern, southern, northern = received
    western = jnp.where(x > 0, western, 0.0).reshape(fields, levels, 1, width)
    eastern = jnp.where(x < rows - 1, eastern, 0.0).reshape(fields, levels, 1, width)
    southern = jnp.where(y > 0, southern, 0.0).reshape(fields, levels, height, 1)
    northern = jnp.where(y < cols - 1, northern, 0.0).reshape(fields, levels, height, 1)
    return western, eastern, southern, northern


def update(values, halo, velocity, mixing):
    west_row, east_row, south_col, north_col = halo
    western = jnp.concatenate([west_row, values[:, :, :-1, :]], axis=2)
    eastern = jnp.concatenate([values[:, :, 1:, :], east_row], axis=2)
    southern = jnp.concatenate([south_col, values[:, :, :, :-1]], axis=3)
    northern = jnp.concatenate([values[:, :, :, 1:], north_col], axis=3)
    along_rows = velocity[0]
    along_columns = velocity[1]
    upwind = (
        jnp.maximum(along_rows, 0.0) * (values - western)
        + jnp.minimum(along_rows, 0.0) * (eastern - values)
        + jnp.maximum(along_columns, 0.0) * (values - southern)
        + jnp.minimum(along_columns, 0.0) * (northern - values)
    )
    return values - upwind + mixing * (eastern + western + northern + southern - 4.0 * values)


def refine_rows(block):
    lower = block[:, :, :-2]
    centre = block[:, :, 1:-1]
    upper = block[:, :, 2:]
    stacked = jnp.stack(
        (third * lower + two_thirds * centre, centre, two_thirds * centre + third * upper), axis=3
    )
    extent = centre.shape
    return stacked.reshape(extent[0], extent[1], 3 * extent[2], extent[3])


def refine_columns(block):
    lower = block[:, :, :, :-2]
    centre = block[:, :, :, 1:-1]
    upper = block[:, :, :, 2:]
    stacked = jnp.stack(
        (third * lower + two_thirds * centre, centre, two_thirds * centre + third * upper), axis=4
    )
    extent = centre.shape
    return stacked.reshape(extent[0], extent[1], extent[2], 3 * extent[3])


def grouping(count):
    rows = jnp.arange(count, dtype=jnp.int32)[:, None] // 3
    return (rows == jnp.arange(count // 3, dtype=jnp.int32)[None, :]).astype(jnp.float32)


def block_mean(state):
    extent = state.shape
    exact = lax.Precision.HIGHEST
    across = jnp.einsum("flrc,cb->flrb", state, grouping(extent[3]), precision=exact)
    down = jnp.einsum("ra,flrb->flab", grouping(extent[2]), across, precision=exact)
    return down / 9.0


def relax_weight(row_global, column_global, total_rows, total_columns):
    row_distance = jnp.minimum(row_global, total_rows - 1 - row_global)
    column_distance = jnp.minimum(column_global, total_columns - 1 - column_global)
    distance = jnp.minimum(row_distance[:, None], column_distance[None, :]).astype(jnp.float32)
    return nudge_floor + (1.0 - nudge_floor) * jnp.exp(-distance / relax_width)


def within(positions, limit):
    return (positions >= 0) & (positions < limit)


def column_pairs(count, base, ratio, k, extra):
    pairs = []
    for m in range(count):
        j = ratio * m + k
        p = base + m + extra
        if j < count and p < count:
            pairs.append((p, j))
    return pairs


def exchange_kernel(axis, patterns, send_ref, recv_ref, send_sems, recv_sems):
    me = lax.axis_index(axis)
    barrier = pltpu.get_barrier_semaphore()
    links = [pair for pairs, _, _ in patterns for pair in pairs]
    for a, b in links:
        @pl.when(me == a)
        def _():
            pl.semaphore_signal(barrier, 1, device_id={axis: b}, device_id_type=MESH)

        @pl.when(me == b)
        def _():
            pl.semaphore_signal(barrier, 1, device_id={axis: a}, device_id_type=MESH)

    peers = {}
    for a, b in links:
        peers[a] = peers.get(a, 0) + 1
        peers[b] = peers.get(b, 0) + 1
    for device, count in sorted(peers.items()):
        @pl.when(me == device)
        def _():
            pl.semaphore_wait(barrier, count)

    copies = []
    for number, (pairs, source, slot) in enumerate(patterns):
        for a, b in pairs:
            copy = pltpu.make_async_remote_copy(
                src_ref=send_ref.at[source],
                dst_ref=recv_ref.at[slot],
                send_sem=send_sems.at[number],
                recv_sem=recv_sems.at[slot],
                device_id={axis: b},
                device_id_type=MESH,
            )
            copies.append((a, b, copy))

            @pl.when(me == a)
            def _():
                copy.start()

    for a, b, copy in copies:
        @pl.when(me == a)
        def _():
            copy.wait_send()

        @pl.when(me == b)
        def _():
            copy.wait_recv()


def exchange(pieces, patterns, slots, axis, identity):
    me = lax.axis_index(axis)
    remote = [([(a, b) for a, b in pairs if a != b], source, slot) for pairs, source, slot in patterns]
    remote = [entry for entry in remote if entry[0]]
    shape = pieces.shape[1:]
    received = pl.pallas_call(
        lambda *refs: exchange_kernel(axis, remote, *refs),
        out_shape=jax.ShapeDtypeStruct((slots,) + shape, pieces.dtype),
        in_specs=[pl.BlockSpec(memory_space=pl.ANY)],
        out_specs=pl.BlockSpec(memory_space=pl.ANY),
        scratch_shapes=[
            pltpu.SemaphoreType.DMA((len(remote),)),
            pltpu.SemaphoreType.DMA((slots,)),
        ],
        compiler_params=pltpu.CompilerParams(collective_id=identity, has_side_effects=True),
    )(pieces)
    parts = [received[slot] for slot in range(slots)]
    for pairs, source, slot in patterns:
        for a, b in pairs:
            if a == b:
                parts[slot] = jnp.where(me == a, pieces[source], parts[slot])
    return parts


def flat(block):
    size = block.size
    return block.reshape(size // 128, 128) if size % 128 == 0 else block.reshape(-1, block.shape[-1])


def per_device(
    parent_fields,
    parent_velocity,
    parent_mixing,
    nest_fields,
    nest_velocity,
    nest_mixing,
    nest_anchor,
):
    row_rank = lax.axis_index("gx")
    column_rank = lax.axis_index("gy")
    row_devices = lax.axis_size("gx")
    column_devices = lax.axis_size("gy")
    parent_rows = parent_fields.shape[2]
    parent_columns = parent_fields.shape[3]
    nest_rows = nest_fields.shape[2]
    nest_columns = nest_fields.shape[3]
    span_rows = nest_rows // 3
    span_columns = nest_columns // 3
    ratio = parent_columns // span_columns
    base = column_devices // 2
    base_column = base * parent_columns
    relay_rows = span_rows + 2
    relay_columns = span_columns + 2
    row_anchor = nest_anchor[0]
    column_anchor = nest_anchor[1]
    offset = column_anchor - 1 - base_column

    parent_next = update(
        parent_fields, neighbours(parent_fields, 2), parent_velocity, parent_mixing
    )

    margin = parent_columns - span_columns
    wide = jnp.pad(parent_next, ((0, 0), (0, 0), (0, 0), (margin, margin)))
    straddle = (ratio - 1) * span_columns - 2
    regimes = (
        lambda k, extra: not (extra == 1 and k == ratio - 2),
        lambda k, extra: True,
        lambda k, extra: not (extra == 0 and k == ratio - 1),
    )
    regime = (offset > straddle - span_columns).astype(jnp.int32) + (
        offset > straddle - span_columns + 1
    ).astype(jnp.int32)
    pieces = []
    routes = []
    for extra in (0, 1):
        for k in range(ratio):
            if extra == 1 and k == 0:
                continue
            start = margin + span_columns * k + offset - extra * parent_columns
            piece = lax.dynamic_slice_in_dim(wide, start, relay_columns, axis=3)
            routes.append((k, extra, len(pieces)))
            pieces.append(flat(piece))
    stacked_pieces = jnp.stack(pieces)
    branches = []
    for number, active in enumerate(regimes):
        patterns = [
            (column_pairs(column_devices, base, ratio, k, extra), index, extra)
            for k, extra, index in routes
            if active(k, extra)
        ]
        identity = (0, 6, 7)[number]
        branches.append(
            lambda stacked, patterns=patterns, identity=identity: tuple(
                exchange(stacked, patterns, 2, "gy", identity)
            )
        )
    within_part, beyond_part = lax.switch(regime, branches, stacked_pieces)
    piece_shape = parent_next.shape[:3] + (relay_columns,)
    own_k = column_rank % ratio
    within_live = jnp.logical_not((regime == 2) & (own_k == ratio - 1))
    beyond_live = (own_k != 0) & jnp.logical_not((regime == 0) & (own_k == ratio - 2))
    relay_cols = jnp.where(within_live, within_part.reshape(piece_shape), 0.0) + jnp.where(
        beyond_live, beyond_part.reshape(piece_shape), 0.0
    )

    padded = jnp.pad(relay_cols, ((0, 0), (0, 0), (relay_rows, relay_rows), (0, 0)))
    slots = []
    for target in range(row_devices):
        first = row_anchor - 1 + span_rows * target - parent_rows * row_rank
        first = jnp.clip(first, -relay_rows, parent_rows) + relay_rows
        slots.append(lax.dynamic_slice_in_dim(padded, first, relay_rows, axis=2))
    stacked = jnp.stack(slots, axis=0)
    received = lax.all_to_all(stacked, "gx", split_axis=0, concat_axis=0, tiled=True)
    relay = jnp.sum(received, axis=0)

    forcing = refine_columns(refine_rows(relay))
    row_global = row_rank * nest_rows + jnp.arange(nest_rows, dtype=jnp.int32)
    column_global = column_rank * nest_columns + jnp.arange(nest_columns, dtype=jnp.int32)
    weight = relax_weight(
        row_global, column_global, row_devices * nest_rows, column_devices * nest_columns
    )
    state = nest_fields
    for substep in range(SUBSTEPS):
        moved = update(state, neighbours(state, 3 + substep), nest_velocity, nest_mixing)
        state = moved + weight * (forcing - moved)

    coarse = block_mean(state)
    gathered = lax.all_gather(coarse, "gx", axis=2, tiled=True)
    total_span = row_devices * span_rows
    gathered = jnp.pad(gathered, ((0, 0), (0, 0), (parent_rows, parent_rows), (0, 0)))
    first = jnp.clip(parent_rows * row_rank - row_anchor, -parent_rows, total_span)
    strip = lax.dynamic_slice_in_dim(gathered, first + parent_rows, parent_rows, axis=2)

    routes = []
    for extra in (1, 0):
        for k in range(ratio):
            if extra == 1 and k == 0:
                continue
            pairs = [(j, p) for (p, j) in column_pairs(column_devices, base, ratio, k, extra)]
            routes.append((k, extra, pairs))
    back_branches = []
    for number, skipped in enumerate(((1, 1), (0, ratio - 1))):
        patterns = [
            (pairs, 0, slot) for slot, (k, extra, pairs) in enumerate(routes)
            if (k, extra) != (skipped[1], skipped[0])
        ]
        identity = (1, 8)[number]
        back_branches.append(
            lambda sent, patterns=patterns, identity=identity: tuple(
                exchange(sent, patterns, len(routes), "gy", identity)
            )
        )
    late = (offset > (ratio - 1) * span_columns - span_columns - 1).astype(jnp.int32)
    parts = lax.switch(late, back_branches, flat(strip)[None])
    joined = jnp.concatenate([part.reshape(strip.shape) for part in parts], axis=3)
    start = (ratio - 1) * span_columns - 1 - offset
    fed_back = lax.dynamic_slice_in_dim(joined, start, parent_columns, axis=3)

    relative_rows = row_rank * parent_rows + jnp.arange(parent_rows, dtype=jnp.int32) - row_anchor
    relative_columns = (
        column_rank * parent_columns + jnp.arange(parent_columns, dtype=jnp.int32) - column_anchor
    )
    rows_valid = within(relative_rows, total_span)
    columns_valid = within(relative_columns, column_devices * span_columns)
    covered = rows_valid[:, None] & columns_valid[None, :]
    parent_result = jnp.where(covered, fed_back, parent_next)
    return (parent_result, state)


def solution(mesh):
    placed = (
        P(None, None, "gx", "gy"),
        P(None, None, "gx", "gy"),
        P(None, "gx", "gy"),
        P(None, None, "gx", "gy"),
        P(None, None, "gx", "gy"),
        P(None, "gx", "gy"),
        P(),
    )
    return jax.shard_map(
        per_device,
        mesh=mesh,
        in_specs=placed,
        out_specs=(P(None, None, "gx", "gy"), P(None, None, "gx", "gy")),
        check_vma=False,
    )
```

```python
import jax
import jax.numpy as jnp
from jax import lax
from jax.experimental import pallas as pl
from jax.experimental.pallas import tpu as pltpu
from jax.sharding import PartitionSpec as P

MESH = pl.DeviceIdType.MESH

SUBSTEPS = 3


third = 1.0 / 3.0
two_thirds = 2.0 / 3.0
nudge_floor = 0.1
relax_width = 4.0


def shift_pairs(count, step):
    return [(i, i + step) for i in range(count) if 0 <= i + step < count]


def halo_kernel(rows, cols, *refs):
    sources, targets, send_sems, recv_sems = refs[:4], refs[4:8], refs[8], refs[9]
    x = lax.axis_index("gx")
    y = lax.axis_index("gy")
    routes = (("gx", x, 1, rows), ("gx", x, -1, rows), ("gy", y, 1, cols), ("gy", y, -1, cols))
    barrier = pltpu.get_barrier_semaphore()
    for axis, own, step, count in routes:
        @pl.when((own + step >= 0) & (own + step < count))
        def _():
            pl.semaphore_signal(barrier, 1, device_id={axis: own + step}, device_id_type=MESH)

    peers = (x + rows - 1) // rows + (2 * rows - 2 - x) // rows
    peers = peers + (y + cols - 1) // cols + (2 * cols - 2 - y) // cols
    pl.semaphore_wait(barrier, peers)
    copies = []
    for number, (axis, own, step, count) in enumerate(routes):
        copy = pltpu.make_async_remote_copy(
            src_ref=sources[number],
            dst_ref=targets[number],
            send_sem=send_sems.at[number],
            recv_sem=recv_sems.at[number],
            device_id={axis: own + step},
            device_id_type=MESH,
        )
        copies.append((own, step, count, copy))

        @pl.when((own + step >= 0) & (own + step < count))
        def _():
            copy.start()

    for own, step, count, copy in copies:
        @pl.when((own + step >= 0) & (own + step < count))
        def _():
            copy.wait_send()

        @pl.when((own - step >= 0) & (own - step < count))
        def _():
            copy.wait_recv()


def neighbours(cells, identity):
    rows = lax.axis_size("gx")
    cols = lax.axis_size("gy")
    x = lax.axis_index("gx")
    y = lax.axis_index("gy")
    fields, levels, height, width = cells.shape
    planes = fields * levels
    sources = (
        cells[:, :, -1, :].reshape(planes, width),
        cells[:, :, 0, :].reshape(planes, width),
        cells[:, :, :, -1].reshape(planes, height),
        cells[:, :, :, 0].reshape(planes, height),
    )
    received = pl.pallas_call(
        lambda *refs: halo_kernel(rows, cols, *refs),
        out_shape=tuple(jax.ShapeDtypeStruct(part.shape, part.dtype) for part in sources),
        in_specs=[pl.BlockSpec(memory_space=pltpu.VMEM)] * 4,
        out_specs=tuple(pl.BlockSpec(memory_space=pltpu.VMEM) for _ in range(4)),
        scratch_shapes=[pltpu.SemaphoreType.DMA((4,)), pltpu.SemaphoreType.DMA((4,))],
        compiler_params=pltpu.CompilerParams(collective_id=identity, has_side_effects=True),
    )(*sources)
    western, eastern, southern, northern = received
    western = jnp.where(x > 0, western, 0.0).reshape(fields, levels, 1, width)
    eastern = jnp.where(x < rows - 1, eastern, 0.0).reshape(fields, levels, 1, width)
    southern = jnp.where(y > 0, southern, 0.0).reshape(fields, levels, height, 1)
    northern = jnp.where(y < cols - 1, northern, 0.0).reshape(fields, levels, height, 1)
    return western, eastern, southern, northern


def update(values, halo, velocity, mixing):
    west_row, east_row, south_col, north_col = halo
    western = jnp.concatenate([west_row, values[:, :, :-1, :]], axis=2)
    eastern = jnp.concatenate([values[:, :, 1:, :], east_row], axis=2)
    southern = jnp.concatenate([south_col, values[:, :, :, :-1]], axis=3)
    northern = jnp.concatenate([values[:, :, :, 1:], north_col], axis=3)
    along_rows = velocity[0]
    along_columns = velocity[1]
    upwind = (
        jnp.maximum(along_rows, 0.0) * (values - western)
        + jnp.minimum(along_rows, 0.0) * (eastern - values)
        + jnp.maximum(along_columns, 0.0) * (values - southern)
        + jnp.minimum(along_columns, 0.0) * (northern - values)
    )
    return values - upwind + mixing * (eastern + western + northern + southern - 4.0 * values)


def refine_rows(block):
    lower = block[:, :, :-2]
    centre = block[:, :, 1:-1]
    upper = block[:, :, 2:]
    stacked = jnp.stack(
        (third * lower + two_thirds * centre, centre, two_thirds * centre + third * upper), axis=3
    )
    extent = centre.shape
    return stacked.reshape(extent[0], extent[1], 3 * extent[2], extent[3])


def refine_columns(block):
    lower = block[:, :, :, :-2]
    centre = block[:, :, :, 1:-1]
    upper = block[:, :, :, 2:]
    stacked = jnp.stack(
        (third * lower + two_thirds * centre, centre, two_thirds * centre + third * upper), axis=4
    )
    extent = centre.shape
    return stacked.reshape(extent[0], extent[1], extent[2], 3 * extent[3])


def grouping(count):
    rows = jnp.arange(count, dtype=jnp.int32)[:, None] // 3
    return (rows == jnp.arange(count // 3, dtype=jnp.int32)[None, :]).astype(jnp.float32)


def block_mean(state):
    extent = state.shape
    exact = lax.Precision.HIGHEST
    across = jnp.einsum("flrc,cb->flrb", state, grouping(extent[3]), precision=exact)
    down = jnp.einsum("ra,flrb->flab", grouping(extent[2]), across, precision=exact)
    return down / 9.0


def relax_weight(row_global, column_global, total_rows, total_columns):
    row_distance = jnp.minimum(row_global, total_rows - 1 - row_global)
    column_distance = jnp.minimum(column_global, total_columns - 1 - column_global)
    distance = jnp.minimum(row_distance[:, None], column_distance[None, :]).astype(jnp.float32)
    return nudge_floor + (1.0 - nudge_floor) * jnp.exp(-distance / relax_width)


def within(positions, limit):
    return (positions >= 0) & (positions < limit)


def column_pairs(count, base, ratio, k, extra):
    pairs = []
    for m in range(count):
        j = ratio * m + k
        p = base + m + extra
        if j < count and p < count:
            pairs.append((p, j))
    return pairs


def exchange_kernel(axis, patterns, send_ref, recv_ref, send_sems, recv_sems):
    me = lax.axis_index(axis)
    barrier = pltpu.get_barrier_semaphore()
    links = [pair for pairs, _, _ in patterns for pair in pairs]
    for a, b in links:
        @pl.when(me == a)
        def _():
            pl.semaphore_signal(barrier, 1, device_id={axis: b}, device_id_type=MESH)

        @pl.when(me == b)
        def _():
            pl.semaphore_signal(barrier, 1, device_id={axis: a}, device_id_type=MESH)

    peers = {}
    for a, b in links:
        peers[a] = peers.get(a, 0) + 1
        peers[b] = peers.get(b, 0) + 1
    for device, count in sorted(peers.items()):
        @pl.when(me == device)
        def _():
            pl.semaphore_wait(barrier, count)

    copies = []
    for number, (pairs, source, slot) in enumerate(patterns):
        for a, b in pairs:
            copy = pltpu.make_async_remote_copy(
                src_ref=send_ref.at[source],
                dst_ref=recv_ref.at[slot],
                send_sem=send_sems.at[number],
                recv_sem=recv_sems.at[slot],
                device_id={axis: b},
                device_id_type=MESH,
            )
            copies.append((a, b, copy))

            @pl.when(me == a)
            def _():
                copy.start()

    for a, b, copy in copies:
        @pl.when(me == a)
        def _():
            copy.wait_send()

        @pl.when(me == b)
        def _():
            copy.wait_recv()


def exchange(pieces, patterns, slots, axis, identity):
    me = lax.axis_index(axis)
    remote = [([(a, b) for a, b in pairs if a != b], source, slot) for pairs, source, slot in patterns]
    remote = [entry for entry in remote if entry[0]]
    shape = pieces.shape[1:]
    received = pl.pallas_call(
        lambda *refs: exchange_kernel(axis, remote, *refs),
        out_shape=jax.ShapeDtypeStruct((slots,) + shape, pieces.dtype),
        in_specs=[pl.BlockSpec(memory_space=pl.ANY)],
        out_specs=pl.BlockSpec(memory_space=pl.ANY),
        scratch_shapes=[
            pltpu.SemaphoreType.DMA((len(remote),)),
            pltpu.SemaphoreType.DMA((slots,)),
        ],
        compiler_params=pltpu.CompilerParams(collective_id=identity, has_side_effects=True),
    )(pieces)
    parts = [received[slot] for slot in range(slots)]
    for pairs, source, slot in patterns:
        for a, b in pairs:
            if a == b:
                parts[slot] = jnp.where(me == a, pieces[source], parts[slot])
    return parts


def gather_kernel(axis, count, source, target, send_sems, recv_sems):
    me = lax.axis_index(axis)
    barrier = pltpu.get_barrier_semaphore()
    for delta in range(1, count):
        pl.semaphore_signal(
            barrier, 1, device_id={axis: (me + delta) % count}, device_id_type=MESH
        )
    pl.semaphore_wait(barrier, count - 1)
    outgoing = []
    for delta in range(1, count):
        copy = pltpu.make_async_remote_copy(
            src_ref=source,
            dst_ref=target.at[me],
            send_sem=send_sems.at[delta - 1],
            recv_sem=recv_sems.at[delta - 1],
            device_id={axis: (me + delta) % count},
            device_id_type=MESH,
        )
        copy.start()
        outgoing.append(copy)
    target[me] = source[...]
    for delta, copy in zip(range(1, count), outgoing):
        copy.wait_send()
        incoming = pltpu.make_async_remote_copy(
            src_ref=source,
            dst_ref=target.at[(me + count - delta) % count],
            send_sem=send_sems.at[delta - 1],
            recv_sem=recv_sems.at[delta - 1],
            device_id={axis: (me + count - delta) % count},
            device_id_type=MESH,
        )
        incoming.wait_recv()


def gather(block, axis, identity):
    count = lax.axis_size(axis)
    return pl.pallas_call(
        lambda *refs: gather_kernel(axis, count, *refs),
        out_shape=jax.ShapeDtypeStruct((count,) + block.shape, block.dtype),
        in_specs=[pl.BlockSpec(memory_space=pltpu.VMEM)],
        out_specs=pl.BlockSpec(memory_space=pltpu.VMEM),
        scratch_shapes=[
            pltpu.SemaphoreType.DMA((count - 1,)),
            pltpu.SemaphoreType.DMA((count - 1,)),
        ],
        compiler_params=pltpu.CompilerParams(collective_id=identity, has_side_effects=True),
    )(block)


def flat(block):
    size = block.size
    return block.reshape(size // 128, 128) if size % 128 == 0 else block.reshape(-1, block.shape[-1])


def per_device(
    parent_fields,
    parent_velocity,
    parent_mixing,
    nest_fields,
    nest_velocity,
    nest_mixing,
    nest_anchor,
):
    row_rank = lax.axis_index("gx")
    column_rank = lax.axis_index("gy")
    row_devices = lax.axis_size("gx")
    column_devices = lax.axis_size("gy")
    parent_rows = parent_fields.shape[2]
    parent_columns = parent_fields.shape[3]
    nest_rows = nest_fields.shape[2]
    nest_columns = nest_fields.shape[3]
    span_rows = nest_rows // 3
    span_columns = nest_columns // 3
    ratio = parent_columns // span_columns
    base = column_devices // 2
    base_column = base * parent_columns
    relay_rows = span_rows + 2
    relay_columns = span_columns + 2
    row_anchor = nest_anchor[0]
    column_anchor = nest_anchor[1]
    offset = column_anchor - 1 - base_column

    parent_next = update(
        parent_fields, neighbours(parent_fields, 2), parent_velocity, parent_mixing
    )

    margin = parent_columns - span_columns
    wide = jnp.pad(parent_next, ((0, 0), (0, 0), (0, 0), (margin, margin)))
    straddle = (ratio - 1) * span_columns - 2
    regimes = (
        lambda k, extra: not (extra == 1 and k == ratio - 2),
        lambda k, extra: True,
        lambda k, extra: not (extra == 0 and k == ratio - 1),
    )
    regime = (offset > straddle - span_columns).astype(jnp.int32) + (
        offset > straddle - span_columns + 1
    ).astype(jnp.int32)
    pieces = []
    routes = []
    for extra in (0, 1):
        for k in range(ratio):
            if extra == 1 and k == 0:
                continue
            start = margin + span_columns * k + offset - extra * parent_columns
            piece = lax.dynamic_slice_in_dim(wide, start, relay_columns, axis=3)
            routes.append((k, extra, len(pieces)))
            pieces.append(flat(piece))
    stacked_pieces = jnp.stack(pieces)
    branches = []
    for number, active in enumerate(regimes):
        patterns = [
            (column_pairs(column_devices, base, ratio, k, extra), index, extra)
            for k, extra, index in routes
            if active(k, extra)
        ]
        identity = (0, 6, 7)[number]
        branches.append(
            lambda stacked, patterns=patterns, identity=identity: tuple(
                exchange(stacked, patterns, 2, "gy", identity)
            )
        )
    within_part, beyond_part = lax.switch(regime, branches, stacked_pieces)
    piece_shape = parent_next.shape[:3] + (relay_columns,)
    own_k = column_rank % ratio
    within_live = jnp.logical_not((regime == 2) & (own_k == ratio - 1))
    beyond_live = (own_k != 0) & jnp.logical_not((regime == 0) & (own_k == ratio - 2))
    relay_cols = jnp.where(within_live, within_part.reshape(piece_shape), 0.0) + jnp.where(
        beyond_live, beyond_part.reshape(piece_shape), 0.0
    )

    padded = jnp.pad(relay_cols, ((0, 0), (0, 0), (relay_rows, relay_rows), (0, 0)))
    slots = []
    for target in range(row_devices):
        first = row_anchor - 1 + span_rows * target - parent_rows * row_rank
        first = jnp.clip(first, -relay_rows, parent_rows) + relay_rows
        slots.append(lax.dynamic_slice_in_dim(padded, first, relay_rows, axis=2))
    stacked = jnp.stack(slots, axis=0)
    received = lax.all_to_all(stacked, "gx", split_axis=0, concat_axis=0, tiled=True)
    relay = jnp.sum(received, axis=0)

    forcing = refine_columns(refine_rows(relay))
    row_global = row_rank * nest_rows + jnp.arange(nest_rows, dtype=jnp.int32)
    column_global = column_rank * nest_columns + jnp.arange(nest_columns, dtype=jnp.int32)
    weight = relax_weight(
        row_global, column_global, row_devices * nest_rows, column_devices * nest_columns
    )
    state = nest_fields
    for substep in range(SUBSTEPS):
        moved = update(state, neighbours(state, 3 + substep), nest_velocity, nest_mixing)
        state = moved + weight * (forcing - moved)

    coarse = block_mean(state)
    fields_count, levels_count = coarse.shape[:2]
    collected = gather(coarse.reshape((-1,) + coarse.shape[2:]), "gx", 9)
    gathered = jnp.moveaxis(collected, 0, 1).reshape(
        fields_count, levels_count, row_devices * span_rows, coarse.shape[3]
    )
    total_span = row_devices * span_rows
    gathered = jnp.pad(gathered, ((0, 0), (0, 0), (parent_rows, parent_rows), (0, 0)))
    first = jnp.clip(parent_rows * row_rank - row_anchor, -parent_rows, total_span)
    strip = lax.dynamic_slice_in_dim(gathered, first + parent_rows, parent_rows, axis=2)

    routes = []
    for extra in (1, 0):
        for k in range(ratio):
            if extra == 1 and k == 0:
                continue
            pairs = [(j, p) for (p, j) in column_pairs(column_devices, base, ratio, k, extra)]
            routes.append((k, extra, pairs))
    back_branches = []
    for number, skipped in enumerate(((1, 1), (0, ratio - 1))):
        patterns = [
            (pairs, 0, slot) for slot, (k, extra, pairs) in enumerate(routes)
            if (k, extra) != (skipped[1], skipped[0])
        ]
        identity = (1, 8)[number]
        back_branches.append(
            lambda sent, patterns=patterns, identity=identity: tuple(
                exchange(sent, patterns, len(routes), "gy", identity)
            )
        )
    late = (offset > (ratio - 1) * span_columns - span_columns - 1).astype(jnp.int32)
    parts = lax.switch(late, back_branches, flat(strip)[None])
    joined = jnp.concatenate([part.reshape(strip.shape) for part in parts], axis=3)
    start = (ratio - 1) * span_columns - 1 - offset
    fed_back = lax.dynamic_slice_in_dim(joined, start, parent_columns, axis=3)

    relative_rows = row_rank * parent_rows + jnp.arange(parent_rows, dtype=jnp.int32) - row_anchor
    relative_columns = (
        column_rank * parent_columns + jnp.arange(parent_columns, dtype=jnp.int32) - column_anchor
    )
    rows_valid = within(relative_rows, total_span)
    columns_valid = within(relative_columns, column_devices * span_columns)
    covered = rows_valid[:, None] & columns_valid[None, :]
    parent_result = jnp.where(covered, fed_back, parent_next)
    return (parent_result, state)


def solution(mesh):
    placed = (
        P(None, None, "gx", "gy"),
        P(None, None, "gx", "gy"),
        P(None, "gx", "gy"),
        P(None, None, "gx", "gy"),
        P(None, None, "gx", "gy"),
        P(None, "gx", "gy"),
        P(),
    )
    return jax.shard_map(
        per_device,
        mesh=mesh,
        in_specs=placed,
        out_specs=(P(None, None, "gx", "gy"), P(None, None, "gx", "gy")),
        check_vma=False,
    )
```

```python
import jax
import jax.numpy as jnp
from jax import lax
from jax.experimental import pallas as pl
from jax.experimental.pallas import tpu as pltpu
from jax.sharding import PartitionSpec as P

MESH = pl.DeviceIdType.MESH

SUBSTEPS = 3


third = 1.0 / 3.0
two_thirds = 2.0 / 3.0
nudge_floor = 0.1
relax_width = 4.0


def shift_pairs(count, step):
    return [(i, i + step) for i in range(count) if 0 <= i + step < count]


def halo_kernel(rows, cols, *refs):
    sources, targets, send_sems, recv_sems = refs[:4], refs[4:8], refs[8], refs[9]
    x = lax.axis_index("gx")
    y = lax.axis_index("gy")
    routes = (("gx", x, 1, rows), ("gx", x, -1, rows), ("gy", y, 1, cols), ("gy", y, -1, cols))
    barrier = pltpu.get_barrier_semaphore()
    for axis, own, step, count in routes:
        @pl.when((own + step >= 0) & (own + step < count))
        def _():
            pl.semaphore_signal(barrier, 1, device_id={axis: own + step}, device_id_type=MESH)

    peers = (x + rows - 1) // rows + (2 * rows - 2 - x) // rows
    peers = peers + (y + cols - 1) // cols + (2 * cols - 2 - y) // cols
    pl.semaphore_wait(barrier, peers)
    copies = []
    for number, (axis, own, step, count) in enumerate(routes):
        copy = pltpu.make_async_remote_copy(
            src_ref=sources[number],
            dst_ref=targets[number],
            send_sem=send_sems.at[number],
            recv_sem=recv_sems.at[number],
            device_id={axis: own + step},
            device_id_type=MESH,
        )
        copies.append((own, step, count, copy))

        @pl.when((own + step >= 0) & (own + step < count))
        def _():
            copy.start()

    for number, (own, step, count, copy) in enumerate(copies):
        @pl.when((own + step >= 0) & (own + step < count))
        def _():
            copy.wait_send()

        @pl.when((own - step >= 0) & (own - step < count))
        def _():
            copy.wait_recv()

        @pl.when((own - step < 0) | (own - step >= count))
        def _():
            targets[number][...] = jnp.zeros(targets[number].shape, targets[number].dtype)


def neighbours(cells, identity):
    rows = lax.axis_size("gx")
    cols = lax.axis_size("gy")
    x = lax.axis_index("gx")
    y = lax.axis_index("gy")
    fields, levels, height, width = cells.shape
    planes = fields * levels
    sources = (
        cells[:, :, -1, :].reshape(planes, width),
        cells[:, :, 0, :].reshape(planes, width),
        cells[:, :, :, -1].reshape(planes, height),
        cells[:, :, :, 0].reshape(planes, height),
    )
    received = pl.pallas_call(
        lambda *refs: halo_kernel(rows, cols, *refs),
        out_shape=tuple(jax.ShapeDtypeStruct(part.shape, part.dtype) for part in sources),
        in_specs=[pl.BlockSpec(memory_space=pltpu.VMEM)] * 4,
        out_specs=tuple(pl.BlockSpec(memory_space=pltpu.VMEM) for _ in range(4)),
        scratch_shapes=[pltpu.SemaphoreType.DMA((4,)), pltpu.SemaphoreType.DMA((4,))],
        compiler_params=pltpu.CompilerParams(collective_id=identity, has_side_effects=True),
    )(*sources)
    western, eastern, southern, northern = received
    western = western.reshape(fields, levels, 1, width)
    eastern = eastern.reshape(fields, levels, 1, width)
    southern = southern.reshape(fields, levels, height, 1)
    northern = northern.reshape(fields, levels, height, 1)
    return western, eastern, southern, northern


def update(values, halo, velocity, mixing):
    west_row, east_row, south_col, north_col = halo
    western = jnp.concatenate([west_row, values[:, :, :-1, :]], axis=2)
    eastern = jnp.concatenate([values[:, :, 1:, :], east_row], axis=2)
    southern = jnp.concatenate([south_col, values[:, :, :, :-1]], axis=3)
    northern = jnp.concatenate([values[:, :, :, 1:], north_col], axis=3)
    along_rows = velocity[0]
    along_columns = velocity[1]
    upwind = (
        jnp.maximum(along_rows, 0.0) * (values - western)
        + jnp.minimum(along_rows, 0.0) * (eastern - values)
        + jnp.maximum(along_columns, 0.0) * (values - southern)
        + jnp.minimum(along_columns, 0.0) * (northern - values)
    )
    return values - upwind + mixing * (eastern + western + northern + southern - 4.0 * values)


def refine_rows(block):
    lower = block[:, :, :-2]
    centre = block[:, :, 1:-1]
    upper = block[:, :, 2:]
    stacked = jnp.stack(
        (third * lower + two_thirds * centre, centre, two_thirds * centre + third * upper), axis=3
    )
    extent = centre.shape
    return stacked.reshape(extent[0], extent[1], 3 * extent[2], extent[3])


def refine_columns(block):
    lower = block[:, :, :, :-2]
    centre = block[:, :, :, 1:-1]
    upper = block[:, :, :, 2:]
    stacked = jnp.stack(
        (third * lower + two_thirds * centre, centre, two_thirds * centre + third * upper), axis=4
    )
    extent = centre.shape
    return stacked.reshape(extent[0], extent[1], extent[2], 3 * extent[3])


def refining(count):
    fine = jnp.arange(3 * count, dtype=jnp.int32)[:, None]
    coarse = jnp.arange(count + 2, dtype=jnp.int32)[None, :]
    centre = fine // 3 + 1
    phase = fine % 3
    lower = jnp.where(phase == 0, third, jnp.where(phase == 2, 0.0, 0.0))
    upper = jnp.where(phase == 2, third, 0.0)
    middle = jnp.where(phase == 1, 1.0, two_thirds)
    return (
        jnp.where(coarse == centre, middle, 0.0)
        + jnp.where(coarse == centre - 1, lower, 0.0)
        + jnp.where(coarse == centre + 1, upper, 0.0)
    ).astype(jnp.float32)


def refine(block):
    exact = lax.Precision.HIGHEST
    rows = block.shape[2] - 2
    cols = block.shape[3] - 2
    down = jnp.einsum("ar,flrc->flac", refining(rows), block, precision=exact)
    return jnp.einsum("flac,bc->flab", down, refining(cols), precision=exact)


def grouping(count):
    rows = jnp.arange(count, dtype=jnp.int32)[:, None] // 3
    return (rows == jnp.arange(count // 3, dtype=jnp.int32)[None, :]).astype(jnp.float32)


def block_mean(state):
    extent = state.shape
    exact = lax.Precision.HIGHEST
    across = jnp.einsum("flrc,cb->flrb", state, grouping(extent[3]), precision=exact)
    down = jnp.einsum("ra,flrb->flab", grouping(extent[2]), across, precision=exact)
    return down / 9.0


def relax_weight(row_global, column_global, total_rows, total_columns):
    row_distance = jnp.minimum(row_global, total_rows - 1 - row_global)
    column_distance = jnp.minimum(column_global, total_columns - 1 - column_global)
    distance = jnp.minimum(row_distance[:, None], column_distance[None, :]).astype(jnp.float32)
    return nudge_floor + (1.0 - nudge_floor) * jnp.exp(-distance / relax_width)


def within(positions, limit):
    return (positions >= 0) & (positions < limit)


def column_pairs(count, base, ratio, k, extra):
    pairs = []
    for m in range(count):
        j = ratio * m + k
        p = base + m + extra
        if j < count and p < count:
            pairs.append((p, j))
    return pairs


def exchange_kernel(axis, patterns, send_ref, recv_ref, send_sems, recv_sems):
    me = lax.axis_index(axis)
    barrier = pltpu.get_barrier_semaphore()
    links = [pair for pairs, _, _ in patterns for pair in pairs]
    for a, b in links:
        @pl.when(me == a)
        def _():
            pl.semaphore_signal(barrier, 1, device_id={axis: b}, device_id_type=MESH)

        @pl.when(me == b)
        def _():
            pl.semaphore_signal(barrier, 1, device_id={axis: a}, device_id_type=MESH)

    peers = {}
    for a, b in links:
        peers[a] = peers.get(a, 0) + 1
        peers[b] = peers.get(b, 0) + 1
    for device, count in sorted(peers.items()):
        @pl.when(me == device)
        def _():
            pl.semaphore_wait(barrier, count)

    copies = []
    for number, (pairs, source, slot) in enumerate(patterns):
        for a, b in pairs:
            copy = pltpu.make_async_remote_copy(
                src_ref=send_ref.at[source],
                dst_ref=recv_ref.at[slot],
                send_sem=send_sems.at[number],
                recv_sem=recv_sems.at[slot],
                device_id={axis: b},
                device_id_type=MESH,
            )
            copies.append((a, b, copy))

            @pl.when(me == a)
            def _():
                copy.start()

    for a, b, copy in copies:
        @pl.when(me == a)
        def _():
            copy.wait_send()

        @pl.when(me == b)
        def _():
            copy.wait_recv()


def exchange(pieces, patterns, slots, axis, identity):
    me = lax.axis_index(axis)
    remote = [([(a, b) for a, b in pairs if a != b], source, slot) for pairs, source, slot in patterns]
    remote = [entry for entry in remote if entry[0]]
    shape = pieces.shape[1:]
    received = pl.pallas_call(
        lambda *refs: exchange_kernel(axis, remote, *refs),
        out_shape=jax.ShapeDtypeStruct((slots,) + shape, pieces.dtype),
        in_specs=[pl.BlockSpec(memory_space=pl.ANY)],
        out_specs=pl.BlockSpec(memory_space=pl.ANY),
        scratch_shapes=[
            pltpu.SemaphoreType.DMA((len(remote),)),
            pltpu.SemaphoreType.DMA((slots,)),
        ],
        compiler_params=pltpu.CompilerParams(collective_id=identity, has_side_effects=True),
    )(pieces)
    parts = [received[slot] for slot in range(slots)]
    for pairs, source, slot in patterns:
        for a, b in pairs:
            if a == b:
                parts[slot] = jnp.where(me == a, pieces[source], parts[slot])
    return parts


def gather_kernel(axis, count, source, target, send_sems, recv_sems):
    me = lax.axis_index(axis)
    barrier = pltpu.get_barrier_semaphore()
    for delta in range(1, count):
        pl.semaphore_signal(
            barrier, 1, device_id={axis: (me + delta) % count}, device_id_type=MESH
        )
    pl.semaphore_wait(barrier, count - 1)
    outgoing = []
    for delta in range(1, count):
        copy = pltpu.make_async_remote_copy(
            src_ref=source,
            dst_ref=target.at[me],
            send_sem=send_sems.at[delta - 1],
            recv_sem=recv_sems.at[delta - 1],
            device_id={axis: (me + delta) % count},
            device_id_type=MESH,
        )
        copy.start()
        outgoing.append(copy)
    target[me] = source[...]
    for delta, copy in zip(range(1, count), outgoing):
        copy.wait_send()
        incoming = pltpu.make_async_remote_copy(
            src_ref=source,
            dst_ref=target.at[(me + count - delta) % count],
            send_sem=send_sems.at[delta - 1],
            recv_sem=recv_sems.at[delta - 1],
            device_id={axis: (me + count - delta) % count},
            device_id_type=MESH,
        )
        incoming.wait_recv()


def gather(block, axis, identity):
    count = lax.axis_size(axis)
    return pl.pallas_call(
        lambda *refs: gather_kernel(axis, count, *refs),
        out_shape=jax.ShapeDtypeStruct((count,) + block.shape, block.dtype),
        in_specs=[pl.BlockSpec(memory_space=pltpu.VMEM)],
        out_specs=pl.BlockSpec(memory_space=pltpu.VMEM),
        scratch_shapes=[
            pltpu.SemaphoreType.DMA((count - 1,)),
            pltpu.SemaphoreType.DMA((count - 1,)),
        ],
        compiler_params=pltpu.CompilerParams(collective_id=identity, has_side_effects=True),
    )(block)


def flat(block):
    size = block.size
    return block.reshape(size // 128, 128) if size % 128 == 0 else block.reshape(-1, block.shape[-1])


def per_device(
    parent_fields,
    parent_velocity,
    parent_mixing,
    nest_fields,
    nest_velocity,
    nest_mixing,
    nest_anchor,
):
    row_rank = lax.axis_index("gx")
    column_rank = lax.axis_index("gy")
    row_devices = lax.axis_size("gx")
    column_devices = lax.axis_size("gy")
    parent_rows = parent_fields.shape[2]
    parent_columns = parent_fields.shape[3]
    nest_rows = nest_fields.shape[2]
    nest_columns = nest_fields.shape[3]
    span_rows = nest_rows // 3
    span_columns = nest_columns // 3
    ratio = parent_columns // span_columns
    base = column_devices // 2
    base_column = base * parent_columns
    relay_rows = span_rows + 2
    relay_columns = span_columns + 2
    row_anchor = nest_anchor[0]
    column_anchor = nest_anchor[1]
    offset = column_anchor - 1 - base_column

    parent_next = update(
        parent_fields, neighbours(parent_fields, 2), parent_velocity, parent_mixing
    )

    margin = parent_columns - span_columns
    wide = jnp.pad(parent_next, ((0, 0), (0, 0), (0, 0), (margin, margin)))
    straddle = (ratio - 1) * span_columns - 2
    regimes = (
        lambda k, extra: not (extra == 1 and k == ratio - 2),
        lambda k, extra: True,
        lambda k, extra: not (extra == 0 and k == ratio - 1),
    )
    regime = (offset > straddle - span_columns).astype(jnp.int32) + (
        offset > straddle - span_columns + 1
    ).astype(jnp.int32)
    pieces = []
    routes = []
    for extra in (0, 1):
        for k in range(ratio):
            if extra == 1 and k == 0:
                continue
            start = margin + span_columns * k + offset - extra * parent_columns
            piece = lax.dynamic_slice_in_dim(wide, start, relay_columns, axis=3)
            routes.append((k, extra, len(pieces)))
            pieces.append(flat(piece))
    stacked_pieces = jnp.stack(pieces)
    branches = []
    for number, active in enumerate(regimes):
        patterns = [
            (column_pairs(column_devices, base, ratio, k, extra), index, extra)
            for k, extra, index in routes
            if active(k, extra)
        ]
        identity = (0, 6, 7)[number]
        branches.append(
            lambda stacked, patterns=patterns, identity=identity: tuple(
                exchange(stacked, patterns, 2, "gy", identity)
            )
        )
    within_part, beyond_part = lax.switch(regime, branches, stacked_pieces)
    piece_shape = parent_next.shape[:3] + (relay_columns,)
    own_k = column_rank % ratio
    within_live = jnp.logical_not((regime == 2) & (own_k == ratio - 1))
    beyond_live = (own_k != 0) & jnp.logical_not((regime == 0) & (own_k == ratio - 2))
    relay_cols = jnp.where(within_live, within_part.reshape(piece_shape), 0.0) + jnp.where(
        beyond_live, beyond_part.reshape(piece_shape), 0.0
    )

    padded = jnp.pad(relay_cols, ((0, 0), (0, 0), (relay_rows, relay_rows), (0, 0)))
    slots = []
    for target in range(row_devices):
        first = row_anchor - 1 + span_rows * target - parent_rows * row_rank
        first = jnp.clip(first, -relay_rows, parent_rows) + relay_rows
        slots.append(lax.dynamic_slice_in_dim(padded, first, relay_rows, axis=2))
    stacked = jnp.stack(slots, axis=0)
    received = lax.all_to_all(stacked, "gx", split_axis=0, concat_axis=0, tiled=True)
    relay = jnp.sum(received, axis=0)

    forcing = refine(relay)
    row_global = row_rank * nest_rows + jnp.arange(nest_rows, dtype=jnp.int32)
    column_global = column_rank * nest_columns + jnp.arange(nest_columns, dtype=jnp.int32)
    weight = relax_weight(
        row_global, column_global, row_devices * nest_rows, column_devices * nest_columns
    )
    state = nest_fields
    for substep in range(SUBSTEPS):
        moved = update(state, neighbours(state, 3 + substep), nest_velocity, nest_mixing)
        state = moved + weight * (forcing - moved)

    coarse = block_mean(state)
    fields_count, levels_count = coarse.shape[:2]
    collected = gather(coarse.reshape((-1,) + coarse.shape[2:]), "gx", 9)
    gathered = jnp.moveaxis(collected, 0, 1).reshape(
        fields_count, levels_count, row_devices * span_rows, coarse.shape[3]
    )
    total_span = row_devices * span_rows
    gathered = jnp.pad(gathered, ((0, 0), (0, 0), (parent_rows, parent_rows), (0, 0)))
    first = jnp.clip(parent_rows * row_rank - row_anchor, -parent_rows, total_span)
    strip = lax.dynamic_slice_in_dim(gathered, first + parent_rows, parent_rows, axis=2)

    routes = []
    for extra in (1, 0):
        for k in range(ratio):
            if extra == 1 and k == 0:
                continue
            pairs = [(j, p) for (p, j) in column_pairs(column_devices, base, ratio, k, extra)]
            routes.append((k, extra, pairs))
    back_branches = []
    for number, skipped in enumerate(((1, 1), (0, ratio - 1))):
        patterns = [
            (pairs, 0, slot) for slot, (k, extra, pairs) in enumerate(routes)
            if (k, extra) != (skipped[1], skipped[0])
        ]
        identity = (1, 8)[number]
        back_branches.append(
            lambda sent, patterns=patterns, identity=identity: tuple(
                exchange(sent, patterns, len(routes), "gy", identity)
            )
        )
    late = (offset > (ratio - 1) * span_columns - span_columns - 1).astype(jnp.int32)
    parts = lax.switch(late, back_branches, flat(strip)[None])
    joined = jnp.concatenate([part.reshape(strip.shape) for part in parts], axis=3)
    start = (ratio - 1) * span_columns - 1 - offset
    fed_back = lax.dynamic_slice_in_dim(joined, start, parent_columns, axis=3)

    relative_rows = row_rank * parent_rows + jnp.arange(parent_rows, dtype=jnp.int32) - row_anchor
    relative_columns = (
        column_rank * parent_columns + jnp.arange(parent_columns, dtype=jnp.int32) - column_anchor
    )
    rows_valid = within(relative_rows, total_span)
    columns_valid = within(relative_columns, column_devices * span_columns)
    covered = rows_valid[:, None] & columns_valid[None, :]
    parent_result = jnp.where(covered, fed_back, parent_next)
    return (parent_result, state)


def solution(mesh):
    placed = (
        P(None, None, "gx", "gy"),
        P(None, None, "gx", "gy"),
        P(None, "gx", "gy"),
        P(None, None, "gx", "gy"),
        P(None, None, "gx", "gy"),
        P(None, "gx", "gy"),
        P(),
    )
    return jax.shard_map(
        per_device,
        mesh=mesh,
        in_specs=placed,
        out_specs=(P(None, None, "gx", "gy"), P(None, None, "gx", "gy")),
        check_vma=False,
    )
```

```python
import jax
import jax.numpy as jnp
from jax import lax
from jax.experimental import pallas as pl
from jax.experimental.pallas import tpu as pltpu
from jax.sharding import PartitionSpec as P

MESH = pl.DeviceIdType.MESH

SUBSTEPS = 3


third = 1.0 / 3.0
two_thirds = 2.0 / 3.0
nudge_floor = 0.1
relax_width = 4.0


def shift_pairs(count, step):
    return [(i, i + step) for i in range(count) if 0 <= i + step < count]


def halo_kernel(rows, cols, *refs):
    sources, targets, send_sems, recv_sems = refs[:4], refs[4:8], refs[8], refs[9]
    x = lax.axis_index("gx")
    y = lax.axis_index("gy")
    routes = (("gx", x, 1, rows), ("gx", x, -1, rows), ("gy", y, 1, cols), ("gy", y, -1, cols))
    barrier = pltpu.get_barrier_semaphore()
    for axis, own, step, count in routes:
        @pl.when((own + step >= 0) & (own + step < count))
        def _():
            pl.semaphore_signal(barrier, 1, device_id={axis: own + step}, device_id_type=MESH)

    peers = (x + rows - 1) // rows + (2 * rows - 2 - x) // rows
    peers = peers + (y + cols - 1) // cols + (2 * cols - 2 - y) // cols
    pl.semaphore_wait(barrier, peers)
    copies = []
    for number, (axis, own, step, count) in enumerate(routes):
        copy = pltpu.make_async_remote_copy(
            src_ref=sources[number],
            dst_ref=targets[number],
            send_sem=send_sems.at[number],
            recv_sem=recv_sems.at[number],
            device_id={axis: own + step},
            device_id_type=MESH,
        )
        copies.append((own, step, count, copy))

        @pl.when((own + step >= 0) & (own + step < count))
        def _():
            copy.start()

    for number, (own, step, count, copy) in enumerate(copies):
        @pl.when((own + step >= 0) & (own + step < count))
        def _():
            copy.wait_send()

        @pl.when((own - step >= 0) & (own - step < count))
        def _():
            copy.wait_recv()

        @pl.when((own - step < 0) | (own - step >= count))
        def _():
            targets[number][...] = jnp.zeros(targets[number].shape, targets[number].dtype)


def neighbours(cells, identity):
    rows = lax.axis_size("gx")
    cols = lax.axis_size("gy")
    x = lax.axis_index("gx")
    y = lax.axis_index("gy")
    fields, levels, height, width = cells.shape
    planes = fields * levels
    sources = (
        cells[:, :, -1, :].reshape(planes, width),
        cells[:, :, 0, :].reshape(planes, width),
        cells[:, :, :, -1].reshape(planes, height),
        cells[:, :, :, 0].reshape(planes, height),
    )
    received = pl.pallas_call(
        lambda *refs: halo_kernel(rows, cols, *refs),
        out_shape=tuple(jax.ShapeDtypeStruct(part.shape, part.dtype) for part in sources),
        in_specs=[pl.BlockSpec(memory_space=pltpu.VMEM)] * 4,
        out_specs=tuple(pl.BlockSpec(memory_space=pltpu.VMEM) for _ in range(4)),
        scratch_shapes=[pltpu.SemaphoreType.DMA((4,)), pltpu.SemaphoreType.DMA((4,))],
        compiler_params=pltpu.CompilerParams(collective_id=identity, has_side_effects=True),
    )(*sources)
    western, eastern, southern, northern = received
    western = western.reshape(fields, levels, 1, width)
    eastern = eastern.reshape(fields, levels, 1, width)
    southern = southern.reshape(fields, levels, height, 1)
    northern = northern.reshape(fields, levels, height, 1)
    return western, eastern, southern, northern


def update(values, halo, velocity, mixing):
    west_row, east_row, south_col, north_col = halo
    western = jnp.concatenate([west_row, values[:, :, :-1, :]], axis=2)
    eastern = jnp.concatenate([values[:, :, 1:, :], east_row], axis=2)
    southern = jnp.concatenate([south_col, values[:, :, :, :-1]], axis=3)
    northern = jnp.concatenate([values[:, :, :, 1:], north_col], axis=3)
    along_rows = velocity[0]
    along_columns = velocity[1]
    upwind = (
        jnp.maximum(along_rows, 0.0) * (values - western)
        + jnp.minimum(along_rows, 0.0) * (eastern - values)
        + jnp.maximum(along_columns, 0.0) * (values - southern)
        + jnp.minimum(along_columns, 0.0) * (northern - values)
    )
    return values - upwind + mixing * (eastern + western + northern + southern - 4.0 * values)


def refine_rows(block):
    lower = block[:, :, :-2]
    centre = block[:, :, 1:-1]
    upper = block[:, :, 2:]
    stacked = jnp.stack(
        (third * lower + two_thirds * centre, centre, two_thirds * centre + third * upper), axis=3
    )
    extent = centre.shape
    return stacked.reshape(extent[0], extent[1], 3 * extent[2], extent[3])


def refine_columns(block):
    lower = block[:, :, :, :-2]
    centre = block[:, :, :, 1:-1]
    upper = block[:, :, :, 2:]
    stacked = jnp.stack(
        (third * lower + two_thirds * centre, centre, two_thirds * centre + third * upper), axis=4
    )
    extent = centre.shape
    return stacked.reshape(extent[0], extent[1], extent[2], 3 * extent[3])


def refining(count):
    fine = jnp.arange(3 * count, dtype=jnp.int32)[:, None]
    coarse = jnp.arange(count + 2, dtype=jnp.int32)[None, :]
    centre = fine // 3 + 1
    phase = fine % 3
    lower = jnp.where(phase == 0, third, jnp.where(phase == 2, 0.0, 0.0))
    upper = jnp.where(phase == 2, third, 0.0)
    middle = jnp.where(phase == 1, 1.0, two_thirds)
    return (
        jnp.where(coarse == centre, middle, 0.0)
        + jnp.where(coarse == centre - 1, lower, 0.0)
        + jnp.where(coarse == centre + 1, upper, 0.0)
    ).astype(jnp.float32)


def refine(block):
    exact = lax.Precision.HIGHEST
    rows = block.shape[2] - 2
    cols = block.shape[3] - 2
    down = jnp.einsum("ar,flrc->flac", refining(rows), block, precision=exact)
    return jnp.einsum("flac,bc->flab", down, refining(cols), precision=exact)


def grouping(count):
    rows = jnp.arange(count, dtype=jnp.int32)[:, None] // 3
    return (rows == jnp.arange(count // 3, dtype=jnp.int32)[None, :]).astype(jnp.float32)


def block_mean(state):
    extent = state.shape
    exact = lax.Precision.HIGHEST
    across = jnp.einsum("flrc,cb->flrb", state, grouping(extent[3]), precision=exact)
    down = jnp.einsum("ra,flrb->flab", grouping(extent[2]), across, precision=exact)
    return down / 9.0


def relax_weight(row_global, column_global, total_rows, total_columns):
    row_distance = jnp.minimum(row_global, total_rows - 1 - row_global)
    column_distance = jnp.minimum(column_global, total_columns - 1 - column_global)
    distance = jnp.minimum(row_distance[:, None], column_distance[None, :]).astype(jnp.float32)
    return nudge_floor + (1.0 - nudge_floor) * jnp.exp(-distance / relax_width)


def within(positions, limit):
    return (positions >= 0) & (positions < limit)


def column_pairs(count, base, ratio, k, extra):
    pairs = []
    for m in range(count):
        j = ratio * m + k
        p = base + m + extra
        if j < count and p < count:
            pairs.append((p, j))
    return pairs


def exchange_kernel(axis, patterns, send_ref, recv_ref, send_sems, recv_sems):
    me = lax.axis_index(axis)
    barrier = pltpu.get_barrier_semaphore()
    links = [pair for pairs, _, _ in patterns for pair in pairs]
    for a, b in links:
        @pl.when(me == a)
        def _():
            pl.semaphore_signal(barrier, 1, device_id={axis: b}, device_id_type=MESH)

        @pl.when(me == b)
        def _():
            pl.semaphore_signal(barrier, 1, device_id={axis: a}, device_id_type=MESH)

    peers = {}
    for a, b in links:
        peers[a] = peers.get(a, 0) + 1
        peers[b] = peers.get(b, 0) + 1
    for device, count in sorted(peers.items()):
        @pl.when(me == device)
        def _():
            pl.semaphore_wait(barrier, count)

    copies = []
    for number, (pairs, source, slot) in enumerate(patterns):
        for a, b in pairs:
            copy = pltpu.make_async_remote_copy(
                src_ref=send_ref.at[source],
                dst_ref=recv_ref.at[slot],
                send_sem=send_sems.at[number],
                recv_sem=recv_sems.at[slot],
                device_id={axis: b},
                device_id_type=MESH,
            )
            copies.append((a, b, copy))

            @pl.when(me == a)
            def _():
                copy.start()

    for a, b, copy in copies:
        @pl.when(me == a)
        def _():
            copy.wait_send()

        @pl.when(me == b)
        def _():
            copy.wait_recv()


def exchange(pieces, patterns, slots, axis, identity):
    me = lax.axis_index(axis)
    remote = [([(a, b) for a, b in pairs if a != b], source, slot) for pairs, source, slot in patterns]
    remote = [entry for entry in remote if entry[0]]
    shape = pieces.shape[1:]
    received = pl.pallas_call(
        lambda *refs: exchange_kernel(axis, remote, *refs),
        out_shape=jax.ShapeDtypeStruct((slots,) + shape, pieces.dtype),
        in_specs=[pl.BlockSpec(memory_space=pl.ANY)],
        out_specs=pl.BlockSpec(memory_space=pl.ANY),
        scratch_shapes=[
            pltpu.SemaphoreType.DMA((len(remote),)),
            pltpu.SemaphoreType.DMA((slots,)),
        ],
        compiler_params=pltpu.CompilerParams(collective_id=identity, has_side_effects=True),
    )(pieces)
    parts = [received[slot] for slot in range(slots)]
    for pairs, source, slot in patterns:
        for a, b in pairs:
            if a == b:
                parts[slot] = jnp.where(me == a, pieces[source], parts[slot])
    return parts


def gather_kernel(axis, count, source, target, send_sems, recv_sems):
    me = lax.axis_index(axis)
    barrier = pltpu.get_barrier_semaphore()
    for delta in range(1, count):
        pl.semaphore_signal(
            barrier, 1, device_id={axis: (me + delta) % count}, device_id_type=MESH
        )
    pl.semaphore_wait(barrier, count - 1)
    outgoing = []
    for delta in range(1, count):
        copy = pltpu.make_async_remote_copy(
            src_ref=source,
            dst_ref=target.at[me],
            send_sem=send_sems.at[delta - 1],
            recv_sem=recv_sems.at[delta - 1],
            device_id={axis: (me + delta) % count},
            device_id_type=MESH,
        )
        copy.start()
        outgoing.append(copy)
    target[me] = source[...]
    for delta, copy in zip(range(1, count), outgoing):
        copy.wait_send()
        incoming = pltpu.make_async_remote_copy(
            src_ref=source,
            dst_ref=target.at[(me + count - delta) % count],
            send_sem=send_sems.at[delta - 1],
            recv_sem=recv_sems.at[delta - 1],
            device_id={axis: (me + count - delta) % count},
            device_id_type=MESH,
        )
        incoming.wait_recv()


def gather(block, axis, identity):
    count = lax.axis_size(axis)
    return pl.pallas_call(
        lambda *refs: gather_kernel(axis, count, *refs),
        out_shape=jax.ShapeDtypeStruct((count,) + block.shape, block.dtype),
        in_specs=[pl.BlockSpec(memory_space=pltpu.VMEM)],
        out_specs=pl.BlockSpec(memory_space=pltpu.VMEM),
        scratch_shapes=[
            pltpu.SemaphoreType.DMA((count - 1,)),
            pltpu.SemaphoreType.DMA((count - 1,)),
        ],
        compiler_params=pltpu.CompilerParams(collective_id=identity, has_side_effects=True),
    )(block)


def stencil_kernel(relaxed, *refs):
    if relaxed:
        (values, velocity, mixing, western, eastern, southern, northern, forcing, weight, out) = refs
    else:
        (values, velocity, mixing, western, eastern, southern, northern, out) = refs
    levels, height, width = values.shape[1:]
    row = lax.broadcasted_iota(jnp.int32, (height, width), 0)
    col = lax.broadcasted_iota(jnp.int32, (height, width), 1)
    for level in range(levels):
        q = values[0, level]
        west = jnp.where(row == 0, western[0, level], pltpu.roll(q, 1, 0))
        east = jnp.where(row == height - 1, eastern[0, level], pltpu.roll(q, height - 1, 0))
        south = jnp.where(col == 0, southern[0, level], pltpu.roll(q, 1, 1))
        north = jnp.where(col == width - 1, northern[0, level], pltpu.roll(q, width - 1, 1))
        along_rows = velocity[0, level]
        along_columns = velocity[1, level]
        upwind = (
            jnp.maximum(along_rows, 0.0) * (q - west)
            + jnp.minimum(along_rows, 0.0) * (east - q)
            + jnp.maximum(along_columns, 0.0) * (q - south)
            + jnp.minimum(along_columns, 0.0) * (north - q)
        )
        moved = q - upwind + mixing[level] * (east + west + north + south - 4.0 * q)
        if relaxed:
            moved = moved + weight[...] * (forcing[0, level] - moved)
        out[0, level] = moved


def stencil(values, halo, velocity, mixing, forcing=None, weight=None):
    fields, levels, height, width = values.shape
    west_row, east_row, south_col, north_col = halo
    plane = pl.BlockSpec((1, levels, height, width), lambda f: (f, 0, 0, 0))
    edge_row = pl.BlockSpec((1, levels, 1, width), lambda f: (f, 0, 0, 0))
    edge_col = pl.BlockSpec((1, levels, height, 1), lambda f: (f, 0, 0, 0))
    operands = [values, velocity, mixing, west_row, east_row, south_col, north_col]
    specs = [
        plane,
        pl.BlockSpec(velocity.shape, lambda f: (0, 0, 0, 0)),
        pl.BlockSpec(mixing.shape, lambda f: (0, 0, 0)),
        edge_row,
        edge_row,
        edge_col,
        edge_col,
    ]
    relaxed = forcing is not None
    if relaxed:
        operands += [forcing, weight]
        specs += [plane, pl.BlockSpec(weight.shape, lambda f: (0, 0))]
    return pl.pallas_call(
        lambda *refs: stencil_kernel(relaxed, *refs),
        out_shape=jax.ShapeDtypeStruct(values.shape, values.dtype),
        grid=(fields,),
        in_specs=specs,
        out_specs=plane,
    )(*operands)


def flat(block):
    size = block.size
    return block.reshape(size // 128, 128) if size % 128 == 0 else block.reshape(-1, block.shape[-1])


def per_device(
    parent_fields,
    parent_velocity,
    parent_mixing,
    nest_fields,
    nest_velocity,
    nest_mixing,
    nest_anchor,
):
    row_rank = lax.axis_index("gx")
    column_rank = lax.axis_index("gy")
    row_devices = lax.axis_size("gx")
    column_devices = lax.axis_size("gy")
    parent_rows = parent_fields.shape[2]
    parent_columns = parent_fields.shape[3]
    nest_rows = nest_fields.shape[2]
    nest_columns = nest_fields.shape[3]
    span_rows = nest_rows // 3
    span_columns = nest_columns // 3
    ratio = parent_columns // span_columns
    base = column_devices // 2
    base_column = base * parent_columns
    relay_rows = span_rows + 2
    relay_columns = span_columns + 2
    row_anchor = nest_anchor[0]
    column_anchor = nest_anchor[1]
    offset = column_anchor - 1 - base_column

    parent_next = stencil(
        parent_fields, neighbours(parent_fields, 2), parent_velocity, parent_mixing
    )

    margin = parent_columns - span_columns
    wide = jnp.pad(parent_next, ((0, 0), (0, 0), (0, 0), (margin, margin)))
    straddle = (ratio - 1) * span_columns - 2
    regimes = (
        lambda k, extra: not (extra == 1 and k == ratio - 2),
        lambda k, extra: True,
        lambda k, extra: not (extra == 0 and k == ratio - 1),
    )
    regime = (offset > straddle - span_columns).astype(jnp.int32) + (
        offset > straddle - span_columns + 1
    ).astype(jnp.int32)
    pieces = []
    routes = []
    for extra in (0, 1):
        for k in range(ratio):
            if extra == 1 and k == 0:
                continue
            start = margin + span_columns * k + offset - extra * parent_columns
            piece = lax.dynamic_slice_in_dim(wide, start, relay_columns, axis=3)
            routes.append((k, extra, len(pieces)))
            pieces.append(flat(piece))
    stacked_pieces = jnp.stack(pieces)
    branches = []
    for number, active in enumerate(regimes):
        patterns = [
            (column_pairs(column_devices, base, ratio, k, extra), index, extra)
            for k, extra, index in routes
            if active(k, extra)
        ]
        identity = (0, 6, 7)[number]
        branches.append(
            lambda stacked, patterns=patterns, identity=identity: tuple(
                exchange(stacked, patterns, 2, "gy", identity)
            )
        )
    within_part, beyond_part = lax.switch(regime, branches, stacked_pieces)
    piece_shape = parent_next.shape[:3] + (relay_columns,)
    own_k = column_rank % ratio
    within_live = jnp.logical_not((regime == 2) & (own_k == ratio - 1))
    beyond_live = (own_k != 0) & jnp.logical_not((regime == 0) & (own_k == ratio - 2))
    relay_cols = jnp.where(within_live, within_part.reshape(piece_shape), 0.0) + jnp.where(
        beyond_live, beyond_part.reshape(piece_shape), 0.0
    )

    padded = jnp.pad(relay_cols, ((0, 0), (0, 0), (relay_rows, relay_rows), (0, 0)))
    slots = []
    for target in range(row_devices):
        first = row_anchor - 1 + span_rows * target - parent_rows * row_rank
        first = jnp.clip(first, -relay_rows, parent_rows) + relay_rows
        slots.append(lax.dynamic_slice_in_dim(padded, first, relay_rows, axis=2))
    stacked = jnp.stack(slots, axis=0)
    received = lax.all_to_all(stacked, "gx", split_axis=0, concat_axis=0, tiled=True)
    relay = jnp.sum(received, axis=0)

    forcing = refine(relay)
    row_global = row_rank * nest_rows + jnp.arange(nest_rows, dtype=jnp.int32)
    column_global = column_rank * nest_columns + jnp.arange(nest_columns, dtype=jnp.int32)
    weight = relax_weight(
        row_global, column_global, row_devices * nest_rows, column_devices * nest_columns
    )
    state = nest_fields
    for substep in range(SUBSTEPS):
        state = stencil(
            state, neighbours(state, 3 + substep), nest_velocity, nest_mixing, forcing, weight
        )

    coarse = block_mean(state)
    fields_count, levels_count = coarse.shape[:2]
    collected = gather(coarse.reshape((-1,) + coarse.shape[2:]), "gx", 9)
    gathered = jnp.moveaxis(collected, 0, 1).reshape(
        fields_count, levels_count, row_devices * span_rows, coarse.shape[3]
    )
    total_span = row_devices * span_rows
    gathered = jnp.pad(gathered, ((0, 0), (0, 0), (parent_rows, parent_rows), (0, 0)))
    first = jnp.clip(parent_rows * row_rank - row_anchor, -parent_rows, total_span)
    strip = lax.dynamic_slice_in_dim(gathered, first + parent_rows, parent_rows, axis=2)

    routes = []
    for extra in (1, 0):
        for k in range(ratio):
            if extra == 1 and k == 0:
                continue
            pairs = [(j, p) for (p, j) in column_pairs(column_devices, base, ratio, k, extra)]
            routes.append((k, extra, pairs))
    back_branches = []
    for number, skipped in enumerate(((1, 1), (0, ratio - 1))):
        patterns = [
            (pairs, 0, slot) for slot, (k, extra, pairs) in enumerate(routes)
            if (k, extra) != (skipped[1], skipped[0])
        ]
        identity = (1, 8)[number]
        back_branches.append(
            lambda sent, patterns=patterns, identity=identity: tuple(
                exchange(sent, patterns, len(routes), "gy", identity)
            )
        )
    late = (offset > (ratio - 1) * span_columns - span_columns - 1).astype(jnp.int32)
    parts = lax.switch(late, back_branches, flat(strip)[None])
    joined = jnp.concatenate([part.reshape(strip.shape) for part in parts], axis=3)
    start = (ratio - 1) * span_columns - 1 - offset
    fed_back = lax.dynamic_slice_in_dim(joined, start, parent_columns, axis=3)

    relative_rows = row_rank * parent_rows + jnp.arange(parent_rows, dtype=jnp.int32) - row_anchor
    relative_columns = (
        column_rank * parent_columns + jnp.arange(parent_columns, dtype=jnp.int32) - column_anchor
    )
    rows_valid = within(relative_rows, total_span)
    columns_valid = within(relative_columns, column_devices * span_columns)
    covered = rows_valid[:, None] & columns_valid[None, :]
    parent_result = jnp.where(covered, fed_back, parent_next)
    return (parent_result, state)


def solution(mesh):
    placed = (
        P(None, None, "gx", "gy"),
        P(None, None, "gx", "gy"),
        P(None, "gx", "gy"),
        P(None, None, "gx", "gy"),
        P(None, None, "gx", "gy"),
        P(None, "gx", "gy"),
        P(),
    )
    return jax.shard_map(
        per_device,
        mesh=mesh,
        in_specs=placed,
        out_specs=(P(None, None, "gx", "gy"), P(None, None, "gx", "gy")),
        check_vma=False,
    )
```

```python
import jax
import jax.numpy as jnp
from jax import lax
from jax.experimental import pallas as pl
from jax.experimental.pallas import tpu as pltpu
from jax.sharding import PartitionSpec as P

MESH = pl.DeviceIdType.MESH

SUBSTEPS = 3


third = 1.0 / 3.0
two_thirds = 2.0 / 3.0
nudge_floor = 0.1
relax_width = 4.0


def shift_pairs(count, step):
    return [(i, i + step) for i in range(count) if 0 <= i + step < count]


def halo_kernel(rows, cols, *refs):
    sources, targets, send_sems, recv_sems = refs[:4], refs[4:8], refs[8], refs[9]
    x = lax.axis_index("gx")
    y = lax.axis_index("gy")
    routes = (("gx", x, 1, rows), ("gx", x, -1, rows), ("gy", y, 1, cols), ("gy", y, -1, cols))
    barrier = pltpu.get_barrier_semaphore()
    for axis, own, step, count in routes:
        @pl.when((own + step >= 0) & (own + step < count))
        def _():
            pl.semaphore_signal(barrier, 1, device_id={axis: own + step}, device_id_type=MESH)

    peers = (x + rows - 1) // rows + (2 * rows - 2 - x) // rows
    peers = peers + (y + cols - 1) // cols + (2 * cols - 2 - y) // cols
    pl.semaphore_wait(barrier, peers)
    copies = []
    for number, (axis, own, step, count) in enumerate(routes):
        copy = pltpu.make_async_remote_copy(
            src_ref=sources[number],
            dst_ref=targets[number],
            send_sem=send_sems.at[number],
            recv_sem=recv_sems.at[number],
            device_id={axis: own + step},
            device_id_type=MESH,
        )
        copies.append((own, step, count, copy))

        @pl.when((own + step >= 0) & (own + step < count))
        def _():
            copy.start()

    for number, (own, step, count, copy) in enumerate(copies):
        @pl.when((own + step >= 0) & (own + step < count))
        def _():
            copy.wait_send()

        @pl.when((own - step >= 0) & (own - step < count))
        def _():
            copy.wait_recv()

        @pl.when((own - step < 0) | (own - step >= count))
        def _():
            targets[number][...] = jnp.zeros(targets[number].shape, targets[number].dtype)


def neighbours(cells, identity):
    rows = lax.axis_size("gx")
    cols = lax.axis_size("gy")
    x = lax.axis_index("gx")
    y = lax.axis_index("gy")
    fields, levels, height, width = cells.shape
    planes = fields * levels
    sources = (
        cells[:, :, -1, :].reshape(planes, width),
        cells[:, :, 0, :].reshape(planes, width),
        cells[:, :, :, -1].reshape(planes, height),
        cells[:, :, :, 0].reshape(planes, height),
    )
    received = pl.pallas_call(
        lambda *refs: halo_kernel(rows, cols, *refs),
        out_shape=tuple(jax.ShapeDtypeStruct(part.shape, part.dtype) for part in sources),
        in_specs=[pl.BlockSpec(memory_space=pltpu.VMEM)] * 4,
        out_specs=tuple(pl.BlockSpec(memory_space=pltpu.VMEM) for _ in range(4)),
        scratch_shapes=[pltpu.SemaphoreType.DMA((4,)), pltpu.SemaphoreType.DMA((4,))],
        compiler_params=pltpu.CompilerParams(collective_id=identity, has_side_effects=True),
    )(*sources)
    western, eastern, southern, northern = received
    western = western.reshape(fields, levels, 1, width)
    eastern = eastern.reshape(fields, levels, 1, width)
    return western, eastern, southern, northern


def update(values, halo, velocity, mixing):
    west_row, east_row, south_col, north_col = halo
    western = jnp.concatenate([west_row, values[:, :, :-1, :]], axis=2)
    eastern = jnp.concatenate([values[:, :, 1:, :], east_row], axis=2)
    southern = jnp.concatenate([south_col, values[:, :, :, :-1]], axis=3)
    northern = jnp.concatenate([values[:, :, :, 1:], north_col], axis=3)
    along_rows = velocity[0]
    along_columns = velocity[1]
    upwind = (
        jnp.maximum(along_rows, 0.0) * (values - western)
        + jnp.minimum(along_rows, 0.0) * (eastern - values)
        + jnp.maximum(along_columns, 0.0) * (values - southern)
        + jnp.minimum(along_columns, 0.0) * (northern - values)
    )
    return values - upwind + mixing * (eastern + western + northern + southern - 4.0 * values)


def refine_rows(block):
    lower = block[:, :, :-2]
    centre = block[:, :, 1:-1]
    upper = block[:, :, 2:]
    stacked = jnp.stack(
        (third * lower + two_thirds * centre, centre, two_thirds * centre + third * upper), axis=3
    )
    extent = centre.shape
    return stacked.reshape(extent[0], extent[1], 3 * extent[2], extent[3])


def refine_columns(block):
    lower = block[:, :, :, :-2]
    centre = block[:, :, :, 1:-1]
    upper = block[:, :, :, 2:]
    stacked = jnp.stack(
        (third * lower + two_thirds * centre, centre, two_thirds * centre + third * upper), axis=4
    )
    extent = centre.shape
    return stacked.reshape(extent[0], extent[1], extent[2], 3 * extent[3])


def refining(count):
    fine = jnp.arange(3 * count, dtype=jnp.int32)[:, None]
    coarse = jnp.arange(count + 2, dtype=jnp.int32)[None, :]
    centre = fine // 3 + 1
    phase = fine % 3
    lower = jnp.where(phase == 0, third, jnp.where(phase == 2, 0.0, 0.0))
    upper = jnp.where(phase == 2, third, 0.0)
    middle = jnp.where(phase == 1, 1.0, two_thirds)
    return (
        jnp.where(coarse == centre, middle, 0.0)
        + jnp.where(coarse == centre - 1, lower, 0.0)
        + jnp.where(coarse == centre + 1, upper, 0.0)
    ).astype(jnp.float32)


def refine(block):
    exact = lax.Precision.HIGHEST
    rows = block.shape[2] - 2
    cols = block.shape[3] - 2
    down = jnp.einsum("ar,flrc->flac", refining(rows), block, precision=exact)
    return jnp.einsum("flac,bc->flab", down, refining(cols), precision=exact)


def grouping(count):
    rows = jnp.arange(count, dtype=jnp.int32)[:, None] // 3
    return (rows == jnp.arange(count // 3, dtype=jnp.int32)[None, :]).astype(jnp.float32)


def block_mean(state):
    extent = state.shape
    exact = lax.Precision.HIGHEST
    across = jnp.einsum("flrc,cb->flrb", state, grouping(extent[3]), precision=exact)
    down = jnp.einsum("ra,flrb->flab", grouping(extent[2]), across, precision=exact)
    return down / 9.0


def relax_weight(row_global, column_global, total_rows, total_columns):
    row_distance = jnp.minimum(row_global, total_rows - 1 - row_global)
    column_distance = jnp.minimum(column_global, total_columns - 1 - column_global)
    distance = jnp.minimum(row_distance[:, None], column_distance[None, :]).astype(jnp.float32)
    return nudge_floor + (1.0 - nudge_floor) * jnp.exp(-distance / relax_width)


def within(positions, limit):
    return (positions >= 0) & (positions < limit)


def column_pairs(count, base, ratio, k, extra):
    pairs = []
    for m in range(count):
        j = ratio * m + k
        p = base + m + extra
        if j < count and p < count:
            pairs.append((p, j))
    return pairs


def exchange_kernel(axis, patterns, send_ref, recv_ref, send_sems, recv_sems):
    me = lax.axis_index(axis)
    barrier = pltpu.get_barrier_semaphore()
    links = [pair for pairs, _, _ in patterns for pair in pairs]
    for a, b in links:
        @pl.when(me == a)
        def _():
            pl.semaphore_signal(barrier, 1, device_id={axis: b}, device_id_type=MESH)

        @pl.when(me == b)
        def _():
            pl.semaphore_signal(barrier, 1, device_id={axis: a}, device_id_type=MESH)

    peers = {}
    for a, b in links:
        peers[a] = peers.get(a, 0) + 1
        peers[b] = peers.get(b, 0) + 1
    for device, count in sorted(peers.items()):
        @pl.when(me == device)
        def _():
            pl.semaphore_wait(barrier, count)

    copies = []
    for number, (pairs, source, slot) in enumerate(patterns):
        for a, b in pairs:
            copy = pltpu.make_async_remote_copy(
                src_ref=send_ref.at[source],
                dst_ref=recv_ref.at[slot],
                send_sem=send_sems.at[number],
                recv_sem=recv_sems.at[slot],
                device_id={axis: b},
                device_id_type=MESH,
            )
            copies.append((a, b, copy))

            @pl.when(me == a)
            def _():
                copy.start()

    for a, b, copy in copies:
        @pl.when(me == a)
        def _():
            copy.wait_send()

        @pl.when(me == b)
        def _():
            copy.wait_recv()


def exchange(pieces, patterns, slots, axis, identity):
    me = lax.axis_index(axis)
    remote = [([(a, b) for a, b in pairs if a != b], source, slot) for pairs, source, slot in patterns]
    remote = [entry for entry in remote if entry[0]]
    shape = pieces.shape[1:]
    received = pl.pallas_call(
        lambda *refs: exchange_kernel(axis, remote, *refs),
        out_shape=jax.ShapeDtypeStruct((slots,) + shape, pieces.dtype),
        in_specs=[pl.BlockSpec(memory_space=pl.ANY)],
        out_specs=pl.BlockSpec(memory_space=pl.ANY),
        scratch_shapes=[
            pltpu.SemaphoreType.DMA((len(remote),)),
            pltpu.SemaphoreType.DMA((slots,)),
        ],
        compiler_params=pltpu.CompilerParams(collective_id=identity, has_side_effects=True),
    )(pieces)
    parts = [received[slot] for slot in range(slots)]
    for pairs, source, slot in patterns:
        for a, b in pairs:
            if a == b:
                parts[slot] = jnp.where(me == a, pieces[source], parts[slot])
    return parts


def gather_kernel(axis, count, source, target, send_sems, recv_sems):
    me = lax.axis_index(axis)
    barrier = pltpu.get_barrier_semaphore()
    for delta in range(1, count):
        pl.semaphore_signal(
            barrier, 1, device_id={axis: (me + delta) % count}, device_id_type=MESH
        )
    pl.semaphore_wait(barrier, count - 1)
    outgoing = []
    for delta in range(1, count):
        copy = pltpu.make_async_remote_copy(
            src_ref=source,
            dst_ref=target.at[me],
            send_sem=send_sems.at[delta - 1],
            recv_sem=recv_sems.at[delta - 1],
            device_id={axis: (me + delta) % count},
            device_id_type=MESH,
        )
        copy.start()
        outgoing.append(copy)
    target[me] = source[...]
    for delta, copy in zip(range(1, count), outgoing):
        copy.wait_send()
        incoming = pltpu.make_async_remote_copy(
            src_ref=source,
            dst_ref=target.at[(me + count - delta) % count],
            send_sem=send_sems.at[delta - 1],
            recv_sem=recv_sems.at[delta - 1],
            device_id={axis: (me + count - delta) % count},
            device_id_type=MESH,
        )
        incoming.wait_recv()


def gather(block, axis, identity):
    count = lax.axis_size(axis)
    return pl.pallas_call(
        lambda *refs: gather_kernel(axis, count, *refs),
        out_shape=jax.ShapeDtypeStruct((count,) + block.shape, block.dtype),
        in_specs=[pl.BlockSpec(memory_space=pltpu.VMEM)],
        out_specs=pl.BlockSpec(memory_space=pltpu.VMEM),
        scratch_shapes=[
            pltpu.SemaphoreType.DMA((count - 1,)),
            pltpu.SemaphoreType.DMA((count - 1,)),
        ],
        compiler_params=pltpu.CompilerParams(collective_id=identity, has_side_effects=True),
    )(block)


def stencil_kernel(relaxed, *refs):
    if relaxed:
        (values, velocity, mixing, western, eastern, southern, northern, forcing, weight, out) = refs
    else:
        (values, velocity, mixing, western, eastern, southern, northern, out) = refs
    levels, height, width = values.shape[1:]
    row = lax.broadcasted_iota(jnp.int32, (height, width), 0)
    col = lax.broadcasted_iota(jnp.int32, (height, width), 1)
    eye = (
        lax.broadcasted_iota(jnp.int32, (height, height), 0)
        == lax.broadcasted_iota(jnp.int32, (height, height), 1)
    ).astype(jnp.float32)
    first = pl.multiple_of(pl.program_id(0) * levels, levels)
    numbers = (((1,), (1,)), ((), ()))
    exact = lax.Precision.HIGHEST
    south_cols = lax.dot_general(
        eye, southern[pl.ds(first, levels), :], numbers, precision=exact,
        preferred_element_type=jnp.float32,
    )
    north_cols = lax.dot_general(
        eye, northern[pl.ds(first, levels), :], numbers, precision=exact,
        preferred_element_type=jnp.float32,
    )
    for level in range(levels):
        q = values[0, level]
        west = jnp.where(row == 0, western[0, level], pltpu.roll(q, 1, 0))
        east = jnp.where(row == height - 1, eastern[0, level], pltpu.roll(q, height - 1, 0))
        south = jnp.where(col == 0, south_cols[:, level:level + 1], pltpu.roll(q, 1, 1))
        north = jnp.where(
            col == width - 1, north_cols[:, level:level + 1], pltpu.roll(q, width - 1, 1)
        )
        along_rows = velocity[0, level]
        along_columns = velocity[1, level]
        upwind = (
            jnp.maximum(along_rows, 0.0) * (q - west)
            + jnp.minimum(along_rows, 0.0) * (east - q)
            + jnp.maximum(along_columns, 0.0) * (q - south)
            + jnp.minimum(along_columns, 0.0) * (north - q)
        )
        moved = q - upwind + mixing[level] * (east + west + north + south - 4.0 * q)
        if relaxed:
            moved = moved + weight[...] * (forcing[0, level] - moved)
        out[0, level] = moved


def stencil(values, halo, velocity, mixing, forcing=None, weight=None):
    fields, levels, height, width = values.shape
    west_row, east_row, south_col, north_col = halo
    plane = pl.BlockSpec((1, levels, height, width), lambda f: (f, 0, 0, 0))
    edge_row = pl.BlockSpec((1, levels, 1, width), lambda f: (f, 0, 0, 0))
    edge_col = pl.BlockSpec((fields * levels, height), lambda f: (0, 0))
    operands = [values, velocity, mixing, west_row, east_row, south_col, north_col]
    specs = [
        plane,
        pl.BlockSpec(velocity.shape, lambda f: (0, 0, 0, 0)),
        pl.BlockSpec(mixing.shape, lambda f: (0, 0, 0)),
        edge_row,
        edge_row,
        edge_col,
        edge_col,
    ]
    relaxed = forcing is not None
    if relaxed:
        operands += [forcing, weight]
        specs += [plane, pl.BlockSpec(weight.shape, lambda f: (0, 0))]
    return pl.pallas_call(
        lambda *refs: stencil_kernel(relaxed, *refs),
        out_shape=jax.ShapeDtypeStruct(values.shape, values.dtype),
        grid=(fields,),
        in_specs=specs,
        out_specs=plane,
    )(*operands)


def flat(block):
    size = block.size
    return block.reshape(size // 128, 128) if size % 128 == 0 else block.reshape(-1, block.shape[-1])


def per_device(
    parent_fields,
    parent_velocity,
    parent_mixing,
    nest_fields,
    nest_velocity,
    nest_mixing,
    nest_anchor,
):
    row_rank = lax.axis_index("gx")
    column_rank = lax.axis_index("gy")
    row_devices = lax.axis_size("gx")
    column_devices = lax.axis_size("gy")
    parent_rows = parent_fields.shape[2]
    parent_columns = parent_fields.shape[3]
    nest_rows = nest_fields.shape[2]
    nest_columns = nest_fields.shape[3]
    span_rows = nest_rows // 3
    span_columns = nest_columns // 3
    ratio = parent_columns // span_columns
    base = column_devices // 2
    base_column = base * parent_columns
    relay_rows = span_rows + 2
    relay_columns = span_columns + 2
    row_anchor = nest_anchor[0]
    column_anchor = nest_anchor[1]
    offset = column_anchor - 1 - base_column

    parent_next = stencil(
        parent_fields, neighbours(parent_fields, 2), parent_velocity, parent_mixing
    )

    margin = parent_columns - span_columns
    wide = jnp.pad(parent_next, ((0, 0), (0, 0), (0, 0), (margin, margin)))
    straddle = (ratio - 1) * span_columns - 2
    regimes = (
        lambda k, extra: not (extra == 1 and k == ratio - 2),
        lambda k, extra: True,
        lambda k, extra: not (extra == 0 and k == ratio - 1),
    )
    regime = (offset > straddle - span_columns).astype(jnp.int32) + (
        offset > straddle - span_columns + 1
    ).astype(jnp.int32)
    pieces = []
    routes = []
    for extra in (0, 1):
        for k in range(ratio):
            if extra == 1 and k == 0:
                continue
            start = margin + span_columns * k + offset - extra * parent_columns
            piece = lax.dynamic_slice_in_dim(wide, start, relay_columns, axis=3)
            routes.append((k, extra, len(pieces)))
            pieces.append(flat(piece))
    stacked_pieces = jnp.stack(pieces)
    branches = []
    for number, active in enumerate(regimes):
        patterns = [
            (column_pairs(column_devices, base, ratio, k, extra), index, extra)
            for k, extra, index in routes
            if active(k, extra)
        ]
        identity = (0, 6, 7)[number]
        branches.append(
            lambda stacked, patterns=patterns, identity=identity: tuple(
                exchange(stacked, patterns, 2, "gy", identity)
            )
        )
    within_part, beyond_part = lax.switch(regime, branches, stacked_pieces)
    piece_shape = parent_next.shape[:3] + (relay_columns,)
    own_k = column_rank % ratio
    within_live = jnp.logical_not((regime == 2) & (own_k == ratio - 1))
    beyond_live = (own_k != 0) & jnp.logical_not((regime == 0) & (own_k == ratio - 2))
    relay_cols = jnp.where(within_live, within_part.reshape(piece_shape), 0.0) + jnp.where(
        beyond_live, beyond_part.reshape(piece_shape), 0.0
    )

    padded = jnp.pad(relay_cols, ((0, 0), (0, 0), (relay_rows, relay_rows), (0, 0)))
    slots = []
    for target in range(row_devices):
        first = row_anchor - 1 + span_rows * target - parent_rows * row_rank
        first = jnp.clip(first, -relay_rows, parent_rows) + relay_rows
        slots.append(lax.dynamic_slice_in_dim(padded, first, relay_rows, axis=2))
    stacked = jnp.stack(slots, axis=0)
    received = lax.all_to_all(stacked, "gx", split_axis=0, concat_axis=0, tiled=True)
    relay = jnp.sum(received, axis=0)

    forcing = refine(relay)
    row_global = row_rank * nest_rows + jnp.arange(nest_rows, dtype=jnp.int32)
    column_global = column_rank * nest_columns + jnp.arange(nest_columns, dtype=jnp.int32)
    weight = relax_weight(
        row_global, column_global, row_devices * nest_rows, column_devices * nest_columns
    )
    state = nest_fields
    for substep in range(SUBSTEPS):
        state = stencil(
            state, neighbours(state, 3 + substep), nest_velocity, nest_mixing, forcing, weight
        )

    coarse = block_mean(state)
    fields_count, levels_count = coarse.shape[:2]
    collected = gather(coarse.reshape((-1,) + coarse.shape[2:]), "gx", 9)
    gathered = jnp.moveaxis(collected, 0, 1).reshape(
        fields_count, levels_count, row_devices * span_rows, coarse.shape[3]
    )
    total_span = row_devices * span_rows
    gathered = jnp.pad(gathered, ((0, 0), (0, 0), (parent_rows, parent_rows), (0, 0)))
    first = jnp.clip(parent_rows * row_rank - row_anchor, -parent_rows, total_span)
    strip = lax.dynamic_slice_in_dim(gathered, first + parent_rows, parent_rows, axis=2)

    routes = []
    for extra in (1, 0):
        for k in range(ratio):
            if extra == 1 and k == 0:
                continue
            pairs = [(j, p) for (p, j) in column_pairs(column_devices, base, ratio, k, extra)]
            routes.append((k, extra, pairs))
    back_branches = []
    for number, skipped in enumerate(((1, 1), (0, ratio - 1))):
        patterns = [
            (pairs, 0, slot) for slot, (k, extra, pairs) in enumerate(routes)
            if (k, extra) != (skipped[1], skipped[0])
        ]
        identity = (1, 8)[number]
        back_branches.append(
            lambda sent, patterns=patterns, identity=identity: tuple(
                exchange(sent, patterns, len(routes), "gy", identity)
            )
        )
    late = (offset > (ratio - 1) * span_columns - span_columns - 1).astype(jnp.int32)
    parts = lax.switch(late, back_branches, flat(strip)[None])
    joined = jnp.concatenate([part.reshape(strip.shape) for part in parts], axis=3)
    start = (ratio - 1) * span_columns - 1 - offset
    fed_back = lax.dynamic_slice_in_dim(joined, start, parent_columns, axis=3)

    relative_rows = row_rank * parent_rows + jnp.arange(parent_rows, dtype=jnp.int32) - row_anchor
    relative_columns = (
        column_rank * parent_columns + jnp.arange(parent_columns, dtype=jnp.int32) - column_anchor
    )
    rows_valid = within(relative_rows, total_span)
    columns_valid = within(relative_columns, column_devices * span_columns)
    covered = rows_valid[:, None] & columns_valid[None, :]
    parent_result = jnp.where(covered, fed_back, parent_next)
    return (parent_result, state)


def solution(mesh):
    placed = (
        P(None, None, "gx", "gy"),
        P(None, None, "gx", "gy"),
        P(None, "gx", "gy"),
        P(None, None, "gx", "gy"),
        P(None, None, "gx", "gy"),
        P(None, "gx", "gy"),
        P(),
    )
    return jax.shard_map(
        per_device,
        mesh=mesh,
        in_specs=placed,
        out_specs=(P(None, None, "gx", "gy"), P(None, None, "gx", "gy")),
        check_vma=False,
    )
```

```python
import jax
import jax.numpy as jnp
from jax import lax
from jax.experimental import pallas as pl
from jax.experimental.pallas import tpu as pltpu
from jax.sharding import PartitionSpec as P

MESH = pl.DeviceIdType.MESH

SUBSTEPS = 3


third = 1.0 / 3.0
two_thirds = 2.0 / 3.0
nudge_floor = 0.1
relax_width = 4.0


def shift_pairs(count, step):
    return [(i, i + step) for i in range(count) if 0 <= i + step < count]


def halo_kernel(rows, cols, *refs):
    sources, targets, send_sems, recv_sems = refs[:4], refs[4:8], refs[8], refs[9]
    x = lax.axis_index("gx")
    y = lax.axis_index("gy")
    routes = (("gx", x, 1, rows), ("gx", x, -1, rows), ("gy", y, 1, cols), ("gy", y, -1, cols))
    barrier = pltpu.get_barrier_semaphore()
    for axis, own, step, count in routes:
        @pl.when((own + step >= 0) & (own + step < count))
        def _():
            pl.semaphore_signal(barrier, 1, device_id={axis: own + step}, device_id_type=MESH)

    peers = (x + rows - 1) // rows + (2 * rows - 2 - x) // rows
    peers = peers + (y + cols - 1) // cols + (2 * cols - 2 - y) // cols
    pl.semaphore_wait(barrier, peers)
    copies = []
    for number, (axis, own, step, count) in enumerate(routes):
        copy = pltpu.make_async_remote_copy(
            src_ref=sources[number],
            dst_ref=targets[number],
            send_sem=send_sems.at[number],
            recv_sem=recv_sems.at[number],
            device_id={axis: own + step},
            device_id_type=MESH,
        )
        copies.append((own, step, count, copy))

        @pl.when((own + step >= 0) & (own + step < count))
        def _():
            copy.start()

    for number, (own, step, count, copy) in enumerate(copies):
        @pl.when((own + step >= 0) & (own + step < count))
        def _():
            copy.wait_send()

        @pl.when((own - step >= 0) & (own - step < count))
        def _():
            copy.wait_recv()

        @pl.when((own - step < 0) | (own - step >= count))
        def _():
            targets[number][...] = jnp.zeros(targets[number].shape, targets[number].dtype)


def edges(cells):
    fields, levels, height, width = cells.shape
    planes = fields * levels
    return (
        cells[:, :, -1, :].reshape(planes, width),
        cells[:, :, 0, :].reshape(planes, width),
        cells[:, :, :, -1].reshape(planes, height),
        cells[:, :, :, 0].reshape(planes, height),
    )


def neighbours(sources, identity):
    rows = lax.axis_size("gx")
    cols = lax.axis_size("gy")
    received = pl.pallas_call(
        lambda *refs: halo_kernel(rows, cols, *refs),
        out_shape=tuple(jax.ShapeDtypeStruct(part.shape, part.dtype) for part in sources),
        in_specs=[pl.BlockSpec(memory_space=pltpu.VMEM)] * 4,
        out_specs=tuple(pl.BlockSpec(memory_space=pltpu.VMEM) for _ in range(4)),
        scratch_shapes=[pltpu.SemaphoreType.DMA((4,)), pltpu.SemaphoreType.DMA((4,))],
        compiler_params=pltpu.CompilerParams(collective_id=identity, has_side_effects=True),
    )(*sources)
    return received


def update(values, halo, velocity, mixing):
    west_row, east_row, south_col, north_col = halo
    western = jnp.concatenate([west_row, values[:, :, :-1, :]], axis=2)
    eastern = jnp.concatenate([values[:, :, 1:, :], east_row], axis=2)
    southern = jnp.concatenate([south_col, values[:, :, :, :-1]], axis=3)
    northern = jnp.concatenate([values[:, :, :, 1:], north_col], axis=3)
    along_rows = velocity[0]
    along_columns = velocity[1]
    upwind = (
        jnp.maximum(along_rows, 0.0) * (values - western)
        + jnp.minimum(along_rows, 0.0) * (eastern - values)
        + jnp.maximum(along_columns, 0.0) * (values - southern)
        + jnp.minimum(along_columns, 0.0) * (northern - values)
    )
    return values - upwind + mixing * (eastern + western + northern + southern - 4.0 * values)


def refine_rows(block):
    lower = block[:, :, :-2]
    centre = block[:, :, 1:-1]
    upper = block[:, :, 2:]
    stacked = jnp.stack(
        (third * lower + two_thirds * centre, centre, two_thirds * centre + third * upper), axis=3
    )
    extent = centre.shape
    return stacked.reshape(extent[0], extent[1], 3 * extent[2], extent[3])


def refine_columns(block):
    lower = block[:, :, :, :-2]
    centre = block[:, :, :, 1:-1]
    upper = block[:, :, :, 2:]
    stacked = jnp.stack(
        (third * lower + two_thirds * centre, centre, two_thirds * centre + third * upper), axis=4
    )
    extent = centre.shape
    return stacked.reshape(extent[0], extent[1], extent[2], 3 * extent[3])


def refining(count):
    fine = jnp.arange(3 * count, dtype=jnp.int32)[:, None]
    coarse = jnp.arange(count + 2, dtype=jnp.int32)[None, :]
    centre = fine // 3 + 1
    phase = fine % 3
    lower = jnp.where(phase == 0, third, jnp.where(phase == 2, 0.0, 0.0))
    upper = jnp.where(phase == 2, third, 0.0)
    middle = jnp.where(phase == 1, 1.0, two_thirds)
    return (
        jnp.where(coarse == centre, middle, 0.0)
        + jnp.where(coarse == centre - 1, lower, 0.0)
        + jnp.where(coarse == centre + 1, upper, 0.0)
    ).astype(jnp.float32)


def refine(block):
    exact = lax.Precision.HIGHEST
    rows = block.shape[2] - 2
    cols = block.shape[3] - 2
    down = jnp.einsum("ar,flrc->flac", refining(rows), block, precision=exact)
    return jnp.einsum("flac,bc->flab", down, refining(cols), precision=exact)


def grouping(count):
    rows = jnp.arange(count, dtype=jnp.int32)[:, None] // 3
    return (rows == jnp.arange(count // 3, dtype=jnp.int32)[None, :]).astype(jnp.float32)


def block_mean(state):
    extent = state.shape
    exact = lax.Precision.HIGHEST
    across = jnp.einsum("flrc,cb->flrb", state, grouping(extent[3]), precision=exact)
    down = jnp.einsum("ra,flrb->flab", grouping(extent[2]), across, precision=exact)
    return down / 9.0


def relax_weight(row_global, column_global, total_rows, total_columns):
    row_distance = jnp.minimum(row_global, total_rows - 1 - row_global)
    column_distance = jnp.minimum(column_global, total_columns - 1 - column_global)
    distance = jnp.minimum(row_distance[:, None], column_distance[None, :]).astype(jnp.float32)
    return nudge_floor + (1.0 - nudge_floor) * jnp.exp(-distance / relax_width)


def within(positions, limit):
    return (positions >= 0) & (positions < limit)


def column_pairs(count, base, ratio, k, extra):
    pairs = []
    for m in range(count):
        j = ratio * m + k
        p = base + m + extra
        if j < count and p < count:
            pairs.append((p, j))
    return pairs


def exchange_kernel(axis, patterns, send_ref, recv_ref, send_sems, recv_sems):
    me = lax.axis_index(axis)
    barrier = pltpu.get_barrier_semaphore()
    links = [pair for pairs, _, _ in patterns for pair in pairs]
    for a, b in links:
        @pl.when(me == a)
        def _():
            pl.semaphore_signal(barrier, 1, device_id={axis: b}, device_id_type=MESH)

        @pl.when(me == b)
        def _():
            pl.semaphore_signal(barrier, 1, device_id={axis: a}, device_id_type=MESH)

    peers = {}
    for a, b in links:
        peers[a] = peers.get(a, 0) + 1
        peers[b] = peers.get(b, 0) + 1
    for device, count in sorted(peers.items()):
        @pl.when(me == device)
        def _():
            pl.semaphore_wait(barrier, count)

    copies = []
    for number, (pairs, source, slot) in enumerate(patterns):
        for a, b in pairs:
            copy = pltpu.make_async_remote_copy(
                src_ref=send_ref.at[source],
                dst_ref=recv_ref.at[slot],
                send_sem=send_sems.at[number],
                recv_sem=recv_sems.at[slot],
                device_id={axis: b},
                device_id_type=MESH,
            )
            copies.append((a, b, copy))

            @pl.when(me == a)
            def _():
                copy.start()

    for a, b, copy in copies:
        @pl.when(me == a)
        def _():
            copy.wait_send()

        @pl.when(me == b)
        def _():
            copy.wait_recv()


def exchange(pieces, patterns, slots, axis, identity):
    me = lax.axis_index(axis)
    remote = [([(a, b) for a, b in pairs if a != b], source, slot) for pairs, source, slot in patterns]
    remote = [entry for entry in remote if entry[0]]
    shape = pieces.shape[1:]
    received = pl.pallas_call(
        lambda *refs: exchange_kernel(axis, remote, *refs),
        out_shape=jax.ShapeDtypeStruct((slots,) + shape, pieces.dtype),
        in_specs=[pl.BlockSpec(memory_space=pl.ANY)],
        out_specs=pl.BlockSpec(memory_space=pl.ANY),
        scratch_shapes=[
            pltpu.SemaphoreType.DMA((len(remote),)),
            pltpu.SemaphoreType.DMA((slots,)),
        ],
        compiler_params=pltpu.CompilerParams(collective_id=identity, has_side_effects=True),
    )(pieces)
    parts = [received[slot] for slot in range(slots)]
    for pairs, source, slot in patterns:
        for a, b in pairs:
            if a == b:
                parts[slot] = jnp.where(me == a, pieces[source], parts[slot])
    return parts


def gather_kernel(axis, count, source, target, send_sems, recv_sems):
    me = lax.axis_index(axis)
    barrier = pltpu.get_barrier_semaphore()
    for delta in range(1, count):
        pl.semaphore_signal(
            barrier, 1, device_id={axis: (me + delta) % count}, device_id_type=MESH
        )
    pl.semaphore_wait(barrier, count - 1)
    outgoing = []
    for delta in range(1, count):
        copy = pltpu.make_async_remote_copy(
            src_ref=source,
            dst_ref=target.at[me],
            send_sem=send_sems.at[delta - 1],
            recv_sem=recv_sems.at[delta - 1],
            device_id={axis: (me + delta) % count},
            device_id_type=MESH,
        )
        copy.start()
        outgoing.append(copy)
    target[me] = source[...]
    for delta, copy in zip(range(1, count), outgoing):
        copy.wait_send()
        incoming = pltpu.make_async_remote_copy(
            src_ref=source,
            dst_ref=target.at[(me + count - delta) % count],
            send_sem=send_sems.at[delta - 1],
            recv_sem=recv_sems.at[delta - 1],
            device_id={axis: (me + count - delta) % count},
            device_id_type=MESH,
        )
        incoming.wait_recv()


def gather(block, axis, identity):
    count = lax.axis_size(axis)
    return pl.pallas_call(
        lambda *refs: gather_kernel(axis, count, *refs),
        out_shape=jax.ShapeDtypeStruct((count,) + block.shape, block.dtype),
        in_specs=[pl.BlockSpec(memory_space=pltpu.VMEM)],
        out_specs=pl.BlockSpec(memory_space=pltpu.VMEM),
        scratch_shapes=[
            pltpu.SemaphoreType.DMA((count - 1,)),
            pltpu.SemaphoreType.DMA((count - 1,)),
        ],
        compiler_params=pltpu.CompilerParams(collective_id=identity, has_side_effects=True),
    )(block)


def stencil_kernel(relaxed, *refs):
    if relaxed:
        (values, velocity, mixing, western, eastern, southern, northern, forcing, weight) = refs[:9]
        out, last_row, first_row, last_col, first_col = refs[9:]
    else:
        (values, velocity, mixing, western, eastern, southern, northern, out) = refs
    levels, height, width = values.shape[1:]
    row = lax.broadcasted_iota(jnp.int32, (height, width), 0)
    col = lax.broadcasted_iota(jnp.int32, (height, width), 1)
    eye = (
        lax.broadcasted_iota(jnp.int32, (height, height), 0)
        == lax.broadcasted_iota(jnp.int32, (height, height), 1)
    ).astype(jnp.float32)
    first = pl.multiple_of(pl.program_id(0) * levels, levels)
    numbers = (((1,), (1,)), ((), ()))
    exact = lax.Precision.HIGHEST
    south_cols = lax.dot_general(
        eye, southern[pl.ds(first, levels), :], numbers, precision=exact,
        preferred_element_type=jnp.float32,
    )
    north_cols = lax.dot_general(
        eye, northern[pl.ds(first, levels), :], numbers, precision=exact,
        preferred_element_type=jnp.float32,
    )
    picks = lax.broadcasted_iota(jnp.int32, (8, width), 1)
    chosen = lax.broadcasted_iota(jnp.int32, (8, width), 0)
    ends = ((chosen == 0) & (picks == 0)) | ((chosen == 1) & (picks == width - 1))
    ends = ends.astype(jnp.float32)
    for level in range(levels):
        q = values[0, level]
        west_row = western[pl.ds(first + level, 1), :]
        east_row = eastern[pl.ds(first + level, 1), :]
        west = jnp.where(row == 0, west_row, pltpu.roll(q, 1, 0))
        east = jnp.where(row == height - 1, east_row, pltpu.roll(q, height - 1, 0))
        south = jnp.where(col == 0, south_cols[:, level:level + 1], pltpu.roll(q, 1, 1))
        north = jnp.where(
            col == width - 1, north_cols[:, level:level + 1], pltpu.roll(q, width - 1, 1)
        )
        along_rows = velocity[0, level]
        along_columns = velocity[1, level]
        upwind = (
            jnp.maximum(along_rows, 0.0) * (q - west)
            + jnp.minimum(along_rows, 0.0) * (east - q)
            + jnp.maximum(along_columns, 0.0) * (q - south)
            + jnp.minimum(along_columns, 0.0) * (north - q)
        )
        moved = q - upwind + mixing[level] * (east + west + north + south - 4.0 * q)
        if relaxed:
            moved = moved + weight[...] * (forcing[0, level] - moved)
            last_row[pl.ds(first + level, 1), :] = moved[height - 1:height, :]
            first_row[pl.ds(first + level, 1), :] = moved[0:1, :]
            sides = lax.dot_general(
                ends, moved, numbers, precision=exact, preferred_element_type=jnp.float32
            )
            first_col[pl.ds(first + level, 1), :] = sides[0:1, :]
            last_col[pl.ds(first + level, 1), :] = sides[1:2, :]
        out[0, level] = moved


def stencil(values, halo, velocity, mixing, forcing=None, weight=None):
    fields, levels, height, width = values.shape
    west_row, east_row, south_col, north_col = halo
    plane = pl.BlockSpec((1, levels, height, width), lambda f: (f, 0, 0, 0))
    edge_row = pl.BlockSpec((fields * levels, width), lambda f: (0, 0))
    edge_col = pl.BlockSpec((fields * levels, height), lambda f: (0, 0))
    operands = [values, velocity, mixing, west_row, east_row, south_col, north_col]
    specs = [
        plane,
        pl.BlockSpec(velocity.shape, lambda f: (0, 0, 0, 0)),
        pl.BlockSpec(mixing.shape, lambda f: (0, 0, 0)),
        edge_row,
        edge_row,
        edge_col,
        edge_col,
    ]
    relaxed = forcing is not None
    out_shape = jax.ShapeDtypeStruct(values.shape, values.dtype)
    out_specs = plane
    if relaxed:
        operands += [forcing, weight]
        specs += [plane, pl.BlockSpec(weight.shape, lambda f: (0, 0))]
        rows_shape = jax.ShapeDtypeStruct((fields * levels, width), values.dtype)
        cols_shape = jax.ShapeDtypeStruct((fields * levels, height), values.dtype)
        out_shape = (out_shape, rows_shape, rows_shape, cols_shape, cols_shape)
        out_specs = (plane, edge_row, edge_row, edge_col, edge_col)
    return pl.pallas_call(
        lambda *refs: stencil_kernel(relaxed, *refs),
        out_shape=out_shape,
        grid=(fields,),
        in_specs=specs,
        out_specs=out_specs,
    )(*operands)


def flat(block):
    size = block.size
    return block.reshape(size // 128, 128) if size % 128 == 0 else block.reshape(-1, block.shape[-1])


def per_device(
    parent_fields,
    parent_velocity,
    parent_mixing,
    nest_fields,
    nest_velocity,
    nest_mixing,
    nest_anchor,
):
    row_rank = lax.axis_index("gx")
    column_rank = lax.axis_index("gy")
    row_devices = lax.axis_size("gx")
    column_devices = lax.axis_size("gy")
    parent_rows = parent_fields.shape[2]
    parent_columns = parent_fields.shape[3]
    nest_rows = nest_fields.shape[2]
    nest_columns = nest_fields.shape[3]
    span_rows = nest_rows // 3
    span_columns = nest_columns // 3
    ratio = parent_columns // span_columns
    base = column_devices // 2
    base_column = base * parent_columns
    relay_rows = span_rows + 2
    relay_columns = span_columns + 2
    row_anchor = nest_anchor[0]
    column_anchor = nest_anchor[1]
    offset = column_anchor - 1 - base_column

    parent_next = stencil(
        parent_fields, neighbours(edges(parent_fields), 2), parent_velocity, parent_mixing
    )

    margin = parent_columns - span_columns
    wide = jnp.pad(parent_next, ((0, 0), (0, 0), (0, 0), (margin, margin)))
    straddle = (ratio - 1) * span_columns - 2
    regimes = (
        lambda k, extra: not (extra == 1 and k == ratio - 2),
        lambda k, extra: True,
        lambda k, extra: not (extra == 0 and k == ratio - 1),
    )
    regime = (offset > straddle - span_columns).astype(jnp.int32) + (
        offset > straddle - span_columns + 1
    ).astype(jnp.int32)
    pieces = []
    routes = []
    for extra in (0, 1):
        for k in range(ratio):
            if extra == 1 and k == 0:
                continue
            start = margin + span_columns * k + offset - extra * parent_columns
            piece = lax.dynamic_slice_in_dim(wide, start, relay_columns, axis=3)
            routes.append((k, extra, len(pieces)))
            pieces.append(flat(piece))
    stacked_pieces = jnp.stack(pieces)
    branches = []
    for number, active in enumerate(regimes):
        patterns = [
            (column_pairs(column_devices, base, ratio, k, extra), index, extra)
            for k, extra, index in routes
            if active(k, extra)
        ]
        identity = (0, 6, 7)[number]
        branches.append(
            lambda stacked, patterns=patterns, identity=identity: tuple(
                exchange(stacked, patterns, 2, "gy", identity)
            )
        )
    within_part, beyond_part = lax.switch(regime, branches, stacked_pieces)
    piece_shape = parent_next.shape[:3] + (relay_columns,)
    own_k = column_rank % ratio
    within_live = jnp.logical_not((regime == 2) & (own_k == ratio - 1))
    beyond_live = (own_k != 0) & jnp.logical_not((regime == 0) & (own_k == ratio - 2))
    relay_cols = jnp.where(within_live, within_part.reshape(piece_shape), 0.0) + jnp.where(
        beyond_live, beyond_part.reshape(piece_shape), 0.0
    )

    padded = jnp.pad(relay_cols, ((0, 0), (0, 0), (relay_rows, relay_rows), (0, 0)))
    slots = []
    for target in range(row_devices):
        first = row_anchor - 1 + span_rows * target - parent_rows * row_rank
        first = jnp.clip(first, -relay_rows, parent_rows) + relay_rows
        slots.append(lax.dynamic_slice_in_dim(padded, first, relay_rows, axis=2))
    stacked = jnp.stack(slots, axis=0)
    received = lax.all_to_all(stacked, "gx", split_axis=0, concat_axis=0, tiled=True)
    relay = jnp.sum(received, axis=0)

    forcing = refine(relay)
    row_global = row_rank * nest_rows + jnp.arange(nest_rows, dtype=jnp.int32)
    column_global = column_rank * nest_columns + jnp.arange(nest_columns, dtype=jnp.int32)
    weight = relax_weight(
        row_global, column_global, row_devices * nest_rows, column_devices * nest_columns
    )
    state = nest_fields
    sides = edges(state)
    for substep in range(SUBSTEPS):
        state, *sides = stencil(
            state, neighbours(sides, 3 + substep), nest_velocity, nest_mixing, forcing, weight
        )

    coarse = block_mean(state)
    fields_count, levels_count = coarse.shape[:2]
    collected = gather(coarse.reshape((-1,) + coarse.shape[2:]), "gx", 9)
    gathered = jnp.moveaxis(collected, 0, 1).reshape(
        fields_count, levels_count, row_devices * span_rows, coarse.shape[3]
    )
    total_span = row_devices * span_rows
    gathered = jnp.pad(gathered, ((0, 0), (0, 0), (parent_rows, parent_rows), (0, 0)))
    first = jnp.clip(parent_rows * row_rank - row_anchor, -parent_rows, total_span)
    strip = lax.dynamic_slice_in_dim(gathered, first + parent_rows, parent_rows, axis=2)

    routes = []
    for extra in (1, 0):
        for k in range(ratio):
            if extra == 1 and k == 0:
                continue
            pairs = [(j, p) for (p, j) in column_pairs(column_devices, base, ratio, k, extra)]
            routes.append((k, extra, pairs))
    back_branches = []
    for number, skipped in enumerate(((1, 1), (0, ratio - 1))):
        patterns = [
            (pairs, 0, slot) for slot, (k, extra, pairs) in enumerate(routes)
            if (k, extra) != (skipped[1], skipped[0])
        ]
        identity = (1, 8)[number]
        back_branches.append(
            lambda sent, patterns=patterns, identity=identity: tuple(
                exchange(sent, patterns, len(routes), "gy", identity)
            )
        )
    late = (offset > (ratio - 1) * span_columns - span_columns - 1).astype(jnp.int32)
    parts = lax.switch(late, back_branches, flat(strip)[None])
    joined = jnp.concatenate([part.reshape(strip.shape) for part in parts], axis=3)
    start = (ratio - 1) * span_columns - 1 - offset
    fed_back = lax.dynamic_slice_in_dim(joined, start, parent_columns, axis=3)

    relative_rows = row_rank * parent_rows + jnp.arange(parent_rows, dtype=jnp.int32) - row_anchor
    relative_columns = (
        column_rank * parent_columns + jnp.arange(parent_columns, dtype=jnp.int32) - column_anchor
    )
    rows_valid = within(relative_rows, total_span)
    columns_valid = within(relative_columns, column_devices * span_columns)
    covered = rows_valid[:, None] & columns_valid[None, :]
    parent_result = jnp.where(covered, fed_back, parent_next)
    return (parent_result, state)


def solution(mesh):
    placed = (
        P(None, None, "gx", "gy"),
        P(None, None, "gx", "gy"),
        P(None, "gx", "gy"),
        P(None, None, "gx", "gy"),
        P(None, None, "gx", "gy"),
        P(None, "gx", "gy"),
        P(),
    )
    return jax.shard_map(
        per_device,
        mesh=mesh,
        in_specs=placed,
        out_specs=(P(None, None, "gx", "gy"), P(None, None, "gx", "gy")),
        check_vma=False,
    )
```

```python
import jax
import jax.numpy as jnp
from jax import lax
from jax.experimental import pallas as pl
from jax.experimental.pallas import tpu as pltpu
from jax.sharding import PartitionSpec as P

MESH = pl.DeviceIdType.MESH

SUBSTEPS = 3


third = 1.0 / 3.0
two_thirds = 2.0 / 3.0
nudge_floor = 0.1
relax_width = 4.0


def shift_pairs(count, step):
    return [(i, i + step) for i in range(count) if 0 <= i + step < count]


def halo_kernel(rows, cols, *refs):
    sources, targets, send_sems, recv_sems = refs[:4], refs[4:8], refs[8], refs[9]
    x = lax.axis_index("gx")
    y = lax.axis_index("gy")
    routes = (("gx", x, 1, rows), ("gx", x, -1, rows), ("gy", y, 1, cols), ("gy", y, -1, cols))
    barrier = pltpu.get_barrier_semaphore()
    for axis, own, step, count in routes:
        @pl.when((own + step >= 0) & (own + step < count))
        def _():
            pl.semaphore_signal(barrier, 1, device_id={axis: own + step}, device_id_type=MESH)

    peers = (x + rows - 1) // rows + (2 * rows - 2 - x) // rows
    peers = peers + (y + cols - 1) // cols + (2 * cols - 2 - y) // cols
    pl.semaphore_wait(barrier, peers)
    copies = []
    for number, (axis, own, step, count) in enumerate(routes):
        copy = pltpu.make_async_remote_copy(
            src_ref=sources[number],
            dst_ref=targets[number],
            send_sem=send_sems.at[number],
            recv_sem=recv_sems.at[number],
            device_id={axis: own + step},
            device_id_type=MESH,
        )
        copies.append((own, step, count, copy))

        @pl.when((own + step >= 0) & (own + step < count))
        def _():
            copy.start()

    for number, (own, step, count, copy) in enumerate(copies):
        @pl.when((own + step >= 0) & (own + step < count))
        def _():
            copy.wait_send()

        @pl.when((own - step >= 0) & (own - step < count))
        def _():
            copy.wait_recv()

        @pl.when((own - step < 0) | (own - step >= count))
        def _():
            targets[number][...] = jnp.zeros(targets[number].shape, targets[number].dtype)


def edges(cells):
    fields, levels, height, width = cells.shape
    planes = fields * levels
    return (
        cells[:, :, -1, :].reshape(planes, width),
        cells[:, :, 0, :].reshape(planes, width),
        cells[:, :, :, -1].reshape(planes, height),
        cells[:, :, :, 0].reshape(planes, height),
    )


def neighbours(sources, identity):
    rows = lax.axis_size("gx")
    cols = lax.axis_size("gy")
    received = pl.pallas_call(
        lambda *refs: halo_kernel(rows, cols, *refs),
        out_shape=tuple(jax.ShapeDtypeStruct(part.shape, part.dtype) for part in sources),
        in_specs=[pl.BlockSpec(memory_space=pltpu.VMEM)] * 4,
        out_specs=tuple(pl.BlockSpec(memory_space=pltpu.VMEM) for _ in range(4)),
        scratch_shapes=[pltpu.SemaphoreType.DMA((4,)), pltpu.SemaphoreType.DMA((4,))],
        compiler_params=pltpu.CompilerParams(collective_id=identity, has_side_effects=True),
    )(*sources)
    return received


def update(values, halo, velocity, mixing):
    west_row, east_row, south_col, north_col = halo
    western = jnp.concatenate([west_row, values[:, :, :-1, :]], axis=2)
    eastern = jnp.concatenate([values[:, :, 1:, :], east_row], axis=2)
    southern = jnp.concatenate([south_col, values[:, :, :, :-1]], axis=3)
    northern = jnp.concatenate([values[:, :, :, 1:], north_col], axis=3)
    along_rows = velocity[0]
    along_columns = velocity[1]
    upwind = (
        jnp.maximum(along_rows, 0.0) * (values - western)
        + jnp.minimum(along_rows, 0.0) * (eastern - values)
        + jnp.maximum(along_columns, 0.0) * (values - southern)
        + jnp.minimum(along_columns, 0.0) * (northern - values)
    )
    return values - upwind + mixing * (eastern + western + northern + southern - 4.0 * values)


def refine_rows(block):
    lower = block[:, :, :-2]
    centre = block[:, :, 1:-1]
    upper = block[:, :, 2:]
    stacked = jnp.stack(
        (third * lower + two_thirds * centre, centre, two_thirds * centre + third * upper), axis=3
    )
    extent = centre.shape
    return stacked.reshape(extent[0], extent[1], 3 * extent[2], extent[3])


def refine_columns(block):
    lower = block[:, :, :, :-2]
    centre = block[:, :, :, 1:-1]
    upper = block[:, :, :, 2:]
    stacked = jnp.stack(
        (third * lower + two_thirds * centre, centre, two_thirds * centre + third * upper), axis=4
    )
    extent = centre.shape
    return stacked.reshape(extent[0], extent[1], extent[2], 3 * extent[3])


def refining(count):
    fine = jnp.arange(3 * count, dtype=jnp.int32)[:, None]
    coarse = jnp.arange(count + 2, dtype=jnp.int32)[None, :]
    centre = fine // 3 + 1
    phase = fine % 3
    lower = jnp.where(phase == 0, third, jnp.where(phase == 2, 0.0, 0.0))
    upper = jnp.where(phase == 2, third, 0.0)
    middle = jnp.where(phase == 1, 1.0, two_thirds)
    return (
        jnp.where(coarse == centre, middle, 0.0)
        + jnp.where(coarse == centre - 1, lower, 0.0)
        + jnp.where(coarse == centre + 1, upper, 0.0)
    ).astype(jnp.float32)


def refine(block):
    exact = lax.Precision.HIGHEST
    rows = block.shape[2] - 2
    cols = block.shape[3] - 2
    down = jnp.einsum("ar,flrc->flac", refining(rows), block, precision=exact)
    return jnp.einsum("flac,bc->flab", down, refining(cols), precision=exact)


def grouping(count):
    rows = jnp.arange(count, dtype=jnp.int32)[:, None] // 3
    return (rows == jnp.arange(count // 3, dtype=jnp.int32)[None, :]).astype(jnp.float32)


def block_mean(state):
    extent = state.shape
    exact = lax.Precision.HIGHEST
    across = jnp.einsum("flrc,cb->flrb", state, grouping(extent[3]), precision=exact)
    down = jnp.einsum("ra,flrb->flab", grouping(extent[2]), across, precision=exact)
    return down / 9.0


def relax_weight(row_global, column_global, total_rows, total_columns):
    row_distance = jnp.minimum(row_global, total_rows - 1 - row_global)
    column_distance = jnp.minimum(column_global, total_columns - 1 - column_global)
    distance = jnp.minimum(row_distance[:, None], column_distance[None, :]).astype(jnp.float32)
    return nudge_floor + (1.0 - nudge_floor) * jnp.exp(-distance / relax_width)


def within(positions, limit):
    return (positions >= 0) & (positions < limit)


def column_pairs(count, base, ratio, k, extra):
    pairs = []
    for m in range(count):
        j = ratio * m + k
        p = base + m + extra
        if j < count and p < count:
            pairs.append((p, j))
    return pairs


def exchange_kernel(axis, patterns, send_ref, recv_ref, send_sems, recv_sems):
    me = lax.axis_index(axis)
    barrier = pltpu.get_barrier_semaphore()
    links = [pair for pairs, _, _ in patterns for pair in pairs]
    for a, b in links:
        @pl.when(me == a)
        def _():
            pl.semaphore_signal(barrier, 1, device_id={axis: b}, device_id_type=MESH)

        @pl.when(me == b)
        def _():
            pl.semaphore_signal(barrier, 1, device_id={axis: a}, device_id_type=MESH)

    peers = {}
    for a, b in links:
        peers[a] = peers.get(a, 0) + 1
        peers[b] = peers.get(b, 0) + 1
    for device, count in sorted(peers.items()):
        @pl.when(me == device)
        def _():
            pl.semaphore_wait(barrier, count)

    copies = []
    for number, (pairs, source, slot) in enumerate(patterns):
        for a, b in pairs:
            copy = pltpu.make_async_remote_copy(
                src_ref=send_ref.at[source],
                dst_ref=recv_ref.at[slot],
                send_sem=send_sems.at[number],
                recv_sem=recv_sems.at[slot],
                device_id={axis: b},
                device_id_type=MESH,
            )
            copies.append((a, b, copy))

            @pl.when(me == a)
            def _():
                copy.start()

    for a, b, copy in copies:
        @pl.when(me == a)
        def _():
            copy.wait_send()

        @pl.when(me == b)
        def _():
            copy.wait_recv()


def exchange(pieces, patterns, slots, axis, identity):
    me = lax.axis_index(axis)
    remote = [([(a, b) for a, b in pairs if a != b], source, slot) for pairs, source, slot in patterns]
    remote = [entry for entry in remote if entry[0]]
    shape = pieces.shape[1:]
    received = pl.pallas_call(
        lambda *refs: exchange_kernel(axis, remote, *refs),
        out_shape=jax.ShapeDtypeStruct((slots,) + shape, pieces.dtype),
        in_specs=[pl.BlockSpec(memory_space=pl.ANY)],
        out_specs=pl.BlockSpec(memory_space=pl.ANY),
        scratch_shapes=[
            pltpu.SemaphoreType.DMA((len(remote),)),
            pltpu.SemaphoreType.DMA((slots,)),
        ],
        compiler_params=pltpu.CompilerParams(collective_id=identity, has_side_effects=True),
    )(pieces)
    parts = [received[slot] for slot in range(slots)]
    for pairs, source, slot in patterns:
        for a, b in pairs:
            if a == b:
                parts[slot] = jnp.where(me == a, pieces[source], parts[slot])
    return parts


def gather_kernel(axis, count, spread, source, target, send_sems, recv_sems):
    me = lax.axis_index(axis)
    barrier = pltpu.get_barrier_semaphore()
    for delta in range(1, count):
        pl.semaphore_signal(
            barrier, 1, device_id={axis: (me + delta) % count}, device_id_type=MESH
        )
    pl.semaphore_wait(barrier, count - 1)
    outgoing = []
    for delta in range(1, count):
        copy = pltpu.make_async_remote_copy(
            src_ref=source.at[(me + delta) % count] if spread else source,
            dst_ref=target.at[me],
            send_sem=send_sems.at[delta - 1],
            recv_sem=recv_sems.at[delta - 1],
            device_id={axis: (me + delta) % count},
            device_id_type=MESH,
        )
        copy.start()
        outgoing.append(copy)
    target[me] = source[me] if spread else source[...]
    for delta, copy in zip(range(1, count), outgoing):
        copy.wait_send()
        incoming = pltpu.make_async_remote_copy(
            src_ref=source.at[0] if spread else source,
            dst_ref=target.at[(me + count - delta) % count],
            send_sem=send_sems.at[delta - 1],
            recv_sem=recv_sems.at[delta - 1],
            device_id={axis: (me + count - delta) % count},
            device_id_type=MESH,
        )
        incoming.wait_recv()


def gather(block, axis, identity, spread=False):
    count = lax.axis_size(axis)
    shape = block.shape[1:] if spread else block.shape
    return pl.pallas_call(
        lambda *refs: gather_kernel(axis, count, spread, *refs),
        out_shape=jax.ShapeDtypeStruct((count,) + shape, block.dtype),
        in_specs=[pl.BlockSpec(memory_space=pltpu.VMEM)],
        out_specs=pl.BlockSpec(memory_space=pltpu.VMEM),
        scratch_shapes=[
            pltpu.SemaphoreType.DMA((count - 1,)),
            pltpu.SemaphoreType.DMA((count - 1,)),
        ],
        compiler_params=pltpu.CompilerParams(collective_id=identity, has_side_effects=True),
    )(block)


def stencil_kernel(relaxed, *refs):
    if relaxed:
        (values, velocity, mixing, western, eastern, southern, northern, forcing, weight) = refs[:9]
        out, last_row, first_row, last_col, first_col = refs[9:]
    else:
        (values, velocity, mixing, western, eastern, southern, northern, out) = refs
    levels, height, width = values.shape[1:]
    row = lax.broadcasted_iota(jnp.int32, (height, width), 0)
    col = lax.broadcasted_iota(jnp.int32, (height, width), 1)
    eye = (
        lax.broadcasted_iota(jnp.int32, (height, height), 0)
        == lax.broadcasted_iota(jnp.int32, (height, height), 1)
    ).astype(jnp.float32)
    first = pl.multiple_of(pl.program_id(0) * levels, levels)
    numbers = (((1,), (1,)), ((), ()))
    exact = lax.Precision.HIGHEST
    south_cols = lax.dot_general(
        eye, southern[pl.ds(first, levels), :], numbers, precision=exact,
        preferred_element_type=jnp.float32,
    )
    north_cols = lax.dot_general(
        eye, northern[pl.ds(first, levels), :], numbers, precision=exact,
        preferred_element_type=jnp.float32,
    )
    picks = lax.broadcasted_iota(jnp.int32, (8, width), 1)
    chosen = lax.broadcasted_iota(jnp.int32, (8, width), 0)
    ends = ((chosen == 0) & (picks == 0)) | ((chosen == 1) & (picks == width - 1))
    ends = ends.astype(jnp.float32)
    for level in range(levels):
        q = values[0, level]
        west_row = western[pl.ds(first + level, 1), :]
        east_row = eastern[pl.ds(first + level, 1), :]
        west = jnp.where(row == 0, west_row, pltpu.roll(q, 1, 0))
        east = jnp.where(row == height - 1, east_row, pltpu.roll(q, height - 1, 0))
        south = jnp.where(col == 0, south_cols[:, level:level + 1], pltpu.roll(q, 1, 1))
        north = jnp.where(
            col == width - 1, north_cols[:, level:level + 1], pltpu.roll(q, width - 1, 1)
        )
        along_rows = velocity[0, level]
        along_columns = velocity[1, level]
        upwind = (
            jnp.maximum(along_rows, 0.0) * (q - west)
            + jnp.minimum(along_rows, 0.0) * (east - q)
            + jnp.maximum(along_columns, 0.0) * (q - south)
            + jnp.minimum(along_columns, 0.0) * (north - q)
        )
        moved = q - upwind + mixing[level] * (east + west + north + south - 4.0 * q)
        if relaxed:
            moved = moved + weight[...] * (forcing[0, level] - moved)
            last_row[pl.ds(first + level, 1), :] = moved[height - 1:height, :]
            first_row[pl.ds(first + level, 1), :] = moved[0:1, :]
            sides = lax.dot_general(
                ends, moved, numbers, precision=exact, preferred_element_type=jnp.float32
            )
            first_col[pl.ds(first + level, 1), :] = sides[0:1, :]
            last_col[pl.ds(first + level, 1), :] = sides[1:2, :]
        out[0, level] = moved


def stencil(values, halo, velocity, mixing, forcing=None, weight=None):
    fields, levels, height, width = values.shape
    west_row, east_row, south_col, north_col = halo
    plane = pl.BlockSpec((1, levels, height, width), lambda f: (f, 0, 0, 0))
    edge_row = pl.BlockSpec((fields * levels, width), lambda f: (0, 0))
    edge_col = pl.BlockSpec((fields * levels, height), lambda f: (0, 0))
    operands = [values, velocity, mixing, west_row, east_row, south_col, north_col]
    specs = [
        plane,
        pl.BlockSpec(velocity.shape, lambda f: (0, 0, 0, 0)),
        pl.BlockSpec(mixing.shape, lambda f: (0, 0, 0)),
        edge_row,
        edge_row,
        edge_col,
        edge_col,
    ]
    relaxed = forcing is not None
    out_shape = jax.ShapeDtypeStruct(values.shape, values.dtype)
    out_specs = plane
    if relaxed:
        operands += [forcing, weight]
        specs += [plane, pl.BlockSpec(weight.shape, lambda f: (0, 0))]
        rows_shape = jax.ShapeDtypeStruct((fields * levels, width), values.dtype)
        cols_shape = jax.ShapeDtypeStruct((fields * levels, height), values.dtype)
        out_shape = (out_shape, rows_shape, rows_shape, cols_shape, cols_shape)
        out_specs = (plane, edge_row, edge_row, edge_col, edge_col)
    return pl.pallas_call(
        lambda *refs: stencil_kernel(relaxed, *refs),
        out_shape=out_shape,
        grid=(fields,),
        in_specs=specs,
        out_specs=out_specs,
    )(*operands)


def flat(block):
    size = block.size
    return block.reshape(size // 128, 128) if size % 128 == 0 else block.reshape(-1, block.shape[-1])


def per_device(
    parent_fields,
    parent_velocity,
    parent_mixing,
    nest_fields,
    nest_velocity,
    nest_mixing,
    nest_anchor,
):
    row_rank = lax.axis_index("gx")
    column_rank = lax.axis_index("gy")
    row_devices = lax.axis_size("gx")
    column_devices = lax.axis_size("gy")
    parent_rows = parent_fields.shape[2]
    parent_columns = parent_fields.shape[3]
    nest_rows = nest_fields.shape[2]
    nest_columns = nest_fields.shape[3]
    span_rows = nest_rows // 3
    span_columns = nest_columns // 3
    ratio = parent_columns // span_columns
    base = column_devices // 2
    base_column = base * parent_columns
    relay_rows = span_rows + 2
    relay_columns = span_columns + 2
    row_anchor = nest_anchor[0]
    column_anchor = nest_anchor[1]
    offset = column_anchor - 1 - base_column

    parent_next = stencil(
        parent_fields, neighbours(edges(parent_fields), 2), parent_velocity, parent_mixing
    )

    margin = parent_columns - span_columns
    wide = jnp.pad(parent_next, ((0, 0), (0, 0), (0, 0), (margin, margin)))
    straddle = (ratio - 1) * span_columns - 2
    regimes = (
        lambda k, extra: not (extra == 1 and k == ratio - 2),
        lambda k, extra: True,
        lambda k, extra: not (extra == 0 and k == ratio - 1),
    )
    regime = (offset > straddle - span_columns).astype(jnp.int32) + (
        offset > straddle - span_columns + 1
    ).astype(jnp.int32)
    pieces = []
    routes = []
    for extra in (0, 1):
        for k in range(ratio):
            if extra == 1 and k == 0:
                continue
            start = margin + span_columns * k + offset - extra * parent_columns
            piece = lax.dynamic_slice_in_dim(wide, start, relay_columns, axis=3)
            routes.append((k, extra, len(pieces)))
            pieces.append(flat(piece))
    stacked_pieces = jnp.stack(pieces)
    branches = []
    for number, active in enumerate(regimes):
        patterns = [
            (column_pairs(column_devices, base, ratio, k, extra), index, extra)
            for k, extra, index in routes
            if active(k, extra)
        ]
        identity = (0, 6, 7)[number]
        branches.append(
            lambda stacked, patterns=patterns, identity=identity: tuple(
                exchange(stacked, patterns, 2, "gy", identity)
            )
        )
    within_part, beyond_part = lax.switch(regime, branches, stacked_pieces)
    piece_shape = parent_next.shape[:3] + (relay_columns,)
    own_k = column_rank % ratio
    within_live = jnp.logical_not((regime == 2) & (own_k == ratio - 1))
    beyond_live = (own_k != 0) & jnp.logical_not((regime == 0) & (own_k == ratio - 2))
    relay_cols = jnp.where(within_live, within_part.reshape(piece_shape), 0.0) + jnp.where(
        beyond_live, beyond_part.reshape(piece_shape), 0.0
    )

    padded = jnp.pad(relay_cols, ((0, 0), (0, 0), (relay_rows, relay_rows), (0, 0)))
    slots = []
    for target in range(row_devices):
        first = row_anchor - 1 + span_rows * target - parent_rows * row_rank
        first = jnp.clip(first, -relay_rows, parent_rows) + relay_rows
        slots.append(lax.dynamic_slice_in_dim(padded, first, relay_rows, axis=2))
    stacked = jnp.stack(slots, axis=0)
    slot_shape = stacked.shape[1:]
    planes = slot_shape[0] * slot_shape[1] * slot_shape[2]
    lanes = relay_columns
    while (planes * lanes) % 128:
        lanes += 1
    stacked = jnp.pad(stacked, ((0, 0),) * 4 + ((0, lanes - relay_columns),))
    stacked = stacked.reshape(row_devices, planes * lanes // 128, 128)
    received = gather(stacked, "gx", 10, spread=True)
    received = received.reshape((row_devices,) + slot_shape[:3] + (lanes,))
    relay = jnp.sum(received[..., :relay_columns], axis=0)

    forcing = refine(relay)
    row_global = row_rank * nest_rows + jnp.arange(nest_rows, dtype=jnp.int32)
    column_global = column_rank * nest_columns + jnp.arange(nest_columns, dtype=jnp.int32)
    weight = relax_weight(
        row_global, column_global, row_devices * nest_rows, column_devices * nest_columns
    )
    state = nest_fields
    sides = edges(state)
    for substep in range(SUBSTEPS):
        state, *sides = stencil(
            state, neighbours(sides, 3 + substep), nest_velocity, nest_mixing, forcing, weight
        )

    coarse = block_mean(state)
    fields_count, levels_count = coarse.shape[:2]
    collected = gather(coarse.reshape((-1,) + coarse.shape[2:]), "gx", 9)
    gathered = jnp.moveaxis(collected, 0, 1).reshape(
        fields_count, levels_count, row_devices * span_rows, coarse.shape[3]
    )
    total_span = row_devices * span_rows
    gathered = jnp.pad(gathered, ((0, 0), (0, 0), (parent_rows, parent_rows), (0, 0)))
    first = jnp.clip(parent_rows * row_rank - row_anchor, -parent_rows, total_span)
    strip = lax.dynamic_slice_in_dim(gathered, first + parent_rows, parent_rows, axis=2)

    routes = []
    for extra in (1, 0):
        for k in range(ratio):
            if extra == 1 and k == 0:
                continue
            pairs = [(j, p) for (p, j) in column_pairs(column_devices, base, ratio, k, extra)]
            routes.append((k, extra, pairs))
    back_branches = []
    for number, skipped in enumerate(((1, 1), (0, ratio - 1))):
        patterns = [
            (pairs, 0, slot) for slot, (k, extra, pairs) in enumerate(routes)
            if (k, extra) != (skipped[1], skipped[0])
        ]
        identity = (1, 8)[number]
        back_branches.append(
            lambda sent, patterns=patterns, identity=identity: tuple(
                exchange(sent, patterns, len(routes), "gy", identity)
            )
        )
    late = (offset > (ratio - 1) * span_columns - span_columns - 1).astype(jnp.int32)
    parts = lax.switch(late, back_branches, flat(strip)[None])
    joined = jnp.concatenate([part.reshape(strip.shape) for part in parts], axis=3)
    start = (ratio - 1) * span_columns - 1 - offset
    fed_back = lax.dynamic_slice_in_dim(joined, start, parent_columns, axis=3)

    relative_rows = row_rank * parent_rows + jnp.arange(parent_rows, dtype=jnp.int32) - row_anchor
    relative_columns = (
        column_rank * parent_columns + jnp.arange(parent_columns, dtype=jnp.int32) - column_anchor
    )
    rows_valid = within(relative_rows, total_span)
    columns_valid = within(relative_columns, column_devices * span_columns)
    covered = rows_valid[:, None] & columns_valid[None, :]
    parent_result = jnp.where(covered, fed_back, parent_next)
    return (parent_result, state)


def solution(mesh):
    placed = (
        P(None, None, "gx", "gy"),
        P(None, None, "gx", "gy"),
        P(None, "gx", "gy"),
        P(None, None, "gx", "gy"),
        P(None, None, "gx", "gy"),
        P(None, "gx", "gy"),
        P(),
    )
    return jax.shard_map(
        per_device,
        mesh=mesh,
        in_specs=placed,
        out_specs=(P(None, None, "gx", "gy"), P(None, None, "gx", "gy")),
        check_vma=False,
    )
```

```python
import jax
import jax.numpy as jnp
from jax import lax
from jax.experimental import pallas as pl
from jax.experimental.pallas import tpu as pltpu
from jax.sharding import PartitionSpec as P

MESH = pl.DeviceIdType.MESH

SUBSTEPS = 3


third = 1.0 / 3.0
two_thirds = 2.0 / 3.0
nudge_floor = 0.1
relax_width = 4.0


def shift_pairs(count, step):
    return [(i, i + step) for i in range(count) if 0 <= i + step < count]


def halo_kernel(rows, cols, *refs):
    sources, targets, send_sems, recv_sems = refs[:4], refs[4:8], refs[8], refs[9]
    x = lax.axis_index("gx")
    y = lax.axis_index("gy")
    routes = (("gx", x, 1, rows), ("gx", x, -1, rows), ("gy", y, 1, cols), ("gy", y, -1, cols))
    barrier = pltpu.get_barrier_semaphore()
    for axis, own, step, count in routes:
        @pl.when((own + step >= 0) & (own + step < count))
        def _():
            pl.semaphore_signal(barrier, 1, device_id={axis: own + step}, device_id_type=MESH)

    peers = (x + rows - 1) // rows + (2 * rows - 2 - x) // rows
    peers = peers + (y + cols - 1) // cols + (2 * cols - 2 - y) // cols
    pl.semaphore_wait(barrier, peers)
    copies = []
    for number, (axis, own, step, count) in enumerate(routes):
        copy = pltpu.make_async_remote_copy(
            src_ref=sources[number],
            dst_ref=targets[number],
            send_sem=send_sems.at[number],
            recv_sem=recv_sems.at[number],
            device_id={axis: own + step},
            device_id_type=MESH,
        )
        copies.append((own, step, count, copy))

        @pl.when((own + step >= 0) & (own + step < count))
        def _():
            copy.start()

    for number, (own, step, count, copy) in enumerate(copies):
        @pl.when((own + step >= 0) & (own + step < count))
        def _():
            copy.wait_send()

        @pl.when((own - step >= 0) & (own - step < count))
        def _():
            copy.wait_recv()

        @pl.when((own - step < 0) | (own - step >= count))
        def _():
            targets[number][...] = jnp.zeros(targets[number].shape, targets[number].dtype)


def edges(cells):
    fields, levels, height, width = cells.shape
    planes = fields * levels
    return (
        cells[:, :, -1, :].reshape(planes, width),
        cells[:, :, 0, :].reshape(planes, width),
        cells[:, :, :, -1].reshape(planes, height),
        cells[:, :, :, 0].reshape(planes, height),
    )


def neighbours(sources, identity):
    rows = lax.axis_size("gx")
    cols = lax.axis_size("gy")
    received = pl.pallas_call(
        lambda *refs: halo_kernel(rows, cols, *refs),
        out_shape=tuple(jax.ShapeDtypeStruct(part.shape, part.dtype) for part in sources),
        in_specs=[pl.BlockSpec(memory_space=pltpu.VMEM)] * 4,
        out_specs=tuple(pl.BlockSpec(memory_space=pltpu.VMEM) for _ in range(4)),
        scratch_shapes=[pltpu.SemaphoreType.DMA((4,)), pltpu.SemaphoreType.DMA((4,))],
        compiler_params=pltpu.CompilerParams(collective_id=identity, has_side_effects=True),
    )(*sources)
    return received


def update(values, halo, velocity, mixing):
    west_row, east_row, south_col, north_col = halo
    western = jnp.concatenate([west_row, values[:, :, :-1, :]], axis=2)
    eastern = jnp.concatenate([values[:, :, 1:, :], east_row], axis=2)
    southern = jnp.concatenate([south_col, values[:, :, :, :-1]], axis=3)
    northern = jnp.concatenate([values[:, :, :, 1:], north_col], axis=3)
    along_rows = velocity[0]
    along_columns = velocity[1]
    upwind = (
        jnp.maximum(along_rows, 0.0) * (values - western)
        + jnp.minimum(along_rows, 0.0) * (eastern - values)
        + jnp.maximum(along_columns, 0.0) * (values - southern)
        + jnp.minimum(along_columns, 0.0) * (northern - values)
    )
    return values - upwind + mixing * (eastern + western + northern + southern - 4.0 * values)


def refine_rows(block):
    lower = block[:, :, :-2]
    centre = block[:, :, 1:-1]
    upper = block[:, :, 2:]
    stacked = jnp.stack(
        (third * lower + two_thirds * centre, centre, two_thirds * centre + third * upper), axis=3
    )
    extent = centre.shape
    return stacked.reshape(extent[0], extent[1], 3 * extent[2], extent[3])


def refine_columns(block):
    lower = block[:, :, :, :-2]
    centre = block[:, :, :, 1:-1]
    upper = block[:, :, :, 2:]
    stacked = jnp.stack(
        (third * lower + two_thirds * centre, centre, two_thirds * centre + third * upper), axis=4
    )
    extent = centre.shape
    return stacked.reshape(extent[0], extent[1], extent[2], 3 * extent[3])


def refining(count):
    fine = jnp.arange(3 * count, dtype=jnp.int32)[:, None]
    coarse = jnp.arange(count + 2, dtype=jnp.int32)[None, :]
    centre = fine // 3 + 1
    phase = fine % 3
    lower = jnp.where(phase == 0, third, jnp.where(phase == 2, 0.0, 0.0))
    upper = jnp.where(phase == 2, third, 0.0)
    middle = jnp.where(phase == 1, 1.0, two_thirds)
    return (
        jnp.where(coarse == centre, middle, 0.0)
        + jnp.where(coarse == centre - 1, lower, 0.0)
        + jnp.where(coarse == centre + 1, upper, 0.0)
    ).astype(jnp.float32)


def refine(block):
    exact = lax.Precision.HIGHEST
    rows = block.shape[2] - 2
    cols = block.shape[3] - 2
    down = jnp.einsum("ar,flrc->flac", refining(rows), block, precision=exact)
    return jnp.einsum("flac,bc->flab", down, refining(cols), precision=exact)


def grouping(count):
    rows = jnp.arange(count, dtype=jnp.int32)[:, None] // 3
    return (rows == jnp.arange(count // 3, dtype=jnp.int32)[None, :]).astype(jnp.float32)


def block_mean(state):
    extent = state.shape
    exact = lax.Precision.HIGHEST
    across = jnp.einsum("flrc,cb->flrb", state, grouping(extent[3]), precision=exact)
    down = jnp.einsum("ra,flrb->flab", grouping(extent[2]), across, precision=exact)
    return down / 9.0


def relax_weight(row_global, column_global, total_rows, total_columns):
    row_distance = jnp.minimum(row_global, total_rows - 1 - row_global)
    column_distance = jnp.minimum(column_global, total_columns - 1 - column_global)
    distance = jnp.minimum(row_distance[:, None], column_distance[None, :]).astype(jnp.float32)
    return nudge_floor + (1.0 - nudge_floor) * jnp.exp(-distance / relax_width)


def within(positions, limit):
    return (positions >= 0) & (positions < limit)


def column_pairs(count, base, ratio, k, extra):
    pairs = []
    for m in range(count):
        j = ratio * m + k
        p = base + m + extra
        if j < count and p < count:
            pairs.append((p, j))
    return pairs


def exchange_kernel(axis, patterns, local, send_ref, recv_ref, send_sems, recv_sems):
    me = lax.axis_index(axis)
    receivers = {}
    for pairs, _, slot in patterns:
        for a, b in pairs:
            receivers.setdefault(slot, set()).add(b)
    for a, source, slot in local:
        receivers.setdefault(slot, set()).add(a)
    for slot in range(recv_ref.shape[0]):
        idle = None
        for device in sorted(receivers.get(slot, ())):
            test = me != device
            idle = test if idle is None else idle & test
        if idle is None:
            recv_ref[slot] = jnp.zeros(recv_ref.shape[1:], recv_ref.dtype)
            continue

        @pl.when(idle)
        def _():
            recv_ref[slot] = jnp.zeros(recv_ref.shape[1:], recv_ref.dtype)

    for a, source, slot in local:
        @pl.when(me == a)
        def _():
            recv_ref[slot] = send_ref[source]

    barrier = pltpu.get_barrier_semaphore()
    links = [pair for pairs, _, _ in patterns for pair in pairs]
    for a, b in links:
        @pl.when(me == a)
        def _():
            pl.semaphore_signal(barrier, 1, device_id={axis: b}, device_id_type=MESH)

        @pl.when(me == b)
        def _():
            pl.semaphore_signal(barrier, 1, device_id={axis: a}, device_id_type=MESH)

    peers = {}
    for a, b in links:
        peers[a] = peers.get(a, 0) + 1
        peers[b] = peers.get(b, 0) + 1
    for device, count in sorted(peers.items()):
        @pl.when(me == device)
        def _():
            pl.semaphore_wait(barrier, count)

    copies = []
    for number, (pairs, source, slot) in enumerate(patterns):
        for a, b in pairs:
            copy = pltpu.make_async_remote_copy(
                src_ref=send_ref.at[source],
                dst_ref=recv_ref.at[slot],
                send_sem=send_sems.at[number],
                recv_sem=recv_sems.at[slot],
                device_id={axis: b},
                device_id_type=MESH,
            )
            copies.append((a, b, copy))

            @pl.when(me == a)
            def _():
                copy.start()

    for a, b, copy in copies:
        @pl.when(me == a)
        def _():
            copy.wait_send()

        @pl.when(me == b)
        def _():
            copy.wait_recv()


def exchange(pieces, patterns, slots, axis, identity):
    remote = [([(a, b) for a, b in pairs if a != b], source, slot) for pairs, source, slot in patterns]
    remote = [entry for entry in remote if entry[0]]
    local = [(a, source, slot) for pairs, source, slot in patterns for a, b in pairs if a == b]
    shape = pieces.shape[1:]
    received = pl.pallas_call(
        lambda *refs: exchange_kernel(axis, remote, local, *refs),
        out_shape=jax.ShapeDtypeStruct((slots,) + shape, pieces.dtype),
        in_specs=[pl.BlockSpec(memory_space=pltpu.VMEM)],
        out_specs=pl.BlockSpec(memory_space=pltpu.VMEM),
        scratch_shapes=[
            pltpu.SemaphoreType.DMA((len(remote),)),
            pltpu.SemaphoreType.DMA((slots,)),
        ],
        compiler_params=pltpu.CompilerParams(collective_id=identity, has_side_effects=True),
    )(pieces)
    return [received[slot] for slot in range(slots)]


def gather_kernel(axis, count, source, target, send_sems, recv_sems):
    me = lax.axis_index(axis)
    barrier = pltpu.get_barrier_semaphore()
    for delta in range(1, count):
        pl.semaphore_signal(
            barrier, 1, device_id={axis: (me + delta) % count}, device_id_type=MESH
        )
    pl.semaphore_wait(barrier, count - 1)
    outgoing = []
    for delta in range(1, count):
        copy = pltpu.make_async_remote_copy(
            src_ref=source,
            dst_ref=target.at[me],
            send_sem=send_sems.at[delta - 1],
            recv_sem=recv_sems.at[delta - 1],
            device_id={axis: (me + delta) % count},
            device_id_type=MESH,
        )
        copy.start()
        outgoing.append(copy)
    target[me] = source[...]
    for delta, copy in zip(range(1, count), outgoing):
        copy.wait_send()
        incoming = pltpu.make_async_remote_copy(
            src_ref=source,
            dst_ref=target.at[(me + count - delta) % count],
            send_sem=send_sems.at[delta - 1],
            recv_sem=recv_sems.at[delta - 1],
            device_id={axis: (me + count - delta) % count},
            device_id_type=MESH,
        )
        incoming.wait_recv()


def gather(block, axis, identity):
    count = lax.axis_size(axis)
    return pl.pallas_call(
        lambda *refs: gather_kernel(axis, count, *refs),
        out_shape=jax.ShapeDtypeStruct((count,) + block.shape, block.dtype),
        in_specs=[pl.BlockSpec(memory_space=pltpu.VMEM)],
        out_specs=pl.BlockSpec(memory_space=pltpu.VMEM),
        scratch_shapes=[
            pltpu.SemaphoreType.DMA((count - 1,)),
            pltpu.SemaphoreType.DMA((count - 1,)),
        ],
        compiler_params=pltpu.CompilerParams(collective_id=identity, has_side_effects=True),
    )(block)


def stencil_kernel(relaxed, *refs):
    if relaxed:
        (values, velocity, mixing, western, eastern, southern, northern, forcing, weight) = refs[:9]
        out, last_row, first_row, last_col, first_col = refs[9:]
    else:
        (values, velocity, mixing, western, eastern, southern, northern, out) = refs
    levels, height, width = values.shape[1:]
    row = lax.broadcasted_iota(jnp.int32, (height, width), 0)
    col = lax.broadcasted_iota(jnp.int32, (height, width), 1)
    eye = (
        lax.broadcasted_iota(jnp.int32, (height, height), 0)
        == lax.broadcasted_iota(jnp.int32, (height, height), 1)
    ).astype(jnp.float32)
    first = pl.multiple_of(pl.program_id(0) * levels, levels)
    numbers = (((1,), (1,)), ((), ()))
    exact = lax.Precision.HIGHEST
    south_cols = lax.dot_general(
        eye, southern[pl.ds(first, levels), :], numbers, precision=exact,
        preferred_element_type=jnp.float32,
    )
    north_cols = lax.dot_general(
        eye, northern[pl.ds(first, levels), :], numbers, precision=exact,
        preferred_element_type=jnp.float32,
    )
    picks = lax.broadcasted_iota(jnp.int32, (8, width), 1)
    chosen = lax.broadcasted_iota(jnp.int32, (8, width), 0)
    ends = ((chosen == 0) & (picks == 0)) | ((chosen == 1) & (picks == width - 1))
    ends = ends.astype(jnp.float32)
    for level in range(levels):
        q = values[0, level]
        west_row = western[pl.ds(first + level, 1), :]
        east_row = eastern[pl.ds(first + level, 1), :]
        west = jnp.where(row == 0, west_row, pltpu.roll(q, 1, 0))
        east = jnp.where(row == height - 1, east_row, pltpu.roll(q, height - 1, 0))
        south = jnp.where(col == 0, south_cols[:, level:level + 1], pltpu.roll(q, 1, 1))
        north = jnp.where(
            col == width - 1, north_cols[:, level:level + 1], pltpu.roll(q, width - 1, 1)
        )
        along_rows = velocity[0, level]
        along_columns = velocity[1, level]
        upwind = (
            jnp.maximum(along_rows, 0.0) * (q - west)
            + jnp.minimum(along_rows, 0.0) * (east - q)
            + jnp.maximum(along_columns, 0.0) * (q - south)
            + jnp.minimum(along_columns, 0.0) * (north - q)
        )
        moved = q - upwind + mixing[level] * (east + west + north + south - 4.0 * q)
        if relaxed:
            moved = moved + weight[...] * (forcing[0, level] - moved)
            last_row[pl.ds(first + level, 1), :] = moved[height - 1:height, :]
            first_row[pl.ds(first + level, 1), :] = moved[0:1, :]
            sides = lax.dot_general(
                ends, moved, numbers, precision=exact, preferred_element_type=jnp.float32
            )
            first_col[pl.ds(first + level, 1), :] = sides[0:1, :]
            last_col[pl.ds(first + level, 1), :] = sides[1:2, :]
        out[0, level] = moved


def stencil(values, halo, velocity, mixing, forcing=None, weight=None):
    fields, levels, height, width = values.shape
    west_row, east_row, south_col, north_col = halo
    plane = pl.BlockSpec((1, levels, height, width), lambda f: (f, 0, 0, 0))
    edge_row = pl.BlockSpec((fields * levels, width), lambda f: (0, 0))
    edge_col = pl.BlockSpec((fields * levels, height), lambda f: (0, 0))
    operands = [values, velocity, mixing, west_row, east_row, south_col, north_col]
    specs = [
        plane,
        pl.BlockSpec(velocity.shape, lambda f: (0, 0, 0, 0)),
        pl.BlockSpec(mixing.shape, lambda f: (0, 0, 0)),
        edge_row,
        edge_row,
        edge_col,
        edge_col,
    ]
    relaxed = forcing is not None
    out_shape = jax.ShapeDtypeStruct(values.shape, values.dtype)
    out_specs = plane
    if relaxed:
        operands += [forcing, weight]
        specs += [plane, pl.BlockSpec(weight.shape, lambda f: (0, 0))]
        rows_shape = jax.ShapeDtypeStruct((fields * levels, width), values.dtype)
        cols_shape = jax.ShapeDtypeStruct((fields * levels, height), values.dtype)
        out_shape = (out_shape, rows_shape, rows_shape, cols_shape, cols_shape)
        out_specs = (plane, edge_row, edge_row, edge_col, edge_col)
    return pl.pallas_call(
        lambda *refs: stencil_kernel(relaxed, *refs),
        out_shape=out_shape,
        grid=(fields,),
        in_specs=specs,
        out_specs=out_specs,
    )(*operands)


def flat(block):
    size = block.size
    return block.reshape(size // 128, 128) if size % 128 == 0 else block.reshape(-1, block.shape[-1])


def per_device(
    parent_fields,
    parent_velocity,
    parent_mixing,
    nest_fields,
    nest_velocity,
    nest_mixing,
    nest_anchor,
):
    row_rank = lax.axis_index("gx")
    column_rank = lax.axis_index("gy")
    row_devices = lax.axis_size("gx")
    column_devices = lax.axis_size("gy")
    parent_rows = parent_fields.shape[2]
    parent_columns = parent_fields.shape[3]
    nest_rows = nest_fields.shape[2]
    nest_columns = nest_fields.shape[3]
    span_rows = nest_rows // 3
    span_columns = nest_columns // 3
    ratio = parent_columns // span_columns
    base = column_devices // 2
    base_column = base * parent_columns
    relay_rows = span_rows + 2
    relay_columns = span_columns + 2
    row_anchor = nest_anchor[0]
    column_anchor = nest_anchor[1]
    offset = column_anchor - 1 - base_column

    parent_next = stencil(
        parent_fields, neighbours(edges(parent_fields), 2), parent_velocity, parent_mixing
    )

    margin = parent_columns - span_columns
    wide = jnp.pad(parent_next, ((0, 0), (0, 0), (0, 0), (margin, margin)))
    straddle = (ratio - 1) * span_columns - 2
    regimes = (
        lambda k, extra: not (extra == 1 and k == ratio - 2),
        lambda k, extra: True,
        lambda k, extra: not (extra == 0 and k == ratio - 1),
    )
    regime = (offset > straddle - span_columns).astype(jnp.int32) + (
        offset > straddle - span_columns + 1
    ).astype(jnp.int32)
    pieces = []
    routes = []
    for extra in (0, 1):
        for k in range(ratio):
            if extra == 1 and k == 0:
                continue
            start = margin + span_columns * k + offset - extra * parent_columns
            piece = lax.dynamic_slice_in_dim(wide, start, relay_columns, axis=3)
            routes.append((k, extra, len(pieces)))
            pieces.append(flat(piece))
    stacked_pieces = jnp.stack(pieces)
    branches = []
    for number, active in enumerate(regimes):
        patterns = [
            (column_pairs(column_devices, base, ratio, k, extra), index, extra)
            for k, extra, index in routes
            if active(k, extra)
        ]
        identity = (0, 6, 7)[number]
        branches.append(
            lambda stacked, patterns=patterns, identity=identity: tuple(
                exchange(stacked, patterns, 2, "gy", identity)
            )
        )
    within_part, beyond_part = lax.switch(regime, branches, stacked_pieces)
    piece_shape = parent_next.shape[:3] + (relay_columns,)
    relay_cols = within_part.reshape(piece_shape) + beyond_part.reshape(piece_shape)

    padded = jnp.pad(relay_cols, ((0, 0), (0, 0), (relay_rows, relay_rows), (0, 0)))
    slots = []
    for target in range(row_devices):
        first = row_anchor - 1 + span_rows * target - parent_rows * row_rank
        first = jnp.clip(first, -relay_rows, parent_rows) + relay_rows
        slots.append(lax.dynamic_slice_in_dim(padded, first, relay_rows, axis=2))
    stacked = jnp.stack(slots, axis=0)
    received = lax.all_to_all(stacked, "gx", split_axis=0, concat_axis=0, tiled=True)
    relay = jnp.sum(received, axis=0)

    forcing = refine(relay)
    row_global = row_rank * nest_rows + jnp.arange(nest_rows, dtype=jnp.int32)
    column_global = column_rank * nest_columns + jnp.arange(nest_columns, dtype=jnp.int32)
    weight = relax_weight(
        row_global, column_global, row_devices * nest_rows, column_devices * nest_columns
    )
    state = nest_fields
    sides = edges(state)
    for substep in range(SUBSTEPS):
        state, *sides = stencil(
            state, neighbours(sides, 3 + substep), nest_velocity, nest_mixing, forcing, weight
        )

    coarse = block_mean(state)
    fields_count, levels_count = coarse.shape[:2]
    collected = gather(coarse.reshape((-1,) + coarse.shape[2:]), "gx", 9)
    gathered = jnp.moveaxis(collected, 0, 1).reshape(
        fields_count, levels_count, row_devices * span_rows, coarse.shape[3]
    )
    total_span = row_devices * span_rows
    gathered = jnp.pad(gathered, ((0, 0), (0, 0), (parent_rows, parent_rows), (0, 0)))
    first = jnp.clip(parent_rows * row_rank - row_anchor, -parent_rows, total_span)
    strip = lax.dynamic_slice_in_dim(gathered, first + parent_rows, parent_rows, axis=2)

    routes = []
    for extra in (1, 0):
        for k in range(ratio):
            if extra == 1 and k == 0:
                continue
            pairs = [(j, p) for (p, j) in column_pairs(column_devices, base, ratio, k, extra)]
            routes.append((k, extra, pairs))
    back_branches = []
    for number, skipped in enumerate(((1, 1), (0, ratio - 1))):
        patterns = [
            (pairs, 0, slot) for slot, (k, extra, pairs) in enumerate(routes)
            if (k, extra) != (skipped[1], skipped[0])
        ]
        identity = (1, 8)[number]
        back_branches.append(
            lambda sent, patterns=patterns, identity=identity: tuple(
                exchange(sent, patterns, len(routes), "gy", identity)
            )
        )
    late = (offset > (ratio - 1) * span_columns - span_columns - 1).astype(jnp.int32)
    parts = lax.switch(late, back_branches, flat(strip)[None])
    joined = jnp.concatenate([part.reshape(strip.shape) for part in parts], axis=3)
    start = (ratio - 1) * span_columns - 1 - offset
    fed_back = lax.dynamic_slice_in_dim(joined, start, parent_columns, axis=3)

    relative_rows = row_rank * parent_rows + jnp.arange(parent_rows, dtype=jnp.int32) - row_anchor
    relative_columns = (
        column_rank * parent_columns + jnp.arange(parent_columns, dtype=jnp.int32) - column_anchor
    )
    rows_valid = within(relative_rows, total_span)
    columns_valid = within(relative_columns, column_devices * span_columns)
    covered = rows_valid[:, None] & columns_valid[None, :]
    parent_result = jnp.where(covered, fed_back, parent_next)
    return (parent_result, state)


def solution(mesh):
    placed = (
        P(None, None, "gx", "gy"),
        P(None, None, "gx", "gy"),
        P(None, "gx", "gy"),
        P(None, None, "gx", "gy"),
        P(None, None, "gx", "gy"),
        P(None, "gx", "gy"),
        P(),
    )
    return jax.shard_map(
        per_device,
        mesh=mesh,
        in_specs=placed,
        out_specs=(P(None, None, "gx", "gy"), P(None, None, "gx", "gy")),
        check_vma=False,
    )
```

```python
import jax
import jax.numpy as jnp
from jax import lax
from jax.experimental import pallas as pl
from jax.experimental.pallas import tpu as pltpu
from jax.sharding import PartitionSpec as P

MESH = pl.DeviceIdType.MESH

SUBSTEPS = 3


third = 1.0 / 3.0
two_thirds = 2.0 / 3.0
nudge_floor = 0.1
relax_width = 4.0


def shift_pairs(count, step):
    return [(i, i + step) for i in range(count) if 0 <= i + step < count]


def halo_kernel(rows, cols, *refs):
    sources, targets, send_sems, recv_sems = refs[:4], refs[4:8], refs[8], refs[9]
    x = lax.axis_index("gx")
    y = lax.axis_index("gy")
    routes = (("gx", x, 1, rows), ("gx", x, -1, rows), ("gy", y, 1, cols), ("gy", y, -1, cols))
    barrier = pltpu.get_barrier_semaphore()
    for axis, own, step, count in routes:
        @pl.when((own + step >= 0) & (own + step < count))
        def _():
            pl.semaphore_signal(barrier, 1, device_id={axis: own + step}, device_id_type=MESH)

    peers = (x + rows - 1) // rows + (2 * rows - 2 - x) // rows
    peers = peers + (y + cols - 1) // cols + (2 * cols - 2 - y) // cols
    pl.semaphore_wait(barrier, peers)
    copies = []
    for number, (axis, own, step, count) in enumerate(routes):
        copy = pltpu.make_async_remote_copy(
            src_ref=sources[number],
            dst_ref=targets[number],
            send_sem=send_sems.at[number],
            recv_sem=recv_sems.at[number],
            device_id={axis: own + step},
            device_id_type=MESH,
        )
        copies.append((own, step, count, copy))

        @pl.when((own + step >= 0) & (own + step < count))
        def _():
            copy.start()

    for number, (own, step, count, copy) in enumerate(copies):
        @pl.when((own + step >= 0) & (own + step < count))
        def _():
            copy.wait_send()

        @pl.when((own - step >= 0) & (own - step < count))
        def _():
            copy.wait_recv()

        @pl.when((own - step < 0) | (own - step >= count))
        def _():
            targets[number][...] = jnp.zeros(targets[number].shape, targets[number].dtype)


def edges(cells):
    fields, levels, height, width = cells.shape
    planes = fields * levels
    return (
        cells[:, :, -1, :].reshape(planes, width),
        cells[:, :, 0, :].reshape(planes, width),
        cells[:, :, :, -1].reshape(planes, height),
        cells[:, :, :, 0].reshape(planes, height),
    )


def neighbours(sources, identity):
    rows = lax.axis_size("gx")
    cols = lax.axis_size("gy")
    received = pl.pallas_call(
        lambda *refs: halo_kernel(rows, cols, *refs),
        out_shape=tuple(jax.ShapeDtypeStruct(part.shape, part.dtype) for part in sources),
        in_specs=[pl.BlockSpec(memory_space=pltpu.VMEM)] * 4,
        out_specs=tuple(pl.BlockSpec(memory_space=pltpu.VMEM) for _ in range(4)),
        scratch_shapes=[pltpu.SemaphoreType.DMA((4,)), pltpu.SemaphoreType.DMA((4,))],
        compiler_params=pltpu.CompilerParams(collective_id=identity, has_side_effects=True),
    )(*sources)
    return received


def update(values, halo, velocity, mixing):
    west_row, east_row, south_col, north_col = halo
    western = jnp.concatenate([west_row, values[:, :, :-1, :]], axis=2)
    eastern = jnp.concatenate([values[:, :, 1:, :], east_row], axis=2)
    southern = jnp.concatenate([south_col, values[:, :, :, :-1]], axis=3)
    northern = jnp.concatenate([values[:, :, :, 1:], north_col], axis=3)
    along_rows = velocity[0]
    along_columns = velocity[1]
    upwind = (
        jnp.maximum(along_rows, 0.0) * (values - western)
        + jnp.minimum(along_rows, 0.0) * (eastern - values)
        + jnp.maximum(along_columns, 0.0) * (values - southern)
        + jnp.minimum(along_columns, 0.0) * (northern - values)
    )
    return values - upwind + mixing * (eastern + western + northern + southern - 4.0 * values)


def refine_rows(block):
    lower = block[:, :, :-2]
    centre = block[:, :, 1:-1]
    upper = block[:, :, 2:]
    stacked = jnp.stack(
        (third * lower + two_thirds * centre, centre, two_thirds * centre + third * upper), axis=3
    )
    extent = centre.shape
    return stacked.reshape(extent[0], extent[1], 3 * extent[2], extent[3])


def refine_columns(block):
    lower = block[:, :, :, :-2]
    centre = block[:, :, :, 1:-1]
    upper = block[:, :, :, 2:]
    stacked = jnp.stack(
        (third * lower + two_thirds * centre, centre, two_thirds * centre + third * upper), axis=4
    )
    extent = centre.shape
    return stacked.reshape(extent[0], extent[1], extent[2], 3 * extent[3])


def refining(count):
    fine = jnp.arange(3 * count, dtype=jnp.int32)[:, None]
    coarse = jnp.arange(count + 2, dtype=jnp.int32)[None, :]
    centre = fine // 3 + 1
    phase = fine % 3
    lower = jnp.where(phase == 0, third, jnp.where(phase == 2, 0.0, 0.0))
    upper = jnp.where(phase == 2, third, 0.0)
    middle = jnp.where(phase == 1, 1.0, two_thirds)
    return (
        jnp.where(coarse == centre, middle, 0.0)
        + jnp.where(coarse == centre - 1, lower, 0.0)
        + jnp.where(coarse == centre + 1, upper, 0.0)
    ).astype(jnp.float32)


def refine(block):
    exact = lax.Precision.HIGHEST
    rows = block.shape[2] - 2
    cols = block.shape[3] - 2
    down = jnp.einsum("ar,flrc->flac", refining(rows), block, precision=exact)
    return jnp.einsum("flac,bc->flab", down, refining(cols), precision=exact)


def grouping(count):
    rows = jnp.arange(count, dtype=jnp.int32)[:, None] // 3
    return (rows == jnp.arange(count // 3, dtype=jnp.int32)[None, :]).astype(jnp.float32)


def block_mean(state):
    extent = state.shape
    exact = lax.Precision.HIGHEST
    across = jnp.einsum("flrc,cb->flrb", state, grouping(extent[3]), precision=exact)
    down = jnp.einsum("ra,flrb->flab", grouping(extent[2]), across, precision=exact)
    return down / 9.0


def relax_weight(row_global, column_global, total_rows, total_columns):
    row_distance = jnp.minimum(row_global, total_rows - 1 - row_global)
    column_distance = jnp.minimum(column_global, total_columns - 1 - column_global)
    distance = jnp.minimum(row_distance[:, None], column_distance[None, :]).astype(jnp.float32)
    return nudge_floor + (1.0 - nudge_floor) * jnp.exp(-distance / relax_width)


def within(positions, limit):
    return (positions >= 0) & (positions < limit)


def column_pairs(count, base, ratio, k, extra):
    pairs = []
    for m in range(count):
        j = ratio * m + k
        p = base + m + extra
        if j < count and p < count:
            pairs.append((p, j))
    return pairs


def exchange_kernel(axis, patterns, local, send_ref, recv_ref, send_sems, recv_sems):
    me = lax.axis_index(axis)
    receivers = {}
    for pairs, _, slot in patterns:
        for a, b in pairs:
            receivers.setdefault(slot, set()).add(b)
    for a, source, slot in local:
        receivers.setdefault(slot, set()).add(a)
    for slot in range(recv_ref.shape[0]):
        idle = None
        for device in sorted(receivers.get(slot, ())):
            test = me != device
            idle = test if idle is None else idle & test
        if idle is None:
            recv_ref[slot] = jnp.zeros(recv_ref.shape[1:], recv_ref.dtype)
            continue

        @pl.when(idle)
        def _():
            recv_ref[slot] = jnp.zeros(recv_ref.shape[1:], recv_ref.dtype)

    for a, source, slot in local:
        @pl.when(me == a)
        def _():
            recv_ref[slot] = send_ref[source]

    barrier = pltpu.get_barrier_semaphore()
    links = [pair for pairs, _, _ in patterns for pair in pairs]
    for a, b in links:
        @pl.when(me == a)
        def _():
            pl.semaphore_signal(barrier, 1, device_id={axis: b}, device_id_type=MESH)

        @pl.when(me == b)
        def _():
            pl.semaphore_signal(barrier, 1, device_id={axis: a}, device_id_type=MESH)

    peers = {}
    for a, b in links:
        peers[a] = peers.get(a, 0) + 1
        peers[b] = peers.get(b, 0) + 1
    for device, count in sorted(peers.items()):
        @pl.when(me == device)
        def _():
            pl.semaphore_wait(barrier, count)

    copies = []
    for number, (pairs, source, slot) in enumerate(patterns):
        for a, b in pairs:
            copy = pltpu.make_async_remote_copy(
                src_ref=send_ref.at[source],
                dst_ref=recv_ref.at[slot],
                send_sem=send_sems.at[number],
                recv_sem=recv_sems.at[slot],
                device_id={axis: b},
                device_id_type=MESH,
            )
            copies.append((a, b, copy))

            @pl.when(me == a)
            def _():
                copy.start()

    for a, b, copy in copies:
        @pl.when(me == a)
        def _():
            copy.wait_send()

        @pl.when(me == b)
        def _():
            copy.wait_recv()


def exchange(pieces, patterns, slots, axis, identity):
    remote = [([(a, b) for a, b in pairs if a != b], source, slot) for pairs, source, slot in patterns]
    remote = [entry for entry in remote if entry[0]]
    local = [(a, source, slot) for pairs, source, slot in patterns for a, b in pairs if a == b]
    shape = pieces.shape[1:]
    received = pl.pallas_call(
        lambda *refs: exchange_kernel(axis, remote, local, *refs),
        out_shape=jax.ShapeDtypeStruct((slots,) + shape, pieces.dtype),
        in_specs=[pl.BlockSpec(memory_space=pltpu.VMEM)],
        out_specs=pl.BlockSpec(memory_space=pltpu.VMEM),
        scratch_shapes=[
            pltpu.SemaphoreType.DMA((len(remote),)),
            pltpu.SemaphoreType.DMA((slots,)),
        ],
        compiler_params=pltpu.CompilerParams(collective_id=identity, has_side_effects=True),
    )(pieces)
    return [received[slot] for slot in range(slots)]


def gather_kernel(axis, count, source, target, send_sems, recv_sems):
    me = lax.axis_index(axis)
    barrier = pltpu.get_barrier_semaphore()
    for delta in range(1, count):
        pl.semaphore_signal(
            barrier, 1, device_id={axis: (me + delta) % count}, device_id_type=MESH
        )
    pl.semaphore_wait(barrier, count - 1)
    outgoing = []
    for delta in range(1, count):
        copy = pltpu.make_async_remote_copy(
            src_ref=source,
            dst_ref=target.at[me],
            send_sem=send_sems.at[delta - 1],
            recv_sem=recv_sems.at[delta - 1],
            device_id={axis: (me + delta) % count},
            device_id_type=MESH,
        )
        copy.start()
        outgoing.append(copy)
    target[me] = source[...]
    for delta, copy in zip(range(1, count), outgoing):
        copy.wait_send()
        incoming = pltpu.make_async_remote_copy(
            src_ref=source,
            dst_ref=target.at[(me + count - delta) % count],
            send_sem=send_sems.at[delta - 1],
            recv_sem=recv_sems.at[delta - 1],
            device_id={axis: (me + count - delta) % count},
            device_id_type=MESH,
        )
        incoming.wait_recv()


def gather(block, axis, identity):
    count = lax.axis_size(axis)
    return pl.pallas_call(
        lambda *refs: gather_kernel(axis, count, *refs),
        out_shape=jax.ShapeDtypeStruct((count,) + block.shape, block.dtype),
        in_specs=[pl.BlockSpec(memory_space=pltpu.VMEM)],
        out_specs=pl.BlockSpec(memory_space=pltpu.VMEM),
        scratch_shapes=[
            pltpu.SemaphoreType.DMA((count - 1,)),
            pltpu.SemaphoreType.DMA((count - 1,)),
        ],
        compiler_params=pltpu.CompilerParams(collective_id=identity, has_side_effects=True),
    )(block)


def stencil_kernel(relaxed, *refs):
    if relaxed:
        (values, velocity, mixing, western, eastern, southern, northern, forcing, weight) = refs[:9]
        out, last_row, first_row, last_col, first_col = refs[9:]
    else:
        (values, velocity, mixing, western, eastern, southern, northern, out) = refs
    levels, height, width = values.shape[1:]
    row = lax.broadcasted_iota(jnp.int32, (height, width), 0)
    col = lax.broadcasted_iota(jnp.int32, (height, width), 1)
    eye = (
        lax.broadcasted_iota(jnp.int32, (height, height), 0)
        == lax.broadcasted_iota(jnp.int32, (height, height), 1)
    ).astype(jnp.float32)
    first = pl.multiple_of(pl.program_id(0) * levels, levels)
    numbers = (((1,), (1,)), ((), ()))
    exact = lax.Precision.HIGHEST
    south_cols = lax.dot_general(
        eye, southern[pl.ds(first, levels), :], numbers, precision=exact,
        preferred_element_type=jnp.float32,
    )
    north_cols = lax.dot_general(
        eye, northern[pl.ds(first, levels), :], numbers, precision=exact,
        preferred_element_type=jnp.float32,
    )
    picks = lax.broadcasted_iota(jnp.int32, (8, width), 1)
    chosen = lax.broadcasted_iota(jnp.int32, (8, width), 0)
    ends = ((chosen == 0) & (picks == 0)) | ((chosen == 1) & (picks == width - 1))
    ends = ends.astype(jnp.float32)
    for level in range(levels):
        q = values[0, level]
        west_row = western[pl.ds(first + level, 1), :]
        east_row = eastern[pl.ds(first + level, 1), :]
        west = jnp.where(row == 0, west_row, pltpu.roll(q, 1, 0))
        east = jnp.where(row == height - 1, east_row, pltpu.roll(q, height - 1, 0))
        south = jnp.where(col == 0, south_cols[:, level:level + 1], pltpu.roll(q, 1, 1))
        north = jnp.where(
            col == width - 1, north_cols[:, level:level + 1], pltpu.roll(q, width - 1, 1)
        )
        along_rows = velocity[0, level]
        along_columns = velocity[1, level]
        upwind = (
            jnp.maximum(along_rows, 0.0) * (q - west)
            + jnp.minimum(along_rows, 0.0) * (east - q)
            + jnp.maximum(along_columns, 0.0) * (q - south)
            + jnp.minimum(along_columns, 0.0) * (north - q)
        )
        moved = q - upwind + mixing[level] * (east + west + north + south - 4.0 * q)
        if relaxed:
            moved = moved + weight[...] * (forcing[0, level] - moved)
            last_row[pl.ds(first + level, 1), :] = moved[height - 1:height, :]
            first_row[pl.ds(first + level, 1), :] = moved[0:1, :]
            sides = lax.dot_general(
                ends, moved, numbers, precision=exact, preferred_element_type=jnp.float32
            )
            first_col[pl.ds(first + level, 1), :] = sides[0:1, :]
            last_col[pl.ds(first + level, 1), :] = sides[1:2, :]
        out[0, level] = moved


def stencil(values, halo, velocity, mixing, forcing=None, weight=None):
    fields, levels, height, width = values.shape
    west_row, east_row, south_col, north_col = halo
    plane = pl.BlockSpec((1, levels, height, width), lambda f: (f, 0, 0, 0))
    edge_row = pl.BlockSpec((fields * levels, width), lambda f: (0, 0))
    edge_col = pl.BlockSpec((fields * levels, height), lambda f: (0, 0))
    operands = [values, velocity, mixing, west_row, east_row, south_col, north_col]
    specs = [
        plane,
        pl.BlockSpec(velocity.shape, lambda f: (0, 0, 0, 0)),
        pl.BlockSpec(mixing.shape, lambda f: (0, 0, 0)),
        edge_row,
        edge_row,
        edge_col,
        edge_col,
    ]
    relaxed = forcing is not None
    out_shape = jax.ShapeDtypeStruct(values.shape, values.dtype)
    out_specs = plane
    if relaxed:
        operands += [forcing, weight]
        specs += [plane, pl.BlockSpec(weight.shape, lambda f: (0, 0))]
        rows_shape = jax.ShapeDtypeStruct((fields * levels, width), values.dtype)
        cols_shape = jax.ShapeDtypeStruct((fields * levels, height), values.dtype)
        out_shape = (out_shape, rows_shape, rows_shape, cols_shape, cols_shape)
        out_specs = (plane, edge_row, edge_row, edge_col, edge_col)
    return pl.pallas_call(
        lambda *refs: stencil_kernel(relaxed, *refs),
        out_shape=out_shape,
        grid=(fields,),
        in_specs=specs,
        out_specs=out_specs,
    )(*operands)


def flat(block):
    size = block.size
    return block.reshape(size // 128, 128) if size % 128 == 0 else block.reshape(-1, block.shape[-1])


def per_device(
    parent_fields,
    parent_velocity,
    parent_mixing,
    nest_fields,
    nest_velocity,
    nest_mixing,
    nest_anchor,
):
    row_rank = lax.axis_index("gx")
    column_rank = lax.axis_index("gy")
    row_devices = lax.axis_size("gx")
    column_devices = lax.axis_size("gy")
    parent_rows = parent_fields.shape[2]
    parent_columns = parent_fields.shape[3]
    nest_rows = nest_fields.shape[2]
    nest_columns = nest_fields.shape[3]
    span_rows = nest_rows // 3
    span_columns = nest_columns // 3
    ratio = parent_columns // span_columns
    base = column_devices // 2
    base_column = base * parent_columns
    relay_rows = span_rows + 2
    relay_columns = span_columns + 2
    row_anchor = nest_anchor[0]
    column_anchor = nest_anchor[1]
    offset = column_anchor - 1 - base_column

    parent_next = stencil(
        parent_fields, neighbours(edges(parent_fields), 2), parent_velocity, parent_mixing
    )

    margin = parent_columns - span_columns
    wide = jnp.pad(parent_next, ((0, 0), (0, 0), (0, 0), (margin, margin)))
    straddle = (ratio - 1) * span_columns - 2
    regimes = (
        lambda k, extra: not (extra == 1 and k == ratio - 2),
        lambda k, extra: True,
        lambda k, extra: not (extra == 0 and k == ratio - 1),
    )
    regime = (offset > straddle - span_columns).astype(jnp.int32) + (
        offset > straddle - span_columns + 1
    ).astype(jnp.int32)
    pieces = []
    routes = []
    for extra in (0, 1):
        for k in range(ratio):
            if extra == 1 and k == 0:
                continue
            start = margin + span_columns * k + offset - extra * parent_columns
            piece = lax.dynamic_slice_in_dim(wide, start, relay_columns, axis=3)
            routes.append((k, extra, len(pieces)))
            pieces.append(flat(piece))
    stacked_pieces = jnp.stack(pieces)
    branches = []
    for number, active in enumerate(regimes):
        patterns = [
            (column_pairs(column_devices, base, ratio, k, extra), index, extra)
            for k, extra, index in routes
            if active(k, extra)
        ]
        identity = (0, 6, 7)[number]
        branches.append(
            lambda stacked, patterns=patterns, identity=identity: tuple(
                exchange(stacked, patterns, 2, "gy", identity)
            )
        )
    within_part, beyond_part = lax.switch(regime, branches, stacked_pieces)
    piece_shape = parent_next.shape[:3] + (relay_columns,)
    relay_cols = within_part.reshape(piece_shape) + beyond_part.reshape(piece_shape)

    padded = jnp.pad(relay_cols, ((0, 0), (0, 0), (relay_rows, relay_rows), (0, 0)))
    targets = jnp.arange(row_devices, dtype=jnp.int32)[:, None]
    first = row_anchor - 1 + span_rows * targets - parent_rows * row_rank
    first = jnp.clip(first, -relay_rows, parent_rows) + relay_rows
    picks = first + jnp.arange(relay_rows, dtype=jnp.int32)[None, :]
    stacked = jnp.take(padded, picks, axis=2)
    received = lax.all_to_all(stacked, "gx", split_axis=2, concat_axis=2, tiled=True)
    relay = jnp.sum(received, axis=2)

    forcing = refine(relay)
    row_global = row_rank * nest_rows + jnp.arange(nest_rows, dtype=jnp.int32)
    column_global = column_rank * nest_columns + jnp.arange(nest_columns, dtype=jnp.int32)
    weight = relax_weight(
        row_global, column_global, row_devices * nest_rows, column_devices * nest_columns
    )
    state = nest_fields
    sides = edges(state)
    for substep in range(SUBSTEPS):
        state, *sides = stencil(
            state, neighbours(sides, 3 + substep), nest_velocity, nest_mixing, forcing, weight
        )

    coarse = block_mean(state)
    fields_count, levels_count = coarse.shape[:2]
    collected = gather(coarse.reshape((-1,) + coarse.shape[2:]), "gx", 9)
    gathered = jnp.moveaxis(collected, 0, 1).reshape(
        fields_count, levels_count, row_devices * span_rows, coarse.shape[3]
    )
    total_span = row_devices * span_rows
    gathered = jnp.pad(gathered, ((0, 0), (0, 0), (parent_rows, parent_rows), (0, 0)))
    first = jnp.clip(parent_rows * row_rank - row_anchor, -parent_rows, total_span)
    strip = lax.dynamic_slice_in_dim(gathered, first + parent_rows, parent_rows, axis=2)

    routes = []
    for extra in (1, 0):
        for k in range(ratio):
            if extra == 1 and k == 0:
                continue
            pairs = [(j, p) for (p, j) in column_pairs(column_devices, base, ratio, k, extra)]
            routes.append((k, extra, pairs))
    back_branches = []
    for number, skipped in enumerate(((1, 1), (0, ratio - 1))):
        patterns = [
            (pairs, 0, slot) for slot, (k, extra, pairs) in enumerate(routes)
            if (k, extra) != (skipped[1], skipped[0])
        ]
        identity = (1, 8)[number]
        back_branches.append(
            lambda sent, patterns=patterns, identity=identity: tuple(
                exchange(sent, patterns, len(routes), "gy", identity)
            )
        )
    late = (offset > (ratio - 1) * span_columns - span_columns - 1).astype(jnp.int32)
    parts = lax.switch(late, back_branches, flat(strip)[None])
    joined = jnp.concatenate([part.reshape(strip.shape) for part in parts], axis=3)
    start = (ratio - 1) * span_columns - 1 - offset
    fed_back = lax.dynamic_slice_in_dim(joined, start, parent_columns, axis=3)

    relative_rows = row_rank * parent_rows + jnp.arange(parent_rows, dtype=jnp.int32) - row_anchor
    relative_columns = (
        column_rank * parent_columns + jnp.arange(parent_columns, dtype=jnp.int32) - column_anchor
    )
    rows_valid = within(relative_rows, total_span)
    columns_valid = within(relative_columns, column_devices * span_columns)
    covered = rows_valid[:, None] & columns_valid[None, :]
    parent_result = jnp.where(covered, fed_back, parent_next)
    return (parent_result, state)


def solution(mesh):
    placed = (
        P(None, None, "gx", "gy"),
        P(None, None, "gx", "gy"),
        P(None, "gx", "gy"),
        P(None, None, "gx", "gy"),
        P(None, None, "gx", "gy"),
        P(None, "gx", "gy"),
        P(),
    )
    return jax.shard_map(
        per_device,
        mesh=mesh,
        in_specs=placed,
        out_specs=(P(None, None, "gx", "gy"), P(None, None, "gx", "gy")),
        check_vma=False,
    )
```

```python
import jax
import jax.numpy as jnp
from jax import lax
from jax.experimental import pallas as pl
from jax.experimental.pallas import tpu as pltpu
from jax.sharding import PartitionSpec as P

MESH = pl.DeviceIdType.MESH

SUBSTEPS = 3


third = 1.0 / 3.0
two_thirds = 2.0 / 3.0
nudge_floor = 0.1
relax_width = 4.0


def shift_pairs(count, step):
    return [(i, i + step) for i in range(count) if 0 <= i + step < count]


def halo_kernel(rows, cols, *refs):
    sources, targets, send_sems, recv_sems = refs[:4], refs[4:8], refs[8], refs[9]
    x = lax.axis_index("gx")
    y = lax.axis_index("gy")
    routes = (("gx", x, 1, rows), ("gx", x, -1, rows), ("gy", y, 1, cols), ("gy", y, -1, cols))
    barrier = pltpu.get_barrier_semaphore()
    for axis, own, step, count in routes:
        @pl.when((own + step >= 0) & (own + step < count))
        def _():
            pl.semaphore_signal(barrier, 1, device_id={axis: own + step}, device_id_type=MESH)

    peers = (x + rows - 1) // rows + (2 * rows - 2 - x) // rows
    peers = peers + (y + cols - 1) // cols + (2 * cols - 2 - y) // cols
    pl.semaphore_wait(barrier, peers)
    copies = []
    for number, (axis, own, step, count) in enumerate(routes):
        copy = pltpu.make_async_remote_copy(
            src_ref=sources[number],
            dst_ref=targets[number],
            send_sem=send_sems.at[number],
            recv_sem=recv_sems.at[number],
            device_id={axis: own + step},
            device_id_type=MESH,
        )
        copies.append((own, step, count, copy))

        @pl.when((own + step >= 0) & (own + step < count))
        def _():
            copy.start()

    for number, (own, step, count, copy) in enumerate(copies):
        @pl.when((own + step >= 0) & (own + step < count))
        def _():
            copy.wait_send()

        @pl.when((own - step >= 0) & (own - step < count))
        def _():
            copy.wait_recv()

        @pl.when((own - step < 0) | (own - step >= count))
        def _():
            targets[number][...] = jnp.zeros(targets[number].shape, targets[number].dtype)


def edges(cells):
    fields, levels, height, width = cells.shape
    planes = fields * levels
    return (
        cells[:, :, -1, :].reshape(planes, width),
        cells[:, :, 0, :].reshape(planes, width),
        cells[:, :, :, -1].reshape(planes, height),
        cells[:, :, :, 0].reshape(planes, height),
    )


def neighbours(sources, identity):
    rows = lax.axis_size("gx")
    cols = lax.axis_size("gy")
    received = pl.pallas_call(
        lambda *refs: halo_kernel(rows, cols, *refs),
        out_shape=tuple(jax.ShapeDtypeStruct(part.shape, part.dtype) for part in sources),
        in_specs=[pl.BlockSpec(memory_space=pltpu.VMEM)] * 4,
        out_specs=tuple(pl.BlockSpec(memory_space=pltpu.VMEM) for _ in range(4)),
        scratch_shapes=[pltpu.SemaphoreType.DMA((4,)), pltpu.SemaphoreType.DMA((4,))],
        compiler_params=pltpu.CompilerParams(collective_id=identity, has_side_effects=True),
    )(*sources)
    return received


def update(values, halo, velocity, mixing):
    west_row, east_row, south_col, north_col = halo
    western = jnp.concatenate([west_row, values[:, :, :-1, :]], axis=2)
    eastern = jnp.concatenate([values[:, :, 1:, :], east_row], axis=2)
    southern = jnp.concatenate([south_col, values[:, :, :, :-1]], axis=3)
    northern = jnp.concatenate([values[:, :, :, 1:], north_col], axis=3)
    along_rows = velocity[0]
    along_columns = velocity[1]
    upwind = (
        jnp.maximum(along_rows, 0.0) * (values - western)
        + jnp.minimum(along_rows, 0.0) * (eastern - values)
        + jnp.maximum(along_columns, 0.0) * (values - southern)
        + jnp.minimum(along_columns, 0.0) * (northern - values)
    )
    return values - upwind + mixing * (eastern + western + northern + southern - 4.0 * values)


def refine_rows(block):
    lower = block[:, :, :-2]
    centre = block[:, :, 1:-1]
    upper = block[:, :, 2:]
    stacked = jnp.stack(
        (third * lower + two_thirds * centre, centre, two_thirds * centre + third * upper), axis=3
    )
    extent = centre.shape
    return stacked.reshape(extent[0], extent[1], 3 * extent[2], extent[3])


def refine_columns(block):
    lower = block[:, :, :, :-2]
    centre = block[:, :, :, 1:-1]
    upper = block[:, :, :, 2:]
    stacked = jnp.stack(
        (third * lower + two_thirds * centre, centre, two_thirds * centre + third * upper), axis=4
    )
    extent = centre.shape
    return stacked.reshape(extent[0], extent[1], extent[2], 3 * extent[3])


def refining(count):
    fine = jnp.arange(3 * count, dtype=jnp.int32)[:, None]
    coarse = jnp.arange(count + 2, dtype=jnp.int32)[None, :]
    centre = fine // 3 + 1
    phase = fine % 3
    lower = jnp.where(phase == 0, third, jnp.where(phase == 2, 0.0, 0.0))
    upper = jnp.where(phase == 2, third, 0.0)
    middle = jnp.where(phase == 1, 1.0, two_thirds)
    return (
        jnp.where(coarse == centre, middle, 0.0)
        + jnp.where(coarse == centre - 1, lower, 0.0)
        + jnp.where(coarse == centre + 1, upper, 0.0)
    ).astype(jnp.float32)


def refine(block):
    exact = lax.Precision.HIGHEST
    rows = block.shape[2] - 2
    cols = block.shape[3] - 2
    down = jnp.einsum("ar,flrc->flac", refining(rows), block, precision=exact)
    return jnp.einsum("flac,bc->flab", down, refining(cols), precision=exact)


def grouping(count):
    rows = jnp.arange(count, dtype=jnp.int32)[:, None] // 3
    return (rows == jnp.arange(count // 3, dtype=jnp.int32)[None, :]).astype(jnp.float32)


def block_mean(state):
    extent = state.shape
    exact = lax.Precision.HIGHEST
    across = jnp.einsum("flrc,cb->flrb", state, grouping(extent[3]), precision=exact)
    down = jnp.einsum("ra,flrb->flab", grouping(extent[2]), across, precision=exact)
    return down / 9.0


def relax_weight(row_global, column_global, total_rows, total_columns):
    row_distance = jnp.minimum(row_global, total_rows - 1 - row_global)
    column_distance = jnp.minimum(column_global, total_columns - 1 - column_global)
    distance = jnp.minimum(row_distance[:, None], column_distance[None, :]).astype(jnp.float32)
    return nudge_floor + (1.0 - nudge_floor) * jnp.exp(-distance / relax_width)


def within(positions, limit):
    return (positions >= 0) & (positions < limit)


def column_pairs(count, base, ratio, k, extra):
    pairs = []
    for m in range(count):
        j = ratio * m + k
        p = base + m + extra
        if j < count and p < count:
            pairs.append((p, j))
    return pairs


def exchange_kernel(axis, patterns, local, count, *refs):
    sends = refs[:count]
    recv_ref, send_sems, recv_sems = refs[count:]
    me = lax.axis_index(axis)
    receivers = {}
    for pairs, _, slot in patterns:
        for a, b in pairs:
            receivers.setdefault(slot, set()).add(b)
    for a, source, slot in local:
        receivers.setdefault(slot, set()).add(a)
    for slot in range(recv_ref.shape[0]):
        idle = None
        for device in sorted(receivers.get(slot, ())):
            test = me != device
            idle = test if idle is None else idle & test
        if idle is None:
            recv_ref[slot] = jnp.zeros(recv_ref.shape[1:], recv_ref.dtype)
            continue

        @pl.when(idle)
        def _():
            recv_ref[slot] = jnp.zeros(recv_ref.shape[1:], recv_ref.dtype)

    for a, source, slot in local:
        @pl.when(me == a)
        def _():
            recv_ref[slot] = sends[source][...]

    barrier = pltpu.get_barrier_semaphore()
    links = [pair for pairs, _, _ in patterns for pair in pairs]
    for a, b in links:
        @pl.when(me == a)
        def _():
            pl.semaphore_signal(barrier, 1, device_id={axis: b}, device_id_type=MESH)

        @pl.when(me == b)
        def _():
            pl.semaphore_signal(barrier, 1, device_id={axis: a}, device_id_type=MESH)

    peers = {}
    for a, b in links:
        peers[a] = peers.get(a, 0) + 1
        peers[b] = peers.get(b, 0) + 1
    for device, count in sorted(peers.items()):
        @pl.when(me == device)
        def _():
            pl.semaphore_wait(barrier, count)

    copies = []
    for number, (pairs, source, slot) in enumerate(patterns):
        for a, b in pairs:
            copy = pltpu.make_async_remote_copy(
                src_ref=sends[source],
                dst_ref=recv_ref.at[slot],
                send_sem=send_sems.at[number],
                recv_sem=recv_sems.at[slot],
                device_id={axis: b},
                device_id_type=MESH,
            )
            copies.append((a, b, copy))

            @pl.when(me == a)
            def _():
                copy.start()

    for a, b, copy in copies:
        @pl.when(me == a)
        def _():
            copy.wait_send()

        @pl.when(me == b)
        def _():
            copy.wait_recv()


def exchange(pieces, patterns, slots, axis, identity):
    remote = [([(a, b) for a, b in pairs if a != b], source, slot) for pairs, source, slot in patterns]
    remote = [entry for entry in remote if entry[0]]
    local = [(a, source, slot) for pairs, source, slot in patterns for a, b in pairs if a == b]
    shape = pieces[0].shape
    received = pl.pallas_call(
        lambda *refs: exchange_kernel(axis, remote, local, len(pieces), *refs),
        out_shape=jax.ShapeDtypeStruct((slots,) + shape, pieces[0].dtype),
        in_specs=[pl.BlockSpec(memory_space=pltpu.VMEM)] * len(pieces),
        out_specs=pl.BlockSpec(memory_space=pltpu.VMEM),
        scratch_shapes=[
            pltpu.SemaphoreType.DMA((len(remote),)),
            pltpu.SemaphoreType.DMA((slots,)),
        ],
        compiler_params=pltpu.CompilerParams(collective_id=identity, has_side_effects=True),
    )(*pieces)
    return [received[slot] for slot in range(slots)]


def gather_kernel(axis, count, source, target, send_sems, recv_sems):
    me = lax.axis_index(axis)
    barrier = pltpu.get_barrier_semaphore()
    for delta in range(1, count):
        pl.semaphore_signal(
            barrier, 1, device_id={axis: (me + delta) % count}, device_id_type=MESH
        )
    pl.semaphore_wait(barrier, count - 1)
    outgoing = []
    for delta in range(1, count):
        copy = pltpu.make_async_remote_copy(
            src_ref=source,
            dst_ref=target.at[me],
            send_sem=send_sems.at[delta - 1],
            recv_sem=recv_sems.at[delta - 1],
            device_id={axis: (me + delta) % count},
            device_id_type=MESH,
        )
        copy.start()
        outgoing.append(copy)
    target[me] = source[...]
    for delta, copy in zip(range(1, count), outgoing):
        copy.wait_send()
        incoming = pltpu.make_async_remote_copy(
            src_ref=source,
            dst_ref=target.at[(me + count - delta) % count],
            send_sem=send_sems.at[delta - 1],
            recv_sem=recv_sems.at[delta - 1],
            device_id={axis: (me + count - delta) % count},
            device_id_type=MESH,
        )
        incoming.wait_recv()


def gather(block, axis, identity):
    count = lax.axis_size(axis)
    return pl.pallas_call(
        lambda *refs: gather_kernel(axis, count, *refs),
        out_shape=jax.ShapeDtypeStruct((count,) + block.shape, block.dtype),
        in_specs=[pl.BlockSpec(memory_space=pltpu.VMEM)],
        out_specs=pl.BlockSpec(memory_space=pltpu.VMEM),
        scratch_shapes=[
            pltpu.SemaphoreType.DMA((count - 1,)),
            pltpu.SemaphoreType.DMA((count - 1,)),
        ],
        compiler_params=pltpu.CompilerParams(collective_id=identity, has_side_effects=True),
    )(block)


def stencil_kernel(relaxed, *refs):
    if relaxed:
        (values, velocity, mixing, western, eastern, southern, northern, forcing, weight) = refs[:9]
        out, last_row, first_row, last_col, first_col = refs[9:]
    else:
        (values, velocity, mixing, western, eastern, southern, northern, out) = refs
    levels, height, width = values.shape[1:]
    row = lax.broadcasted_iota(jnp.int32, (height, width), 0)
    col = lax.broadcasted_iota(jnp.int32, (height, width), 1)
    eye = (
        lax.broadcasted_iota(jnp.int32, (height, height), 0)
        == lax.broadcasted_iota(jnp.int32, (height, height), 1)
    ).astype(jnp.float32)
    first = pl.multiple_of(pl.program_id(0) * levels, levels)
    numbers = (((1,), (1,)), ((), ()))
    exact = lax.Precision.HIGHEST
    south_cols = lax.dot_general(
        eye, southern[pl.ds(first, levels), :], numbers, precision=exact,
        preferred_element_type=jnp.float32,
    )
    north_cols = lax.dot_general(
        eye, northern[pl.ds(first, levels), :], numbers, precision=exact,
        preferred_element_type=jnp.float32,
    )
    picks = lax.broadcasted_iota(jnp.int32, (8, width), 1)
    chosen = lax.broadcasted_iota(jnp.int32, (8, width), 0)
    ends = ((chosen == 0) & (picks == 0)) | ((chosen == 1) & (picks == width - 1))
    ends = ends.astype(jnp.float32)
    for level in range(levels):
        q = values[0, level]
        west_row = western[pl.ds(first + level, 1), :]
        east_row = eastern[pl.ds(first + level, 1), :]
        west = jnp.where(row == 0, west_row, pltpu.roll(q, 1, 0))
        east = jnp.where(row == height - 1, east_row, pltpu.roll(q, height - 1, 0))
        south = jnp.where(col == 0, south_cols[:, level:level + 1], pltpu.roll(q, 1, 1))
        north = jnp.where(
            col == width - 1, north_cols[:, level:level + 1], pltpu.roll(q, width - 1, 1)
        )
        along_rows = velocity[0, level]
        along_columns = velocity[1, level]
        upwind = (
            jnp.maximum(along_rows, 0.0) * (q - west)
            + jnp.minimum(along_rows, 0.0) * (east - q)
            + jnp.maximum(along_columns, 0.0) * (q - south)
            + jnp.minimum(along_columns, 0.0) * (north - q)
        )
        moved = q - upwind + mixing[level] * (east + west + north + south - 4.0 * q)
        if relaxed:
            moved = moved + weight[...] * (forcing[0, level] - moved)
            last_row[pl.ds(first + level, 1), :] = moved[height - 1:height, :]
            first_row[pl.ds(first + level, 1), :] = moved[0:1, :]
            sides = lax.dot_general(
                ends, moved, numbers, precision=exact, preferred_element_type=jnp.float32
            )
            first_col[pl.ds(first + level, 1), :] = sides[0:1, :]
            last_col[pl.ds(first + level, 1), :] = sides[1:2, :]
        out[0, level] = moved


def stencil(values, halo, velocity, mixing, forcing=None, weight=None):
    fields, levels, height, width = values.shape
    west_row, east_row, south_col, north_col = halo
    plane = pl.BlockSpec((1, levels, height, width), lambda f: (f, 0, 0, 0))
    edge_row = pl.BlockSpec((fields * levels, width), lambda f: (0, 0))
    edge_col = pl.BlockSpec((fields * levels, height), lambda f: (0, 0))
    operands = [values, velocity, mixing, west_row, east_row, south_col, north_col]
    specs = [
        plane,
        pl.BlockSpec(velocity.shape, lambda f: (0, 0, 0, 0)),
        pl.BlockSpec(mixing.shape, lambda f: (0, 0, 0)),
        edge_row,
        edge_row,
        edge_col,
        edge_col,
    ]
    relaxed = forcing is not None
    out_shape = jax.ShapeDtypeStruct(values.shape, values.dtype)
    out_specs = plane
    if relaxed:
        operands += [forcing, weight]
        specs += [plane, pl.BlockSpec(weight.shape, lambda f: (0, 0))]
        rows_shape = jax.ShapeDtypeStruct((fields * levels, width), values.dtype)
        cols_shape = jax.ShapeDtypeStruct((fields * levels, height), values.dtype)
        out_shape = (out_shape, rows_shape, rows_shape, cols_shape, cols_shape)
        out_specs = (plane, edge_row, edge_row, edge_col, edge_col)
    return pl.pallas_call(
        lambda *refs: stencil_kernel(relaxed, *refs),
        out_shape=out_shape,
        grid=(fields,),
        in_specs=specs,
        out_specs=out_specs,
    )(*operands)


def flat(block):
    size = block.size
    return block.reshape(size // 128, 128) if size % 128 == 0 else block.reshape(-1, block.shape[-1])


def per_device(
    parent_fields,
    parent_velocity,
    parent_mixing,
    nest_fields,
    nest_velocity,
    nest_mixing,
    nest_anchor,
):
    row_rank = lax.axis_index("gx")
    column_rank = lax.axis_index("gy")
    row_devices = lax.axis_size("gx")
    column_devices = lax.axis_size("gy")
    parent_rows = parent_fields.shape[2]
    parent_columns = parent_fields.shape[3]
    nest_rows = nest_fields.shape[2]
    nest_columns = nest_fields.shape[3]
    span_rows = nest_rows // 3
    span_columns = nest_columns // 3
    ratio = parent_columns // span_columns
    base = column_devices // 2
    base_column = base * parent_columns
    relay_rows = span_rows + 2
    relay_columns = span_columns + 2
    row_anchor = nest_anchor[0]
    column_anchor = nest_anchor[1]
    offset = column_anchor - 1 - base_column

    parent_next = stencil(
        parent_fields, neighbours(edges(parent_fields), 2), parent_velocity, parent_mixing
    )

    margin = parent_columns - span_columns
    wide = jnp.pad(parent_next, ((0, 0), (0, 0), (0, 0), (margin, margin)))
    straddle = (ratio - 1) * span_columns - 2
    regimes = (
        lambda k, extra: not (extra == 1 and k == ratio - 2),
        lambda k, extra: True,
        lambda k, extra: not (extra == 0 and k == ratio - 1),
    )
    regime = (offset > straddle - span_columns).astype(jnp.int32) + (
        offset > straddle - span_columns + 1
    ).astype(jnp.int32)
    pieces = []
    routes = []
    for extra in (0, 1):
        for k in range(ratio):
            if extra == 1 and k == 0:
                continue
            start = margin + span_columns * k + offset - extra * parent_columns
            piece = lax.dynamic_slice_in_dim(wide, start, relay_columns, axis=3)
            routes.append((k, extra, len(pieces)))
            pieces.append(flat(piece))
    stacked_pieces = tuple(pieces)
    branches = []
    for number, active in enumerate(regimes):
        patterns = [
            (column_pairs(column_devices, base, ratio, k, extra), index, extra)
            for k, extra, index in routes
            if active(k, extra)
        ]
        identity = (0, 6, 7)[number]
        branches.append(
            lambda stacked, patterns=patterns, identity=identity: tuple(
                exchange(stacked, patterns, 2, "gy", identity)
            )
        )
    within_part, beyond_part = lax.switch(regime, branches, stacked_pieces)
    piece_shape = parent_next.shape[:3] + (relay_columns,)
    relay_cols = within_part.reshape(piece_shape) + beyond_part.reshape(piece_shape)

    padded = jnp.pad(relay_cols, ((0, 0), (0, 0), (relay_rows, relay_rows), (0, 0)))
    targets = jnp.arange(row_devices, dtype=jnp.int32)[:, None]
    first = row_anchor - 1 + span_rows * targets - parent_rows * row_rank
    first = jnp.clip(first, -relay_rows, parent_rows) + relay_rows
    picks = first + jnp.arange(relay_rows, dtype=jnp.int32)[None, :]
    stacked = jnp.take(padded, picks, axis=2)
    received = lax.all_to_all(stacked, "gx", split_axis=2, concat_axis=2, tiled=True)
    relay = jnp.sum(received, axis=2)

    forcing = refine(relay)
    row_global = row_rank * nest_rows + jnp.arange(nest_rows, dtype=jnp.int32)
    column_global = column_rank * nest_columns + jnp.arange(nest_columns, dtype=jnp.int32)
    weight = relax_weight(
        row_global, column_global, row_devices * nest_rows, column_devices * nest_columns
    )
    state = nest_fields
    sides = edges(state)
    for substep in range(SUBSTEPS):
        state, *sides = stencil(
            state, neighbours(sides, 3 + substep), nest_velocity, nest_mixing, forcing, weight
        )

    coarse = block_mean(state)
    fields_count, levels_count = coarse.shape[:2]
    collected = gather(coarse.reshape((-1,) + coarse.shape[2:]), "gx", 9)
    gathered = jnp.moveaxis(collected, 0, 1).reshape(
        fields_count, levels_count, row_devices * span_rows, coarse.shape[3]
    )
    total_span = row_devices * span_rows
    gathered = jnp.pad(gathered, ((0, 0), (0, 0), (parent_rows, parent_rows), (0, 0)))
    first = jnp.clip(parent_rows * row_rank - row_anchor, -parent_rows, total_span)
    strip = lax.dynamic_slice_in_dim(gathered, first + parent_rows, parent_rows, axis=2)

    routes = []
    for extra in (1, 0):
        for k in range(ratio):
            if extra == 1 and k == 0:
                continue
            pairs = [(j, p) for (p, j) in column_pairs(column_devices, base, ratio, k, extra)]
            routes.append((k, extra, pairs))
    back_branches = []
    for number, skipped in enumerate(((1, 1), (0, ratio - 1))):
        patterns = [
            (pairs, 0, slot) for slot, (k, extra, pairs) in enumerate(routes)
            if (k, extra) != (skipped[1], skipped[0])
        ]
        identity = (1, 8)[number]
        back_branches.append(
            lambda sent, patterns=patterns, identity=identity: tuple(
                exchange(sent, patterns, len(routes), "gy", identity)
            )
        )
    late = (offset > (ratio - 1) * span_columns - span_columns - 1).astype(jnp.int32)
    parts = lax.switch(late, back_branches, (flat(strip),))
    joined = jnp.concatenate([part.reshape(strip.shape) for part in parts], axis=3)
    start = (ratio - 1) * span_columns - 1 - offset
    fed_back = lax.dynamic_slice_in_dim(joined, start, parent_columns, axis=3)

    relative_rows = row_rank * parent_rows + jnp.arange(parent_rows, dtype=jnp.int32) - row_anchor
    relative_columns = (
        column_rank * parent_columns + jnp.arange(parent_columns, dtype=jnp.int32) - column_anchor
    )
    rows_valid = within(relative_rows, total_span)
    columns_valid = within(relative_columns, column_devices * span_columns)
    covered = rows_valid[:, None] & columns_valid[None, :]
    parent_result = jnp.where(covered, fed_back, parent_next)
    return (parent_result, state)


def solution(mesh):
    placed = (
        P(None, None, "gx", "gy"),
        P(None, None, "gx", "gy"),
        P(None, "gx", "gy"),
        P(None, None, "gx", "gy"),
        P(None, None, "gx", "gy"),
        P(None, "gx", "gy"),
        P(),
    )
    return jax.shard_map(
        per_device,
        mesh=mesh,
        in_specs=placed,
        out_specs=(P(None, None, "gx", "gy"), P(None, None, "gx", "gy")),
        check_vma=False,
    )
```

```python
import jax
import jax.numpy as jnp
from jax import lax
from jax.experimental import pallas as pl
from jax.experimental.pallas import tpu as pltpu
from jax.sharding import PartitionSpec as P

MESH = pl.DeviceIdType.MESH

SUBSTEPS = 3


third = 1.0 / 3.0
two_thirds = 2.0 / 3.0
nudge_floor = 0.1
relax_width = 4.0


def shift_pairs(count, step):
    return [(i, i + step) for i in range(count) if 0 <= i + step < count]


def halo_kernel(rows, cols, *refs):
    sources, targets, send_sems, recv_sems = refs[:4], refs[4:8], refs[8], refs[9]
    x = lax.axis_index("gx")
    y = lax.axis_index("gy")
    routes = (("gx", x, 1, rows), ("gx", x, -1, rows), ("gy", y, 1, cols), ("gy", y, -1, cols))
    barrier = pltpu.get_barrier_semaphore()
    for axis, own, step, count in routes:
        @pl.when((own + step >= 0) & (own + step < count))
        def _():
            pl.semaphore_signal(barrier, 1, device_id={axis: own + step}, device_id_type=MESH)

    peers = (x + rows - 1) // rows + (2 * rows - 2 - x) // rows
    peers = peers + (y + cols - 1) // cols + (2 * cols - 2 - y) // cols
    pl.semaphore_wait(barrier, peers)
    copies = []
    for number, (axis, own, step, count) in enumerate(routes):
        copy = pltpu.make_async_remote_copy(
            src_ref=sources[number],
            dst_ref=targets[number],
            send_sem=send_sems.at[number],
            recv_sem=recv_sems.at[number],
            device_id={axis: own + step},
            device_id_type=MESH,
        )
        copies.append((own, step, count, copy))

        @pl.when((own + step >= 0) & (own + step < count))
        def _():
            copy.start()

    for number, (own, step, count, copy) in enumerate(copies):
        @pl.when((own + step >= 0) & (own + step < count))
        def _():
            copy.wait_send()

        @pl.when((own - step >= 0) & (own - step < count))
        def _():
            copy.wait_recv()

        @pl.when((own - step < 0) | (own - step >= count))
        def _():
            targets[number][...] = jnp.zeros(targets[number].shape, targets[number].dtype)


def edges(cells):
    fields, levels, height, width = cells.shape
    planes = fields * levels
    return (
        cells[:, :, -1, :].reshape(planes, width),
        cells[:, :, 0, :].reshape(planes, width),
        cells[:, :, :, -1].reshape(planes, height),
        cells[:, :, :, 0].reshape(planes, height),
    )


def neighbours(sources, identity):
    rows = lax.axis_size("gx")
    cols = lax.axis_size("gy")
    received = pl.pallas_call(
        lambda *refs: halo_kernel(rows, cols, *refs),
        out_shape=tuple(jax.ShapeDtypeStruct(part.shape, part.dtype) for part in sources),
        in_specs=[pl.BlockSpec(memory_space=pltpu.VMEM)] * 4,
        out_specs=tuple(pl.BlockSpec(memory_space=pltpu.VMEM) for _ in range(4)),
        scratch_shapes=[pltpu.SemaphoreType.DMA((4,)), pltpu.SemaphoreType.DMA((4,))],
        compiler_params=pltpu.CompilerParams(collective_id=identity, has_side_effects=True),
    )(*sources)
    return received


def update(values, halo, velocity, mixing):
    west_row, east_row, south_col, north_col = halo
    western = jnp.concatenate([west_row, values[:, :, :-1, :]], axis=2)
    eastern = jnp.concatenate([values[:, :, 1:, :], east_row], axis=2)
    southern = jnp.concatenate([south_col, values[:, :, :, :-1]], axis=3)
    northern = jnp.concatenate([values[:, :, :, 1:], north_col], axis=3)
    along_rows = velocity[0]
    along_columns = velocity[1]
    upwind = (
        jnp.maximum(along_rows, 0.0) * (values - western)
        + jnp.minimum(along_rows, 0.0) * (eastern - values)
        + jnp.maximum(along_columns, 0.0) * (values - southern)
        + jnp.minimum(along_columns, 0.0) * (northern - values)
    )
    return values - upwind + mixing * (eastern + western + northern + southern - 4.0 * values)


def refine_rows(block):
    lower = block[:, :, :-2]
    centre = block[:, :, 1:-1]
    upper = block[:, :, 2:]
    stacked = jnp.stack(
        (third * lower + two_thirds * centre, centre, two_thirds * centre + third * upper), axis=3
    )
    extent = centre.shape
    return stacked.reshape(extent[0], extent[1], 3 * extent[2], extent[3])


def refine_columns(block):
    lower = block[:, :, :, :-2]
    centre = block[:, :, :, 1:-1]
    upper = block[:, :, :, 2:]
    stacked = jnp.stack(
        (third * lower + two_thirds * centre, centre, two_thirds * centre + third * upper), axis=4
    )
    extent = centre.shape
    return stacked.reshape(extent[0], extent[1], extent[2], 3 * extent[3])


def refining(count):
    fine = jnp.arange(3 * count, dtype=jnp.int32)[:, None]
    coarse = jnp.arange(count + 2, dtype=jnp.int32)[None, :]
    centre = fine // 3 + 1
    phase = fine % 3
    lower = jnp.where(phase == 0, third, jnp.where(phase == 2, 0.0, 0.0))
    upper = jnp.where(phase == 2, third, 0.0)
    middle = jnp.where(phase == 1, 1.0, two_thirds)
    return (
        jnp.where(coarse == centre, middle, 0.0)
        + jnp.where(coarse == centre - 1, lower, 0.0)
        + jnp.where(coarse == centre + 1, upper, 0.0)
    ).astype(jnp.float32)


def refine(block):
    exact = lax.Precision.HIGHEST
    rows = block.shape[2] - 2
    cols = block.shape[3] - 2
    down = jnp.einsum("ar,flrc->flac", refining(rows), block, precision=exact)
    return jnp.einsum("flac,bc->flab", down, refining(cols), precision=exact)


def grouping(count):
    rows = jnp.arange(count, dtype=jnp.int32)[:, None] // 3
    return (rows == jnp.arange(count // 3, dtype=jnp.int32)[None, :]).astype(jnp.float32)


def block_mean(state):
    extent = state.shape
    exact = lax.Precision.HIGHEST
    across = jnp.einsum("flrc,cb->flrb", state, grouping(extent[3]), precision=exact)
    down = jnp.einsum("ra,flrb->flab", grouping(extent[2]), across, precision=exact)
    return down / 9.0


def relax_weight(row_global, column_global, total_rows, total_columns):
    row_distance = jnp.minimum(row_global, total_rows - 1 - row_global)
    column_distance = jnp.minimum(column_global, total_columns - 1 - column_global)
    distance = jnp.minimum(row_distance[:, None], column_distance[None, :]).astype(jnp.float32)
    return nudge_floor + (1.0 - nudge_floor) * jnp.exp(-distance / relax_width)


def within(positions, limit):
    return (positions >= 0) & (positions < limit)


def column_pairs(count, base, ratio, k, extra):
    pairs = []
    for m in range(count):
        j = ratio * m + k
        p = base + m + extra
        if j < count and p < count:
            pairs.append((p, j))
    return pairs


def exchange_kernel(axis, patterns, local, send_ref, recv_ref, send_sems, recv_sems):
    me = lax.axis_index(axis)
    receivers = {}
    for pairs, _, slot in patterns:
        for a, b in pairs:
            receivers.setdefault(slot, set()).add(b)
    for a, source, slot in local:
        receivers.setdefault(slot, set()).add(a)
    for slot in range(recv_ref.shape[0]):
        idle = None
        for device in sorted(receivers.get(slot, ())):
            test = me != device
            idle = test if idle is None else idle & test
        if idle is None:
            recv_ref[slot] = jnp.zeros(recv_ref.shape[1:], recv_ref.dtype)
            continue

        @pl.when(idle)
        def _():
            recv_ref[slot] = jnp.zeros(recv_ref.shape[1:], recv_ref.dtype)

    for a, source, slot in local:
        @pl.when(me == a)
        def _():
            recv_ref[slot] = send_ref[source]

    barrier = pltpu.get_barrier_semaphore()
    links = [pair for pairs, _, _ in patterns for pair in pairs]
    for a, b in links:
        @pl.when(me == a)
        def _():
            pl.semaphore_signal(barrier, 1, device_id={axis: b}, device_id_type=MESH)

        @pl.when(me == b)
        def _():
            pl.semaphore_signal(barrier, 1, device_id={axis: a}, device_id_type=MESH)

    peers = {}
    for a, b in links:
        peers[a] = peers.get(a, 0) + 1
        peers[b] = peers.get(b, 0) + 1
    for device, count in sorted(peers.items()):
        @pl.when(me == device)
        def _():
            pl.semaphore_wait(barrier, count)

    copies = []
    for number, (pairs, source, slot) in enumerate(patterns):
        for a, b in pairs:
            copy = pltpu.make_async_remote_copy(
                src_ref=send_ref.at[source],
                dst_ref=recv_ref.at[slot],
                send_sem=send_sems.at[number],
                recv_sem=recv_sems.at[slot],
                device_id={axis: b},
                device_id_type=MESH,
            )
            copies.append((a, b, copy))

            @pl.when(me == a)
            def _():
                copy.start()

    for a, b, copy in copies:
        @pl.when(me == a)
        def _():
            copy.wait_send()

        @pl.when(me == b)
        def _():
            copy.wait_recv()


def exchange(pieces, patterns, slots, axis, identity):
    remote = [([(a, b) for a, b in pairs if a != b], source, slot) for pairs, source, slot in patterns]
    remote = [entry for entry in remote if entry[0]]
    local = [(a, source, slot) for pairs, source, slot in patterns for a, b in pairs if a == b]
    shape = pieces.shape[1:]
    received = pl.pallas_call(
        lambda *refs: exchange_kernel(axis, remote, local, *refs),
        out_shape=jax.ShapeDtypeStruct((slots,) + shape, pieces.dtype),
        in_specs=[pl.BlockSpec(memory_space=pltpu.VMEM)],
        out_specs=pl.BlockSpec(memory_space=pltpu.VMEM),
        scratch_shapes=[
            pltpu.SemaphoreType.DMA((len(remote),)),
            pltpu.SemaphoreType.DMA((slots,)),
        ],
        compiler_params=pltpu.CompilerParams(collective_id=identity, has_side_effects=True),
    )(pieces)
    return [received[slot] for slot in range(slots)]


def gather_kernel(axis, count, source, target, send_sems, recv_sems):
    me = lax.axis_index(axis)
    barrier = pltpu.get_barrier_semaphore()
    for delta in range(1, count):
        pl.semaphore_signal(
            barrier, 1, device_id={axis: (me + delta) % count}, device_id_type=MESH
        )
    pl.semaphore_wait(barrier, count - 1)
    outgoing = []
    for delta in range(1, count):
        copy = pltpu.make_async_remote_copy(
            src_ref=source,
            dst_ref=target.at[me],
            send_sem=send_sems.at[delta - 1],
            recv_sem=recv_sems.at[delta - 1],
            device_id={axis: (me + delta) % count},
            device_id_type=MESH,
        )
        copy.start()
        outgoing.append(copy)
    target[me] = source[...]
    for delta, copy in zip(range(1, count), outgoing):
        copy.wait_send()
        incoming = pltpu.make_async_remote_copy(
            src_ref=source,
            dst_ref=target.at[(me + count - delta) % count],
            send_sem=send_sems.at[delta - 1],
            recv_sem=recv_sems.at[delta - 1],
            device_id={axis: (me + count - delta) % count},
            device_id_type=MESH,
        )
        incoming.wait_recv()


def gather(block, axis, identity):
    count = lax.axis_size(axis)
    return pl.pallas_call(
        lambda *refs: gather_kernel(axis, count, *refs),
        out_shape=jax.ShapeDtypeStruct((count,) + block.shape, block.dtype),
        in_specs=[pl.BlockSpec(memory_space=pltpu.VMEM)],
        out_specs=pl.BlockSpec(memory_space=pltpu.VMEM),
        scratch_shapes=[
            pltpu.SemaphoreType.DMA((count - 1,)),
            pltpu.SemaphoreType.DMA((count - 1,)),
        ],
        compiler_params=pltpu.CompilerParams(collective_id=identity, has_side_effects=True),
    )(block)


def stencil_kernel(relaxed, margin, *refs):
    if relaxed:
        (values, velocity, mixing, western, eastern, southern, northern, forcing, weight) = refs[:9]
        out, last_row, first_row, last_col, first_col = refs[9:]
    else:
        (values, velocity, mixing, western, eastern, southern, northern, out) = refs
    levels, height, width = values.shape[1:]
    row = lax.broadcasted_iota(jnp.int32, (height, width), 0)
    col = lax.broadcasted_iota(jnp.int32, (height, width), 1)
    eye = (
        lax.broadcasted_iota(jnp.int32, (height, height), 0)
        == lax.broadcasted_iota(jnp.int32, (height, height), 1)
    ).astype(jnp.float32)
    first = pl.multiple_of(pl.program_id(0) * levels, levels)
    numbers = (((1,), (1,)), ((), ()))
    exact = lax.Precision.HIGHEST
    south_cols = lax.dot_general(
        eye, southern[pl.ds(first, levels), :], numbers, precision=exact,
        preferred_element_type=jnp.float32,
    )
    north_cols = lax.dot_general(
        eye, northern[pl.ds(first, levels), :], numbers, precision=exact,
        preferred_element_type=jnp.float32,
    )
    picks = lax.broadcasted_iota(jnp.int32, (8, width), 1)
    chosen = lax.broadcasted_iota(jnp.int32, (8, width), 0)
    ends = ((chosen == 0) & (picks == 0)) | ((chosen == 1) & (picks == width - 1))
    ends = ends.astype(jnp.float32)
    for level in range(levels):
        q = values[0, level]
        west_row = western[pl.ds(first + level, 1), :]
        east_row = eastern[pl.ds(first + level, 1), :]
        west = jnp.where(row == 0, west_row, pltpu.roll(q, 1, 0))
        east = jnp.where(row == height - 1, east_row, pltpu.roll(q, height - 1, 0))
        south = jnp.where(col == 0, south_cols[:, level:level + 1], pltpu.roll(q, 1, 1))
        north = jnp.where(
            col == width - 1, north_cols[:, level:level + 1], pltpu.roll(q, width - 1, 1)
        )
        along_rows = velocity[0, level]
        along_columns = velocity[1, level]
        upwind = (
            jnp.maximum(along_rows, 0.0) * (q - west)
            + jnp.minimum(along_rows, 0.0) * (east - q)
            + jnp.maximum(along_columns, 0.0) * (q - south)
            + jnp.minimum(along_columns, 0.0) * (north - q)
        )
        moved = q - upwind + mixing[level] * (east + west + north + south - 4.0 * q)
        if relaxed:
            moved = moved + weight[...] * (forcing[0, level] - moved)
            last_row[pl.ds(first + level, 1), :] = moved[height - 1:height, :]
            first_row[pl.ds(first + level, 1), :] = moved[0:1, :]
            sides = lax.dot_general(
                ends, moved, numbers, precision=exact, preferred_element_type=jnp.float32
            )
            first_col[pl.ds(first + level, 1), :] = sides[0:1, :]
            last_col[pl.ds(first + level, 1), :] = sides[1:2, :]
        if margin:
            blank = jnp.zeros((height, margin), moved.dtype)
            out[0, level, :, :margin] = blank
            out[0, level, :, margin:margin + width] = moved
            out[0, level, :, margin + width:] = blank
        else:
            out[0, level] = moved


def stencil(values, halo, velocity, mixing, forcing=None, weight=None, margin=0):
    fields, levels, height, width = values.shape
    west_row, east_row, south_col, north_col = halo
    plane = pl.BlockSpec((1, levels, height, width), lambda f: (f, 0, 0, 0))
    edge_row = pl.BlockSpec((fields * levels, width), lambda f: (0, 0))
    edge_col = pl.BlockSpec((fields * levels, height), lambda f: (0, 0))
    operands = [values, velocity, mixing, west_row, east_row, south_col, north_col]
    specs = [
        plane,
        pl.BlockSpec(velocity.shape, lambda f: (0, 0, 0, 0)),
        pl.BlockSpec(mixing.shape, lambda f: (0, 0, 0)),
        edge_row,
        edge_row,
        edge_col,
        edge_col,
    ]
    relaxed = forcing is not None
    out_shape = jax.ShapeDtypeStruct(
        (fields, levels, height, width + 2 * margin), values.dtype
    )
    out_specs = pl.BlockSpec((1, levels, height, width + 2 * margin), lambda f: (f, 0, 0, 0))
    if relaxed:
        operands += [forcing, weight]
        specs += [plane, pl.BlockSpec(weight.shape, lambda f: (0, 0))]
        rows_shape = jax.ShapeDtypeStruct((fields * levels, width), values.dtype)
        cols_shape = jax.ShapeDtypeStruct((fields * levels, height), values.dtype)
        out_shape = (out_shape, rows_shape, rows_shape, cols_shape, cols_shape)
        out_specs = (plane, edge_row, edge_row, edge_col, edge_col)
    return pl.pallas_call(
        lambda *refs: stencil_kernel(relaxed, margin, *refs),
        out_shape=out_shape,
        grid=(fields,),
        in_specs=specs,
        out_specs=out_specs,
    )(*operands)


def flat(block):
    size = block.size
    return block.reshape(size // 128, 128) if size % 128 == 0 else block.reshape(-1, block.shape[-1])


def per_device(
    parent_fields,
    parent_velocity,
    parent_mixing,
    nest_fields,
    nest_velocity,
    nest_mixing,
    nest_anchor,
):
    row_rank = lax.axis_index("gx")
    column_rank = lax.axis_index("gy")
    row_devices = lax.axis_size("gx")
    column_devices = lax.axis_size("gy")
    parent_rows = parent_fields.shape[2]
    parent_columns = parent_fields.shape[3]
    nest_rows = nest_fields.shape[2]
    nest_columns = nest_fields.shape[3]
    span_rows = nest_rows // 3
    span_columns = nest_columns // 3
    ratio = parent_columns // span_columns
    base = column_devices // 2
    base_column = base * parent_columns
    relay_rows = span_rows + 2
    relay_columns = span_columns + 2
    row_anchor = nest_anchor[0]
    column_anchor = nest_anchor[1]
    offset = column_anchor - 1 - base_column

    margin = parent_columns - span_columns
    wide = stencil(
        parent_fields,
        neighbours(edges(parent_fields), 2),
        parent_velocity,
        parent_mixing,
        margin=margin,
    )
    parent_next = wide[:, :, :, margin:margin + parent_columns]
    straddle = (ratio - 1) * span_columns - 2
    regimes = (
        lambda k, extra: not (extra == 1 and k == ratio - 2),
        lambda k, extra: True,
        lambda k, extra: not (extra == 0 and k == ratio - 1),
    )
    regime = (offset > straddle - span_columns).astype(jnp.int32) + (
        offset > straddle - span_columns + 1
    ).astype(jnp.int32)
    pieces = []
    routes = []
    for extra in (0, 1):
        for k in range(ratio):
            if extra == 1 and k == 0:
                continue
            start = margin + span_columns * k + offset - extra * parent_columns
            piece = lax.dynamic_slice_in_dim(wide, start, relay_columns, axis=3)
            routes.append((k, extra, len(pieces)))
            pieces.append(flat(piece))
    stacked_pieces = jnp.stack(pieces)
    branches = []
    for number, active in enumerate(regimes):
        patterns = [
            (column_pairs(column_devices, base, ratio, k, extra), index, extra)
            for k, extra, index in routes
            if active(k, extra)
        ]
        identity = (0, 6, 7)[number]
        branches.append(
            lambda stacked, patterns=patterns, identity=identity: tuple(
                exchange(stacked, patterns, 2, "gy", identity)
            )
        )
    within_part, beyond_part = lax.switch(regime, branches, stacked_pieces)
    piece_shape = parent_next.shape[:3] + (relay_columns,)
    relay_cols = within_part.reshape(piece_shape) + beyond_part.reshape(piece_shape)

    padded = jnp.pad(relay_cols, ((0, 0), (0, 0), (relay_rows, relay_rows), (0, 0)))
    targets = jnp.arange(row_devices, dtype=jnp.int32)[:, None]
    first = row_anchor - 1 + span_rows * targets - parent_rows * row_rank
    first = jnp.clip(first, -relay_rows, parent_rows) + relay_rows
    picks = first + jnp.arange(relay_rows, dtype=jnp.int32)[None, :]
    stacked = jnp.take(padded, picks, axis=2)
    received = lax.all_to_all(stacked, "gx", split_axis=2, concat_axis=2, tiled=True)
    relay = jnp.sum(received, axis=2)

    forcing = refine(relay)
    row_global = row_rank * nest_rows + jnp.arange(nest_rows, dtype=jnp.int32)
    column_global = column_rank * nest_columns + jnp.arange(nest_columns, dtype=jnp.int32)
    weight = relax_weight(
        row_global, column_global, row_devices * nest_rows, column_devices * nest_columns
    )
    state = nest_fields
    sides = edges(state)
    for substep in range(SUBSTEPS):
        state, *sides = stencil(
            state, neighbours(sides, 3 + substep), nest_velocity, nest_mixing, forcing, weight
        )

    coarse = block_mean(state)
    fields_count, levels_count = coarse.shape[:2]
    collected = gather(coarse.reshape((-1,) + coarse.shape[2:]), "gx", 9)
    gathered = jnp.moveaxis(collected, 0, 1).reshape(
        fields_count, levels_count, row_devices * span_rows, coarse.shape[3]
    )
    total_span = row_devices * span_rows
    gathered = jnp.pad(gathered, ((0, 0), (0, 0), (parent_rows, parent_rows), (0, 0)))
    first = jnp.clip(parent_rows * row_rank - row_anchor, -parent_rows, total_span)
    strip = lax.dynamic_slice_in_dim(gathered, first + parent_rows, parent_rows, axis=2)

    routes = []
    for extra in (1, 0):
        for k in range(ratio):
            if extra == 1 and k == 0:
                continue
            pairs = [(j, p) for (p, j) in column_pairs(column_devices, base, ratio, k, extra)]
            routes.append((k, extra, pairs))
    back_branches = []
    for number, skipped in enumerate(((1, 1), (0, ratio - 1))):
        patterns = [
            (pairs, 0, slot) for slot, (k, extra, pairs) in enumerate(routes)
            if (k, extra) != (skipped[1], skipped[0])
        ]
        identity = (1, 8)[number]
        back_branches.append(
            lambda sent, patterns=patterns, identity=identity: tuple(
                exchange(sent, patterns, len(routes), "gy", identity)
            )
        )
    late = (offset > (ratio - 1) * span_columns - span_columns - 1).astype(jnp.int32)
    parts = lax.switch(late, back_branches, flat(strip)[None])
    joined = jnp.concatenate([part.reshape(strip.shape) for part in parts], axis=3)
    start = (ratio - 1) * span_columns - 1 - offset
    fed_back = lax.dynamic_slice_in_dim(joined, start, parent_columns, axis=3)

    relative_rows = row_rank * parent_rows + jnp.arange(parent_rows, dtype=jnp.int32) - row_anchor
    relative_columns = (
        column_rank * parent_columns + jnp.arange(parent_columns, dtype=jnp.int32) - column_anchor
    )
    rows_valid = within(relative_rows, total_span)
    columns_valid = within(relative_columns, column_devices * span_columns)
    covered = rows_valid[:, None] & columns_valid[None, :]
    parent_result = jnp.where(covered, fed_back, parent_next)
    return (parent_result, state)


def solution(mesh):
    placed = (
        P(None, None, "gx", "gy"),
        P(None, None, "gx", "gy"),
        P(None, "gx", "gy"),
        P(None, None, "gx", "gy"),
        P(None, None, "gx", "gy"),
        P(None, "gx", "gy"),
        P(),
    )
    return jax.shard_map(
        per_device,
        mesh=mesh,
        in_specs=placed,
        out_specs=(P(None, None, "gx", "gy"), P(None, None, "gx", "gy")),
        check_vma=False,
    )
```

```python
import jax
import jax.numpy as jnp
from jax import lax
from jax.experimental import pallas as pl
from jax.experimental.pallas import tpu as pltpu
from jax.sharding import PartitionSpec as P

MESH = pl.DeviceIdType.MESH

SUBSTEPS = 3


third = 1.0 / 3.0
two_thirds = 2.0 / 3.0
nudge_floor = 0.1
relax_width = 4.0


def shift_pairs(count, step):
    return [(i, i + step) for i in range(count) if 0 <= i + step < count]


def halo_kernel(rows, cols, *refs):
    sources, targets, send_sems, recv_sems = refs[:4], refs[4:8], refs[8], refs[9]
    x = lax.axis_index("gx")
    y = lax.axis_index("gy")
    routes = (("gx", x, 1, rows), ("gx", x, -1, rows), ("gy", y, 1, cols), ("gy", y, -1, cols))
    barrier = pltpu.get_barrier_semaphore()
    for axis, own, step, count in routes:
        @pl.when((own + step >= 0) & (own + step < count))
        def _():
            pl.semaphore_signal(barrier, 1, device_id={axis: own + step}, device_id_type=MESH)

    peers = (x + rows - 1) // rows + (2 * rows - 2 - x) // rows
    peers = peers + (y + cols - 1) // cols + (2 * cols - 2 - y) // cols
    pl.semaphore_wait(barrier, peers)
    copies = []
    for number, (axis, own, step, count) in enumerate(routes):
        copy = pltpu.make_async_remote_copy(
            src_ref=sources[number],
            dst_ref=targets[number],
            send_sem=send_sems.at[number],
            recv_sem=recv_sems.at[number],
            device_id={axis: own + step},
            device_id_type=MESH,
        )
        copies.append((own, step, count, copy))

        @pl.when((own + step >= 0) & (own + step < count))
        def _():
            copy.start()

    for number, (own, step, count, copy) in enumerate(copies):
        @pl.when((own + step >= 0) & (own + step < count))
        def _():
            copy.wait_send()

        @pl.when((own - step >= 0) & (own - step < count))
        def _():
            copy.wait_recv()

        @pl.when((own - step < 0) | (own - step >= count))
        def _():
            targets[number][...] = jnp.zeros(targets[number].shape, targets[number].dtype)


def edges(cells):
    fields, levels, height, width = cells.shape
    planes = fields * levels
    return (
        cells[:, :, -1, :].reshape(planes, width),
        cells[:, :, 0, :].reshape(planes, width),
        cells[:, :, :, -1].reshape(planes, height),
        cells[:, :, :, 0].reshape(planes, height),
    )


def neighbours(sources, identity):
    rows = lax.axis_size("gx")
    cols = lax.axis_size("gy")
    received = pl.pallas_call(
        lambda *refs: halo_kernel(rows, cols, *refs),
        out_shape=tuple(jax.ShapeDtypeStruct(part.shape, part.dtype) for part in sources),
        in_specs=[pl.BlockSpec(memory_space=pltpu.VMEM)] * 4,
        out_specs=tuple(pl.BlockSpec(memory_space=pltpu.VMEM) for _ in range(4)),
        scratch_shapes=[pltpu.SemaphoreType.DMA((4,)), pltpu.SemaphoreType.DMA((4,))],
        compiler_params=pltpu.CompilerParams(collective_id=identity, has_side_effects=True),
    )(*sources)
    return received


def update(values, halo, velocity, mixing):
    west_row, east_row, south_col, north_col = halo
    western = jnp.concatenate([west_row, values[:, :, :-1, :]], axis=2)
    eastern = jnp.concatenate([values[:, :, 1:, :], east_row], axis=2)
    southern = jnp.concatenate([south_col, values[:, :, :, :-1]], axis=3)
    northern = jnp.concatenate([values[:, :, :, 1:], north_col], axis=3)
    along_rows = velocity[0]
    along_columns = velocity[1]
    upwind = (
        jnp.maximum(along_rows, 0.0) * (values - western)
        + jnp.minimum(along_rows, 0.0) * (eastern - values)
        + jnp.maximum(along_columns, 0.0) * (values - southern)
        + jnp.minimum(along_columns, 0.0) * (northern - values)
    )
    return values - upwind + mixing * (eastern + western + northern + southern - 4.0 * values)


def refine_rows(block):
    lower = block[:, :, :-2]
    centre = block[:, :, 1:-1]
    upper = block[:, :, 2:]
    stacked = jnp.stack(
        (third * lower + two_thirds * centre, centre, two_thirds * centre + third * upper), axis=3
    )
    extent = centre.shape
    return stacked.reshape(extent[0], extent[1], 3 * extent[2], extent[3])


def refine_columns(block):
    lower = block[:, :, :, :-2]
    centre = block[:, :, :, 1:-1]
    upper = block[:, :, :, 2:]
    stacked = jnp.stack(
        (third * lower + two_thirds * centre, centre, two_thirds * centre + third * upper), axis=4
    )
    extent = centre.shape
    return stacked.reshape(extent[0], extent[1], extent[2], 3 * extent[3])


def refining(count):
    fine = jnp.arange(3 * count, dtype=jnp.int32)[:, None]
    coarse = jnp.arange(count + 2, dtype=jnp.int32)[None, :]
    centre = fine // 3 + 1
    phase = fine % 3
    lower = jnp.where(phase == 0, third, jnp.where(phase == 2, 0.0, 0.0))
    upper = jnp.where(phase == 2, third, 0.0)
    middle = jnp.where(phase == 1, 1.0, two_thirds)
    return (
        jnp.where(coarse == centre, middle, 0.0)
        + jnp.where(coarse == centre - 1, lower, 0.0)
        + jnp.where(coarse == centre + 1, upper, 0.0)
    ).astype(jnp.float32)


def refine(block):
    exact = lax.Precision.HIGHEST
    rows = block.shape[2] - 2
    cols = block.shape[3] - 2
    down = jnp.einsum("ar,flrc->flac", refining(rows), block, precision=exact)
    return jnp.einsum("flac,bc->flab", down, refining(cols), precision=exact)


def grouping(count):
    rows = jnp.arange(count, dtype=jnp.int32)[:, None] // 3
    return (rows == jnp.arange(count // 3, dtype=jnp.int32)[None, :]).astype(jnp.float32)


def block_mean(state):
    extent = state.shape
    exact = lax.Precision.HIGHEST
    across = jnp.einsum("flrc,cb->flrb", state, grouping(extent[3]), precision=exact)
    down = jnp.einsum("ra,flrb->flab", grouping(extent[2]), across, precision=exact)
    return down / 9.0


def relax_weight(row_global, column_global, total_rows, total_columns):
    row_distance = jnp.minimum(row_global, total_rows - 1 - row_global)
    column_distance = jnp.minimum(column_global, total_columns - 1 - column_global)
    distance = jnp.minimum(row_distance[:, None], column_distance[None, :]).astype(jnp.float32)
    return nudge_floor + (1.0 - nudge_floor) * jnp.exp(-distance / relax_width)


def within(positions, limit):
    return (positions >= 0) & (positions < limit)


def column_pairs(count, base, ratio, k, extra):
    pairs = []
    for m in range(count):
        j = ratio * m + k
        p = base + m + extra
        if j < count and p < count:
            pairs.append((p, j))
    return pairs


def exchange_kernel(axis, patterns, local, send_ref, recv_ref, send_sems, recv_sems):
    me = lax.axis_index(axis)
    receivers = {}
    for pairs, _, slot in patterns:
        for a, b in pairs:
            receivers.setdefault(slot, set()).add(b)
    for a, source, slot in local:
        receivers.setdefault(slot, set()).add(a)
    for slot in range(recv_ref.shape[0]):
        idle = None
        for device in sorted(receivers.get(slot, ())):
            test = me != device
            idle = test if idle is None else idle & test
        if idle is None:
            recv_ref[slot] = jnp.zeros(recv_ref.shape[1:], recv_ref.dtype)
            continue

        @pl.when(idle)
        def _():
            recv_ref[slot] = jnp.zeros(recv_ref.shape[1:], recv_ref.dtype)

    for a, source, slot in local:
        @pl.when(me == a)
        def _():
            recv_ref[slot] = send_ref[source]

    barrier = pltpu.get_barrier_semaphore()
    links = [pair for pairs, _, _ in patterns for pair in pairs]
    for a, b in links:
        @pl.when(me == a)
        def _():
            pl.semaphore_signal(barrier, 1, device_id={axis: b}, device_id_type=MESH)

        @pl.when(me == b)
        def _():
            pl.semaphore_signal(barrier, 1, device_id={axis: a}, device_id_type=MESH)

    peers = {}
    for a, b in links:
        peers[a] = peers.get(a, 0) + 1
        peers[b] = peers.get(b, 0) + 1
    for device, count in sorted(peers.items()):
        @pl.when(me == device)
        def _():
            pl.semaphore_wait(barrier, count)

    copies = []
    for number, (pairs, source, slot) in enumerate(patterns):
        for a, b in pairs:
            copy = pltpu.make_async_remote_copy(
                src_ref=send_ref.at[source],
                dst_ref=recv_ref.at[slot],
                send_sem=send_sems.at[number],
                recv_sem=recv_sems.at[slot],
                device_id={axis: b},
                device_id_type=MESH,
            )
            copies.append((a, b, copy))

            @pl.when(me == a)
            def _():
                copy.start()

    for a, b, copy in copies:
        @pl.when(me == a)
        def _():
            copy.wait_send()

        @pl.when(me == b)
        def _():
            copy.wait_recv()


def exchange(pieces, patterns, slots, axis, identity):
    remote = [([(a, b) for a, b in pairs if a != b], source, slot) for pairs, source, slot in patterns]
    remote = [entry for entry in remote if entry[0]]
    local = [(a, source, slot) for pairs, source, slot in patterns for a, b in pairs if a == b]
    shape = pieces.shape[1:]
    received = pl.pallas_call(
        lambda *refs: exchange_kernel(axis, remote, local, *refs),
        out_shape=jax.ShapeDtypeStruct((slots,) + shape, pieces.dtype),
        in_specs=[pl.BlockSpec(memory_space=pltpu.VMEM)],
        out_specs=pl.BlockSpec(memory_space=pltpu.VMEM),
        scratch_shapes=[
            pltpu.SemaphoreType.DMA((len(remote),)),
            pltpu.SemaphoreType.DMA((slots,)),
        ],
        compiler_params=pltpu.CompilerParams(collective_id=identity, has_side_effects=True),
    )(pieces)
    return [received[slot] for slot in range(slots)]


def gather_kernel(axis, count, source, target, send_sems, recv_sems):
    me = lax.axis_index(axis)
    barrier = pltpu.get_barrier_semaphore()
    for delta in range(1, count):
        pl.semaphore_signal(
            barrier, 1, device_id={axis: (me + delta) % count}, device_id_type=MESH
        )
    pl.semaphore_wait(barrier, count - 1)
    outgoing = []
    for delta in range(1, count):
        copy = pltpu.make_async_remote_copy(
            src_ref=source,
            dst_ref=target.at[me],
            send_sem=send_sems.at[delta - 1],
            recv_sem=recv_sems.at[delta - 1],
            device_id={axis: (me + delta) % count},
            device_id_type=MESH,
        )
        copy.start()
        outgoing.append(copy)
    target[me] = source[...]
    for delta, copy in zip(range(1, count), outgoing):
        copy.wait_send()
        incoming = pltpu.make_async_remote_copy(
            src_ref=source,
            dst_ref=target.at[(me + count - delta) % count],
            send_sem=send_sems.at[delta - 1],
            recv_sem=recv_sems.at[delta - 1],
            device_id={axis: (me + count - delta) % count},
            device_id_type=MESH,
        )
        incoming.wait_recv()


def gather(block, axis, identity):
    count = lax.axis_size(axis)
    return pl.pallas_call(
        lambda *refs: gather_kernel(axis, count, *refs),
        out_shape=jax.ShapeDtypeStruct((count,) + block.shape, block.dtype),
        in_specs=[pl.BlockSpec(memory_space=pltpu.VMEM)],
        out_specs=pl.BlockSpec(memory_space=pltpu.VMEM),
        scratch_shapes=[
            pltpu.SemaphoreType.DMA((count - 1,)),
            pltpu.SemaphoreType.DMA((count - 1,)),
        ],
        compiler_params=pltpu.CompilerParams(collective_id=identity, has_side_effects=True),
    )(block)


def stencil_kernel(relaxed, *refs):
    if relaxed:
        (values, velocity, mixing, western, eastern, southern, northern, forcing, weight) = refs[:9]
        out, last_row, first_row, last_col, first_col = refs[9:]
    else:
        (values, velocity, mixing, western, eastern, southern, northern, out) = refs
    levels, height, width = values.shape[1:]
    row = lax.broadcasted_iota(jnp.int32, (height, width), 0)
    col = lax.broadcasted_iota(jnp.int32, (height, width), 1)
    eye = (
        lax.broadcasted_iota(jnp.int32, (height, height), 0)
        == lax.broadcasted_iota(jnp.int32, (height, height), 1)
    ).astype(jnp.float32)
    first = pl.multiple_of(pl.program_id(0) * levels, levels)
    numbers = (((1,), (1,)), ((), ()))
    exact = lax.Precision.HIGHEST
    south_cols = lax.dot_general(
        eye, southern[pl.ds(first, levels), :], numbers, precision=exact,
        preferred_element_type=jnp.float32,
    )
    north_cols = lax.dot_general(
        eye, northern[pl.ds(first, levels), :], numbers, precision=exact,
        preferred_element_type=jnp.float32,
    )
    picks = lax.broadcasted_iota(jnp.int32, (8, width), 1)
    chosen = lax.broadcasted_iota(jnp.int32, (8, width), 0)
    ends = ((chosen == 0) & (picks == 0)) | ((chosen == 1) & (picks == width - 1))
    ends = ends.astype(jnp.float32)
    for level in range(levels):
        q = values[0, level]
        west_row = western[pl.ds(first + level, 1), :]
        east_row = eastern[pl.ds(first + level, 1), :]
        west = jnp.where(row == 0, west_row, pltpu.roll(q, 1, 0))
        east = jnp.where(row == height - 1, east_row, pltpu.roll(q, height - 1, 0))
        south = jnp.where(col == 0, south_cols[:, level:level + 1], pltpu.roll(q, 1, 1))
        north = jnp.where(
            col == width - 1, north_cols[:, level:level + 1], pltpu.roll(q, width - 1, 1)
        )
        along_rows = velocity[0, level]
        along_columns = velocity[1, level]
        upwind = (
            jnp.maximum(along_rows, 0.0) * (q - west)
            + jnp.minimum(along_rows, 0.0) * (east - q)
            + jnp.maximum(along_columns, 0.0) * (q - south)
            + jnp.minimum(along_columns, 0.0) * (north - q)
        )
        moved = q - upwind + mixing[level] * (east + west + north + south - 4.0 * q)
        if relaxed:
            moved = moved + weight[...] * (forcing[0, level] - moved)
            last_row[pl.ds(first + level, 1), :] = moved[height - 1:height, :]
            first_row[pl.ds(first + level, 1), :] = moved[0:1, :]
            sides = lax.dot_general(
                ends, moved, numbers, precision=exact, preferred_element_type=jnp.float32
            )
            first_col[pl.ds(first + level, 1), :] = sides[0:1, :]
            last_col[pl.ds(first + level, 1), :] = sides[1:2, :]
        out[0, level] = moved


def stencil(values, halo, velocity, mixing, forcing=None, weight=None):
    fields, levels, height, width = values.shape
    west_row, east_row, south_col, north_col = halo
    plane = pl.BlockSpec((1, levels, height, width), lambda f: (f, 0, 0, 0))
    edge_row = pl.BlockSpec((fields * levels, width), lambda f: (0, 0))
    edge_col = pl.BlockSpec((fields * levels, height), lambda f: (0, 0))
    operands = [values, velocity, mixing, west_row, east_row, south_col, north_col]
    specs = [
        plane,
        pl.BlockSpec(velocity.shape, lambda f: (0, 0, 0, 0)),
        pl.BlockSpec(mixing.shape, lambda f: (0, 0, 0)),
        edge_row,
        edge_row,
        edge_col,
        edge_col,
    ]
    relaxed = forcing is not None
    out_shape = jax.ShapeDtypeStruct(values.shape, values.dtype)
    out_specs = plane
    if relaxed:
        operands += [forcing, weight]
        specs += [plane, pl.BlockSpec(weight.shape, lambda f: (0, 0))]
        rows_shape = jax.ShapeDtypeStruct((fields * levels, width), values.dtype)
        cols_shape = jax.ShapeDtypeStruct((fields * levels, height), values.dtype)
        out_shape = (out_shape, rows_shape, rows_shape, cols_shape, cols_shape)
        out_specs = (plane, edge_row, edge_row, edge_col, edge_col)
    return pl.pallas_call(
        lambda *refs: stencil_kernel(relaxed, *refs),
        out_shape=out_shape,
        grid=(fields,),
        in_specs=specs,
        out_specs=out_specs,
    )(*operands)


def flat(block):
    size = block.size
    return block.reshape(size // 128, 128) if size % 128 == 0 else block.reshape(-1, block.shape[-1])


def per_device(
    parent_fields,
    parent_velocity,
    parent_mixing,
    nest_fields,
    nest_velocity,
    nest_mixing,
    nest_anchor,
):
    row_rank = lax.axis_index("gx")
    column_rank = lax.axis_index("gy")
    row_devices = lax.axis_size("gx")
    column_devices = lax.axis_size("gy")
    parent_rows = parent_fields.shape[2]
    parent_columns = parent_fields.shape[3]
    nest_rows = nest_fields.shape[2]
    nest_columns = nest_fields.shape[3]
    span_rows = nest_rows // 3
    span_columns = nest_columns // 3
    ratio = parent_columns // span_columns
    base = column_devices // 2
    base_column = base * parent_columns
    relay_rows = span_rows + 2
    relay_columns = span_columns + 2
    row_anchor = nest_anchor[0]
    column_anchor = nest_anchor[1]
    offset = column_anchor - 1 - base_column

    parent_next = stencil(
        parent_fields, neighbours(edges(parent_fields), 2), parent_velocity, parent_mixing
    )

    margin = parent_columns - span_columns
    wide = jnp.pad(parent_next, ((0, 0), (0, 0), (0, 0), (margin, margin)))
    straddle = (ratio - 1) * span_columns - 2
    regimes = (
        lambda k, extra: not (extra == 1 and k == ratio - 2),
        lambda k, extra: True,
        lambda k, extra: not (extra == 0 and k == ratio - 1),
    )
    regime = (offset > straddle - span_columns).astype(jnp.int32) + (
        offset > straddle - span_columns + 1
    ).astype(jnp.int32)
    pieces = []
    routes = []
    for extra in (0, 1):
        for k in range(ratio):
            if extra == 1 and k == 0:
                continue
            start = margin + span_columns * k + offset - extra * parent_columns
            piece = lax.dynamic_slice_in_dim(wide, start, relay_columns, axis=3)
            routes.append((k, extra, len(pieces)))
            pieces.append(flat(piece))
    stacked_pieces = jnp.stack(pieces)
    branches = []
    for number, active in enumerate(regimes):
        patterns = [
            (column_pairs(column_devices, base, ratio, k, extra), index, extra)
            for k, extra, index in routes
            if active(k, extra)
        ]
        identity = (0, 6, 7)[number]
        branches.append(
            lambda stacked, patterns=patterns, identity=identity: tuple(
                exchange(stacked, patterns, 2, "gy", identity)
            )
        )
    within_part, beyond_part = lax.switch(regime, branches, stacked_pieces)
    piece_shape = parent_next.shape[:3] + (relay_columns,)
    relay_cols = within_part.reshape(piece_shape) + beyond_part.reshape(piece_shape)

    padded = jnp.pad(relay_cols, ((0, 0), (0, 0), (relay_rows, relay_rows), (0, 0)))
    targets = jnp.arange(row_devices, dtype=jnp.int32)[:, None]
    first = row_anchor - 1 + span_rows * targets - parent_rows * row_rank
    first = jnp.clip(first, -relay_rows, parent_rows) + relay_rows
    picks = first + jnp.arange(relay_rows, dtype=jnp.int32)[None, :]
    stacked = jnp.take(padded, picks, axis=2, mode="clip")
    received = lax.all_to_all(stacked, "gx", split_axis=2, concat_axis=2, tiled=True)
    relay = jnp.sum(received, axis=2)

    forcing = refine(relay)
    row_global = row_rank * nest_rows + jnp.arange(nest_rows, dtype=jnp.int32)
    column_global = column_rank * nest_columns + jnp.arange(nest_columns, dtype=jnp.int32)
    weight = relax_weight(
        row_global, column_global, row_devices * nest_rows, column_devices * nest_columns
    )
    state = nest_fields
    sides = edges(state)
    for substep in range(SUBSTEPS):
        state, *sides = stencil(
            state, neighbours(sides, 3 + substep), nest_velocity, nest_mixing, forcing, weight
        )

    coarse = block_mean(state)
    fields_count, levels_count = coarse.shape[:2]
    collected = gather(coarse.reshape((-1,) + coarse.shape[2:]), "gx", 9)
    gathered = jnp.moveaxis(collected, 0, 1).reshape(
        fields_count, levels_count, row_devices * span_rows, coarse.shape[3]
    )
    total_span = row_devices * span_rows
    gathered = jnp.pad(gathered, ((0, 0), (0, 0), (parent_rows, parent_rows), (0, 0)))
    first = jnp.clip(parent_rows * row_rank - row_anchor, -parent_rows, total_span)
    strip = lax.dynamic_slice_in_dim(gathered, first + parent_rows, parent_rows, axis=2)

    routes = []
    for extra in (1, 0):
        for k in range(ratio):
            if extra == 1 and k == 0:
                continue
            pairs = [(j, p) for (p, j) in column_pairs(column_devices, base, ratio, k, extra)]
            routes.append((k, extra, pairs))
    back_branches = []
    for number, skipped in enumerate(((1, 1), (0, ratio - 1))):
        patterns = [
            (pairs, 0, slot) for slot, (k, extra, pairs) in enumerate(routes)
            if (k, extra) != (skipped[1], skipped[0])
        ]
        identity = (1, 8)[number]
        back_branches.append(
            lambda sent, patterns=patterns, identity=identity: tuple(
                exchange(sent, patterns, len(routes), "gy", identity)
            )
        )
    late = (offset > (ratio - 1) * span_columns - span_columns - 1).astype(jnp.int32)
    parts = lax.switch(late, back_branches, flat(strip)[None])
    joined = jnp.concatenate([part.reshape(strip.shape) for part in parts], axis=3)
    start = (ratio - 1) * span_columns - 1 - offset
    fed_back = lax.dynamic_slice_in_dim(joined, start, parent_columns, axis=3)

    relative_rows = row_rank * parent_rows + jnp.arange(parent_rows, dtype=jnp.int32) - row_anchor
    relative_columns = (
        column_rank * parent_columns + jnp.arange(parent_columns, dtype=jnp.int32) - column_anchor
    )
    rows_valid = within(relative_rows, total_span)
    columns_valid = within(relative_columns, column_devices * span_columns)
    covered = rows_valid[:, None] & columns_valid[None, :]
    parent_result = jnp.where(covered, fed_back, parent_next)
    return (parent_result, state)


def solution(mesh):
    placed = (
        P(None, None, "gx", "gy"),
        P(None, None, "gx", "gy"),
        P(None, "gx", "gy"),
        P(None, None, "gx", "gy"),
        P(None, None, "gx", "gy"),
        P(None, "gx", "gy"),
        P(),
    )
    return jax.shard_map(
        per_device,
        mesh=mesh,
        in_specs=placed,
        out_specs=(P(None, None, "gx", "gy"), P(None, None, "gx", "gy")),
        check_vma=False,
    )
```

```python
import jax
import jax.numpy as jnp
from jax import lax
from jax.experimental import pallas as pl
from jax.experimental.pallas import tpu as pltpu
from jax.sharding import PartitionSpec as P

MESH = pl.DeviceIdType.MESH

SUBSTEPS = 3


third = 1.0 / 3.0
two_thirds = 2.0 / 3.0
nudge_floor = 0.1
relax_width = 4.0


def shift_pairs(count, step):
    return [(i, i + step) for i in range(count) if 0 <= i + step < count]


def halo_kernel(rows, cols, *refs):
    sources, targets, send_sems, recv_sems = refs[:4], refs[4:8], refs[8], refs[9]
    x = lax.axis_index("gx")
    y = lax.axis_index("gy")
    routes = (("gx", x, 1, rows), ("gx", x, -1, rows), ("gy", y, 1, cols), ("gy", y, -1, cols))
    barrier = pltpu.get_barrier_semaphore()
    for axis, own, step, count in routes:
        @pl.when((own + step >= 0) & (own + step < count))
        def _():
            pl.semaphore_signal(barrier, 1, device_id={axis: own + step}, device_id_type=MESH)

    peers = (x + rows - 1) // rows + (2 * rows - 2 - x) // rows
    peers = peers + (y + cols - 1) // cols + (2 * cols - 2 - y) // cols
    pl.semaphore_wait(barrier, peers)
    copies = []
    for number, (axis, own, step, count) in enumerate(routes):
        copy = pltpu.make_async_remote_copy(
            src_ref=sources[number],
            dst_ref=targets[number],
            send_sem=send_sems.at[number],
            recv_sem=recv_sems.at[number],
            device_id={axis: own + step},
            device_id_type=MESH,
        )
        copies.append((own, step, count, copy))

        @pl.when((own + step >= 0) & (own + step < count))
        def _():
            copy.start()

    for number, (own, step, count, copy) in enumerate(copies):
        @pl.when((own + step >= 0) & (own + step < count))
        def _():
            copy.wait_send()

        @pl.when((own - step >= 0) & (own - step < count))
        def _():
            copy.wait_recv()

        @pl.when((own - step < 0) | (own - step >= count))
        def _():
            targets[number][...] = jnp.zeros(targets[number].shape, targets[number].dtype)


def edges(cells):
    fields, levels, height, width = cells.shape
    planes = fields * levels
    return (
        cells[:, :, -1, :].reshape(planes, width),
        cells[:, :, 0, :].reshape(planes, width),
        cells[:, :, :, -1].reshape(planes, height),
        cells[:, :, :, 0].reshape(planes, height),
    )


def neighbours(sources, identity):
    rows = lax.axis_size("gx")
    cols = lax.axis_size("gy")
    received = pl.pallas_call(
        lambda *refs: halo_kernel(rows, cols, *refs),
        out_shape=tuple(jax.ShapeDtypeStruct(part.shape, part.dtype) for part in sources),
        in_specs=[pl.BlockSpec(memory_space=pltpu.VMEM)] * 4,
        out_specs=tuple(pl.BlockSpec(memory_space=pltpu.VMEM) for _ in range(4)),
        scratch_shapes=[pltpu.SemaphoreType.DMA((4,)), pltpu.SemaphoreType.DMA((4,))],
        compiler_params=pltpu.CompilerParams(collective_id=identity, has_side_effects=True),
    )(*sources)
    return received


def update(values, halo, velocity, mixing):
    west_row, east_row, south_col, north_col = halo
    western = jnp.concatenate([west_row, values[:, :, :-1, :]], axis=2)
    eastern = jnp.concatenate([values[:, :, 1:, :], east_row], axis=2)
    southern = jnp.concatenate([south_col, values[:, :, :, :-1]], axis=3)
    northern = jnp.concatenate([values[:, :, :, 1:], north_col], axis=3)
    along_rows = velocity[0]
    along_columns = velocity[1]
    upwind = (
        jnp.maximum(along_rows, 0.0) * (values - western)
        + jnp.minimum(along_rows, 0.0) * (eastern - values)
        + jnp.maximum(along_columns, 0.0) * (values - southern)
        + jnp.minimum(along_columns, 0.0) * (northern - values)
    )
    return values - upwind + mixing * (eastern + western + northern + southern - 4.0 * values)


def refine_rows(block):
    lower = block[:, :, :-2]
    centre = block[:, :, 1:-1]
    upper = block[:, :, 2:]
    stacked = jnp.stack(
        (third * lower + two_thirds * centre, centre, two_thirds * centre + third * upper), axis=3
    )
    extent = centre.shape
    return stacked.reshape(extent[0], extent[1], 3 * extent[2], extent[3])


def refine_columns(block):
    lower = block[:, :, :, :-2]
    centre = block[:, :, :, 1:-1]
    upper = block[:, :, :, 2:]
    stacked = jnp.stack(
        (third * lower + two_thirds * centre, centre, two_thirds * centre + third * upper), axis=4
    )
    extent = centre.shape
    return stacked.reshape(extent[0], extent[1], extent[2], 3 * extent[3])


def refining(count):
    fine = jnp.arange(3 * count, dtype=jnp.int32)[:, None]
    coarse = jnp.arange(count + 2, dtype=jnp.int32)[None, :]
    centre = fine // 3 + 1
    phase = fine % 3
    lower = jnp.where(phase == 0, third, jnp.where(phase == 2, 0.0, 0.0))
    upper = jnp.where(phase == 2, third, 0.0)
    middle = jnp.where(phase == 1, 1.0, two_thirds)
    return (
        jnp.where(coarse == centre, middle, 0.0)
        + jnp.where(coarse == centre - 1, lower, 0.0)
        + jnp.where(coarse == centre + 1, upper, 0.0)
    ).astype(jnp.float32)


def refine(block):
    exact = lax.Precision.HIGHEST
    rows = block.shape[2] - 2
    cols = block.shape[3] - 2
    down = jnp.einsum("ar,flrc->flac", refining(rows), block, precision=exact)
    return jnp.einsum("flac,bc->flab", down, refining(cols), precision=exact)


def grouping(count):
    rows = jnp.arange(count, dtype=jnp.int32)[:, None] // 3
    return (rows == jnp.arange(count // 3, dtype=jnp.int32)[None, :]).astype(jnp.float32)


def block_mean(state):
    extent = state.shape
    exact = lax.Precision.HIGHEST
    across = jnp.einsum("flrc,cb->flrb", state, grouping(extent[3]), precision=exact)
    down = jnp.einsum("ra,flrb->flab", grouping(extent[2]), across, precision=exact)
    return down / 9.0


def relax_weight(row_global, column_global, total_rows, total_columns):
    row_distance = jnp.minimum(row_global, total_rows - 1 - row_global)
    column_distance = jnp.minimum(column_global, total_columns - 1 - column_global)
    distance = jnp.minimum(row_distance[:, None], column_distance[None, :]).astype(jnp.float32)
    return nudge_floor + (1.0 - nudge_floor) * jnp.exp(-distance / relax_width)


def within(positions, limit):
    return (positions >= 0) & (positions < limit)


def column_pairs(count, base, ratio, k, extra):
    pairs = []
    for m in range(count):
        j = ratio * m + k
        p = base + m + extra
        if j < count and p < count:
            pairs.append((p, j))
    return pairs


def exchange_kernel(axis, patterns, local, send_ref, recv_ref, send_sems, recv_sems):
    me = lax.axis_index(axis)
    receivers = {}
    for pairs, _, slot in patterns:
        for a, b in pairs:
            receivers.setdefault(slot, set()).add(b)
    for a, source, slot in local:
        receivers.setdefault(slot, set()).add(a)
    for slot in range(recv_ref.shape[0]):
        idle = None
        for device in sorted(receivers.get(slot, ())):
            test = me != device
            idle = test if idle is None else idle & test
        if idle is None:
            recv_ref[slot] = jnp.zeros(recv_ref.shape[1:], recv_ref.dtype)
            continue

        @pl.when(idle)
        def _():
            recv_ref[slot] = jnp.zeros(recv_ref.shape[1:], recv_ref.dtype)

    for a, source, slot in local:
        @pl.when(me == a)
        def _():
            recv_ref[slot] = send_ref[source]

    barrier = pltpu.get_barrier_semaphore()
    links = [pair for pairs, _, _ in patterns for pair in pairs]
    for a, b in links:
        @pl.when(me == a)
        def _():
            pl.semaphore_signal(barrier, 1, device_id={axis: b}, device_id_type=MESH)

        @pl.when(me == b)
        def _():
            pl.semaphore_signal(barrier, 1, device_id={axis: a}, device_id_type=MESH)

    peers = {}
    for a, b in links:
        peers[a] = peers.get(a, 0) + 1
        peers[b] = peers.get(b, 0) + 1
    for device, count in sorted(peers.items()):
        @pl.when(me == device)
        def _():
            pl.semaphore_wait(barrier, count)

    copies = []
    for number, (pairs, source, slot) in enumerate(patterns):
        for a, b in pairs:
            copy = pltpu.make_async_remote_copy(
                src_ref=send_ref.at[source],
                dst_ref=recv_ref.at[slot],
                send_sem=send_sems.at[number],
                recv_sem=recv_sems.at[slot],
                device_id={axis: b},
                device_id_type=MESH,
            )
            copies.append((a, b, copy))

            @pl.when(me == a)
            def _():
                copy.start()

    for a, b, copy in copies:
        @pl.when(me == a)
        def _():
            copy.wait_send()

        @pl.when(me == b)
        def _():
            copy.wait_recv()


def exchange(pieces, patterns, slots, axis, identity):
    remote = [([(a, b) for a, b in pairs if a != b], source, slot) for pairs, source, slot in patterns]
    remote = [entry for entry in remote if entry[0]]
    local = [(a, source, slot) for pairs, source, slot in patterns for a, b in pairs if a == b]
    shape = pieces.shape[1:]
    received = pl.pallas_call(
        lambda *refs: exchange_kernel(axis, remote, local, *refs),
        out_shape=jax.ShapeDtypeStruct((slots,) + shape, pieces.dtype),
        in_specs=[pl.BlockSpec(memory_space=pltpu.VMEM)],
        out_specs=pl.BlockSpec(memory_space=pltpu.VMEM),
        scratch_shapes=[
            pltpu.SemaphoreType.DMA((len(remote),)),
            pltpu.SemaphoreType.DMA((slots,)),
        ],
        compiler_params=pltpu.CompilerParams(collective_id=identity, has_side_effects=True),
    )(pieces)
    return [received[slot] for slot in range(slots)]


def gather_kernel(axis, count, source, target, send_sems, recv_sems):
    me = lax.axis_index(axis)
    barrier = pltpu.get_barrier_semaphore()
    for delta in range(1, count):
        pl.semaphore_signal(
            barrier, 1, device_id={axis: (me + delta) % count}, device_id_type=MESH
        )
    pl.semaphore_wait(barrier, count - 1)
    outgoing = []
    for delta in range(1, count):
        copy = pltpu.make_async_remote_copy(
            src_ref=source,
            dst_ref=target.at[me],
            send_sem=send_sems.at[delta - 1],
            recv_sem=recv_sems.at[delta - 1],
            device_id={axis: (me + delta) % count},
            device_id_type=MESH,
        )
        copy.start()
        outgoing.append(copy)
    target[me] = source[...]
    for delta, copy in zip(range(1, count), outgoing):
        copy.wait_send()
        incoming = pltpu.make_async_remote_copy(
            src_ref=source,
            dst_ref=target.at[(me + count - delta) % count],
            send_sem=send_sems.at[delta - 1],
            recv_sem=recv_sems.at[delta - 1],
            device_id={axis: (me + count - delta) % count},
            device_id_type=MESH,
        )
        incoming.wait_recv()


def gather(block, axis, identity):
    count = lax.axis_size(axis)
    return pl.pallas_call(
        lambda *refs: gather_kernel(axis, count, *refs),
        out_shape=jax.ShapeDtypeStruct((count,) + block.shape, block.dtype),
        in_specs=[pl.BlockSpec(memory_space=pltpu.VMEM)],
        out_specs=pl.BlockSpec(memory_space=pltpu.VMEM),
        scratch_shapes=[
            pltpu.SemaphoreType.DMA((count - 1,)),
            pltpu.SemaphoreType.DMA((count - 1,)),
        ],
        compiler_params=pltpu.CompilerParams(collective_id=identity, has_side_effects=True),
    )(block)


def stencil_kernel(relaxed, *refs):
    if relaxed:
        (values, velocity, mixing, western, eastern, southern, northern, forcing, weight) = refs[:9]
        out, last_row, first_row, last_col, first_col = refs[9:]
    else:
        (values, velocity, mixing, western, eastern, southern, northern, out) = refs
    levels, height, width = values.shape[1:]
    row = lax.broadcasted_iota(jnp.int32, (height, width), 0)
    col = lax.broadcasted_iota(jnp.int32, (height, width), 1)
    eye = (
        lax.broadcasted_iota(jnp.int32, (height, height), 0)
        == lax.broadcasted_iota(jnp.int32, (height, height), 1)
    ).astype(jnp.float32)
    first = pl.multiple_of(pl.program_id(0) * levels, levels)
    numbers = (((1,), (1,)), ((), ()))
    exact = lax.Precision.HIGHEST
    south_cols = lax.dot_general(
        eye, southern[pl.ds(first, levels), :], numbers, precision=exact,
        preferred_element_type=jnp.float32,
    )
    north_cols = lax.dot_general(
        eye, northern[pl.ds(first, levels), :], numbers, precision=exact,
        preferred_element_type=jnp.float32,
    )
    picks = lax.broadcasted_iota(jnp.int32, (8, width), 1)
    chosen = lax.broadcasted_iota(jnp.int32, (8, width), 0)
    ends = ((chosen == 0) & (picks == 0)) | ((chosen == 1) & (picks == width - 1))
    ends = ends.astype(jnp.float32)
    for level in range(levels):
        q = values[0, level]
        west_row = western[pl.ds(first + level, 1), :]
        east_row = eastern[pl.ds(first + level, 1), :]
        west = jnp.where(row == 0, west_row, pltpu.roll(q, 1, 0))
        east = jnp.where(row == height - 1, east_row, pltpu.roll(q, height - 1, 0))
        south = jnp.where(col == 0, south_cols[:, level:level + 1], pltpu.roll(q, 1, 1))
        north = jnp.where(
            col == width - 1, north_cols[:, level:level + 1], pltpu.roll(q, width - 1, 1)
        )
        along_rows = velocity[0, level]
        along_columns = velocity[1, level]
        upwind = (
            jnp.maximum(along_rows, 0.0) * (q - west)
            + jnp.minimum(along_rows, 0.0) * (east - q)
            + jnp.maximum(along_columns, 0.0) * (q - south)
            + jnp.minimum(along_columns, 0.0) * (north - q)
        )
        moved = q - upwind + mixing[level] * (east + west + north + south - 4.0 * q)
        if relaxed:
            moved = moved + weight[...] * (forcing[0, level] - moved)
            last_row[pl.ds(first + level, 1), :] = moved[height - 1:height, :]
            first_row[pl.ds(first + level, 1), :] = moved[0:1, :]
            sides = lax.dot_general(
                ends, moved, numbers, precision=exact, preferred_element_type=jnp.float32
            )
            first_col[pl.ds(first + level, 1), :] = sides[0:1, :]
            last_col[pl.ds(first + level, 1), :] = sides[1:2, :]
        out[0, level] = moved


def stencil(values, halo, velocity, mixing, forcing=None, weight=None):
    fields, levels, height, width = values.shape
    west_row, east_row, south_col, north_col = halo
    plane = pl.BlockSpec((1, levels, height, width), lambda f: (f, 0, 0, 0))
    edge_row = pl.BlockSpec((fields * levels, width), lambda f: (0, 0))
    edge_col = pl.BlockSpec((fields * levels, height), lambda f: (0, 0))
    operands = [values, velocity, mixing, west_row, east_row, south_col, north_col]
    specs = [
        plane,
        pl.BlockSpec(velocity.shape, lambda f: (0, 0, 0, 0)),
        pl.BlockSpec(mixing.shape, lambda f: (0, 0, 0)),
        edge_row,
        edge_row,
        edge_col,
        edge_col,
    ]
    relaxed = forcing is not None
    out_shape = jax.ShapeDtypeStruct(values.shape, values.dtype)
    out_specs = plane
    if relaxed:
        operands += [forcing, weight]
        specs += [plane, pl.BlockSpec(weight.shape, lambda f: (0, 0))]
        rows_shape = jax.ShapeDtypeStruct((fields * levels, width), values.dtype)
        cols_shape = jax.ShapeDtypeStruct((fields * levels, height), values.dtype)
        out_shape = (out_shape, rows_shape, rows_shape, cols_shape, cols_shape)
        out_specs = (plane, edge_row, edge_row, edge_col, edge_col)
    return pl.pallas_call(
        lambda *refs: stencil_kernel(relaxed, *refs),
        out_shape=out_shape,
        grid=(fields,),
        in_specs=specs,
        out_specs=out_specs,
    )(*operands)


def flat(block):
    size = block.size
    return block.reshape(size // 128, 128) if size % 128 == 0 else block.reshape(-1, block.shape[-1])


def per_device(
    parent_fields,
    parent_velocity,
    parent_mixing,
    nest_fields,
    nest_velocity,
    nest_mixing,
    nest_anchor,
):
    row_rank = lax.axis_index("gx")
    column_rank = lax.axis_index("gy")
    row_devices = lax.axis_size("gx")
    column_devices = lax.axis_size("gy")
    parent_rows = parent_fields.shape[2]
    parent_columns = parent_fields.shape[3]
    nest_rows = nest_fields.shape[2]
    nest_columns = nest_fields.shape[3]
    span_rows = nest_rows // 3
    span_columns = nest_columns // 3
    ratio = parent_columns // span_columns
    base = column_devices // 2
    base_column = base * parent_columns
    relay_rows = span_rows + 2
    relay_columns = span_columns + 2
    row_anchor = nest_anchor[0]
    column_anchor = nest_anchor[1]
    offset = column_anchor - 1 - base_column

    parent_next = stencil(
        parent_fields, neighbours(edges(parent_fields), 2), parent_velocity, parent_mixing
    )

    margin = parent_columns - span_columns
    wide = jnp.pad(parent_next, ((0, 0), (0, 0), (0, 0), (margin, margin)))
    straddle = (ratio - 1) * span_columns - 2
    regimes = (
        lambda k, extra: not (extra == 1 and k == ratio - 2),
        lambda k, extra: True,
        lambda k, extra: not (extra == 0 and k == ratio - 1),
    )
    regime = (offset > straddle - span_columns).astype(jnp.int32) + (
        offset > straddle - span_columns + 1
    ).astype(jnp.int32)
    pieces = []
    routes = []
    for extra in (0, 1):
        for k in range(ratio):
            if extra == 1 and k == 0:
                continue
            start = margin + span_columns * k + offset - extra * parent_columns
            piece = lax.dynamic_slice_in_dim(wide, start, relay_columns, axis=3)
            routes.append((k, extra, len(pieces)))
            pieces.append(flat(piece))
    stacked_pieces = jnp.stack(pieces)
    branches = []
    for number, active in enumerate(regimes):
        patterns = [
            (column_pairs(column_devices, base, ratio, k, extra), index, extra)
            for k, extra, index in routes
            if active(k, extra)
        ]
        identity = (0, 6, 7)[number]
        branches.append(
            lambda stacked, patterns=patterns, identity=identity: tuple(
                exchange(stacked, patterns, 2, "gy", identity)
            )
        )
    within_part, beyond_part = lax.switch(regime, branches, stacked_pieces)
    piece_shape = parent_next.shape[:3] + (relay_columns,)
    relay_cols = within_part.reshape(piece_shape) + beyond_part.reshape(piece_shape)

    padded = jnp.pad(relay_cols, ((0, 0), (0, 0), (relay_rows, relay_rows), (0, 0)))
    targets = jnp.arange(row_devices, dtype=jnp.int32)[:, None]
    first = row_anchor - 1 + span_rows * targets - parent_rows * row_rank
    first = jnp.clip(first, -relay_rows, parent_rows) + relay_rows
    picks = first + jnp.arange(relay_rows, dtype=jnp.int32)[None, :]
    stacked = jnp.take(padded, picks, axis=2, mode="clip")
    received = lax.all_to_all(stacked, "gx", split_axis=2, concat_axis=2, tiled=True)
    relay = jnp.sum(received, axis=2)

    forcing = refine(relay)
    row_global = row_rank * nest_rows + jnp.arange(nest_rows, dtype=jnp.int32)
    column_global = column_rank * nest_columns + jnp.arange(nest_columns, dtype=jnp.int32)
    weight = relax_weight(
        row_global, column_global, row_devices * nest_rows, column_devices * nest_columns
    )
    state = nest_fields
    sides = edges(state)
    for substep in range(SUBSTEPS):
        state, *sides = stencil(
            state, neighbours(sides, 3 + substep), nest_velocity, nest_mixing, forcing, weight
        )

    coarse = block_mean(state)
    fields_count, levels_count = coarse.shape[:2]
    collected = gather(coarse.reshape((-1,) + coarse.shape[2:]), "gx", 9)
    gathered = jnp.moveaxis(collected, 0, 1).reshape(
        fields_count, levels_count, row_devices * span_rows, coarse.shape[3]
    )
    total_span = row_devices * span_rows
    picks = parent_rows * row_rank - row_anchor + jnp.arange(parent_rows, dtype=jnp.int32)
    strip = jnp.take(gathered, jnp.clip(picks, 0, total_span - 1), axis=2, mode="clip")

    routes = []
    for extra in (1, 0):
        for k in range(ratio):
            if extra == 1 and k == 0:
                continue
            pairs = [(j, p) for (p, j) in column_pairs(column_devices, base, ratio, k, extra)]
            routes.append((k, extra, pairs))
    back_branches = []
    for number, skipped in enumerate(((1, 1), (0, ratio - 1))):
        patterns = [
            (pairs, 0, slot) for slot, (k, extra, pairs) in enumerate(routes)
            if (k, extra) != (skipped[1], skipped[0])
        ]
        identity = (1, 8)[number]
        back_branches.append(
            lambda sent, patterns=patterns, identity=identity: tuple(
                exchange(sent, patterns, len(routes), "gy", identity)
            )
        )
    late = (offset > (ratio - 1) * span_columns - span_columns - 1).astype(jnp.int32)
    parts = lax.switch(late, back_branches, flat(strip)[None])
    joined = jnp.concatenate([part.reshape(strip.shape) for part in parts], axis=3)
    start = (ratio - 1) * span_columns - 1 - offset
    fed_back = lax.dynamic_slice_in_dim(joined, start, parent_columns, axis=3)

    relative_rows = row_rank * parent_rows + jnp.arange(parent_rows, dtype=jnp.int32) - row_anchor
    relative_columns = (
        column_rank * parent_columns + jnp.arange(parent_columns, dtype=jnp.int32) - column_anchor
    )
    rows_valid = within(relative_rows, total_span)
    columns_valid = within(relative_columns, column_devices * span_columns)
    covered = rows_valid[:, None] & columns_valid[None, :]
    parent_result = jnp.where(covered, fed_back, parent_next)
    return (parent_result, state)


def solution(mesh):
    placed = (
        P(None, None, "gx", "gy"),
        P(None, None, "gx", "gy"),
        P(None, "gx", "gy"),
        P(None, None, "gx", "gy"),
        P(None, None, "gx", "gy"),
        P(None, "gx", "gy"),
        P(),
    )
    return jax.shard_map(
        per_device,
        mesh=mesh,
        in_specs=placed,
        out_specs=(P(None, None, "gx", "gy"), P(None, None, "gx", "gy")),
        check_vma=False,
    )
```

```python
import jax
import jax.numpy as jnp
from jax import lax
from jax.experimental import pallas as pl
from jax.experimental.pallas import tpu as pltpu
from jax.sharding import PartitionSpec as P

MESH = pl.DeviceIdType.MESH

SUBSTEPS = 3


third = 1.0 / 3.0
two_thirds = 2.0 / 3.0
nudge_floor = 0.1
relax_width = 4.0


def shift_pairs(count, step):
    return [(i, i + step) for i in range(count) if 0 <= i + step < count]


def halo_kernel(rows, cols, *refs):
    sources, targets, send_sems, recv_sems = refs[:4], refs[4:8], refs[8], refs[9]
    x = lax.axis_index("gx")
    y = lax.axis_index("gy")
    routes = (("gx", x, 1, rows), ("gx", x, -1, rows), ("gy", y, 1, cols), ("gy", y, -1, cols))
    barrier = pltpu.get_barrier_semaphore()
    for axis, own, step, count in routes:
        @pl.when((own + step >= 0) & (own + step < count))
        def _():
            pl.semaphore_signal(barrier, 1, device_id={axis: own + step}, device_id_type=MESH)

    peers = (x + rows - 1) // rows + (2 * rows - 2 - x) // rows
    peers = peers + (y + cols - 1) // cols + (2 * cols - 2 - y) // cols
    pl.semaphore_wait(barrier, peers)
    copies = []
    for number, (axis, own, step, count) in enumerate(routes):
        copy = pltpu.make_async_remote_copy(
            src_ref=sources[number],
            dst_ref=targets[number],
            send_sem=send_sems.at[number],
            recv_sem=recv_sems.at[number],
            device_id={axis: own + step},
            device_id_type=MESH,
        )
        copies.append((own, step, count, copy))

        @pl.when((own + step >= 0) & (own + step < count))
        def _():
            copy.start()

    for number, (own, step, count, copy) in enumerate(copies):
        @pl.when((own + step >= 0) & (own + step < count))
        def _():
            copy.wait_send()

        @pl.when((own - step >= 0) & (own - step < count))
        def _():
            copy.wait_recv()

        @pl.when((own - step < 0) | (own - step >= count))
        def _():
            targets[number][...] = jnp.zeros(targets[number].shape, targets[number].dtype)


def edges(cells):
    fields, levels, height, width = cells.shape
    planes = fields * levels
    return (
        cells[:, :, -1, :].reshape(planes, width),
        cells[:, :, 0, :].reshape(planes, width),
        cells[:, :, :, -1].reshape(planes, height),
        cells[:, :, :, 0].reshape(planes, height),
    )


def neighbours(sources, identity):
    rows = lax.axis_size("gx")
    cols = lax.axis_size("gy")
    received = pl.pallas_call(
        lambda *refs: halo_kernel(rows, cols, *refs),
        out_shape=tuple(jax.ShapeDtypeStruct(part.shape, part.dtype) for part in sources),
        in_specs=[pl.BlockSpec(memory_space=pltpu.VMEM)] * 4,
        out_specs=tuple(pl.BlockSpec(memory_space=pltpu.VMEM) for _ in range(4)),
        scratch_shapes=[pltpu.SemaphoreType.DMA((4,)), pltpu.SemaphoreType.DMA((4,))],
        compiler_params=pltpu.CompilerParams(collective_id=identity, has_side_effects=True),
    )(*sources)
    return received


def update(values, halo, velocity, mixing):
    west_row, east_row, south_col, north_col = halo
    western = jnp.concatenate([west_row, values[:, :, :-1, :]], axis=2)
    eastern = jnp.concatenate([values[:, :, 1:, :], east_row], axis=2)
    southern = jnp.concatenate([south_col, values[:, :, :, :-1]], axis=3)
    northern = jnp.concatenate([values[:, :, :, 1:], north_col], axis=3)
    along_rows = velocity[0]
    along_columns = velocity[1]
    upwind = (
        jnp.maximum(along_rows, 0.0) * (values - western)
        + jnp.minimum(along_rows, 0.0) * (eastern - values)
        + jnp.maximum(along_columns, 0.0) * (values - southern)
        + jnp.minimum(along_columns, 0.0) * (northern - values)
    )
    return values - upwind + mixing * (eastern + western + northern + southern - 4.0 * values)


def refine_rows(block):
    lower = block[:, :, :-2]
    centre = block[:, :, 1:-1]
    upper = block[:, :, 2:]
    stacked = jnp.stack(
        (third * lower + two_thirds * centre, centre, two_thirds * centre + third * upper), axis=3
    )
    extent = centre.shape
    return stacked.reshape(extent[0], extent[1], 3 * extent[2], extent[3])


def refine_columns(block):
    lower = block[:, :, :, :-2]
    centre = block[:, :, :, 1:-1]
    upper = block[:, :, :, 2:]
    stacked = jnp.stack(
        (third * lower + two_thirds * centre, centre, two_thirds * centre + third * upper), axis=4
    )
    extent = centre.shape
    return stacked.reshape(extent[0], extent[1], extent[2], 3 * extent[3])


def refining(count):
    fine = jnp.arange(3 * count, dtype=jnp.int32)[:, None]
    coarse = jnp.arange(count + 2, dtype=jnp.int32)[None, :]
    centre = fine // 3 + 1
    phase = fine % 3
    lower = jnp.where(phase == 0, third, jnp.where(phase == 2, 0.0, 0.0))
    upper = jnp.where(phase == 2, third, 0.0)
    middle = jnp.where(phase == 1, 1.0, two_thirds)
    return (
        jnp.where(coarse == centre, middle, 0.0)
        + jnp.where(coarse == centre - 1, lower, 0.0)
        + jnp.where(coarse == centre + 1, upper, 0.0)
    ).astype(jnp.float32)


def refine(block):
    exact = lax.Precision.HIGHEST
    rows = block.shape[2] - 2
    cols = block.shape[3] - 2
    across = jnp.einsum("flrc,bc->flrb", block, refining(cols), precision=exact)
    return jnp.einsum("ar,flrb->flab", refining(rows), across, precision=exact)


def grouping(count):
    rows = jnp.arange(count, dtype=jnp.int32)[:, None] // 3
    return (rows == jnp.arange(count // 3, dtype=jnp.int32)[None, :]).astype(jnp.float32)


def block_mean(state):
    extent = state.shape
    exact = lax.Precision.HIGHEST
    across = jnp.einsum("flrc,cb->flrb", state, grouping(extent[3]), precision=exact)
    down = jnp.einsum("ra,flrb->flab", grouping(extent[2]), across, precision=exact)
    return down / 9.0


def relax_weight(row_global, column_global, total_rows, total_columns):
    row_distance = jnp.minimum(row_global, total_rows - 1 - row_global)
    column_distance = jnp.minimum(column_global, total_columns - 1 - column_global)
    distance = jnp.minimum(row_distance[:, None], column_distance[None, :]).astype(jnp.float32)
    return nudge_floor + (1.0 - nudge_floor) * jnp.exp(-distance / relax_width)


def within(positions, limit):
    return (positions >= 0) & (positions < limit)


def column_pairs(count, base, ratio, k, extra):
    pairs = []
    for m in range(count):
        j = ratio * m + k
        p = base + m + extra
        if j < count and p < count:
            pairs.append((p, j))
    return pairs


def exchange_kernel(axis, patterns, local, send_ref, recv_ref, send_sems, recv_sems):
    me = lax.axis_index(axis)
    receivers = {}
    for pairs, _, slot in patterns:
        for a, b in pairs:
            receivers.setdefault(slot, set()).add(b)
    for a, source, slot in local:
        receivers.setdefault(slot, set()).add(a)
    for slot in range(recv_ref.shape[0]):
        idle = None
        for device in sorted(receivers.get(slot, ())):
            test = me != device
            idle = test if idle is None else idle & test
        if idle is None:
            recv_ref[slot] = jnp.zeros(recv_ref.shape[1:], recv_ref.dtype)
            continue

        @pl.when(idle)
        def _():
            recv_ref[slot] = jnp.zeros(recv_ref.shape[1:], recv_ref.dtype)

    for a, source, slot in local:
        @pl.when(me == a)
        def _():
            recv_ref[slot] = send_ref[source]

    barrier = pltpu.get_barrier_semaphore()
    links = [pair for pairs, _, _ in patterns for pair in pairs]
    for a, b in links:
        @pl.when(me == a)
        def _():
            pl.semaphore_signal(barrier, 1, device_id={axis: b}, device_id_type=MESH)

        @pl.when(me == b)
        def _():
            pl.semaphore_signal(barrier, 1, device_id={axis: a}, device_id_type=MESH)

    peers = {}
    for a, b in links:
        peers[a] = peers.get(a, 0) + 1
        peers[b] = peers.get(b, 0) + 1
    for device, count in sorted(peers.items()):
        @pl.when(me == device)
        def _():
            pl.semaphore_wait(barrier, count)

    copies = []
    for number, (pairs, source, slot) in enumerate(patterns):
        for a, b in pairs:
            copy = pltpu.make_async_remote_copy(
                src_ref=send_ref.at[source],
                dst_ref=recv_ref.at[slot],
                send_sem=send_sems.at[number],
                recv_sem=recv_sems.at[slot],
                device_id={axis: b},
                device_id_type=MESH,
            )
            copies.append((a, b, copy))

            @pl.when(me == a)
            def _():
                copy.start()

    for a, b, copy in copies:
        @pl.when(me == a)
        def _():
            copy.wait_send()

        @pl.when(me == b)
        def _():
            copy.wait_recv()


def exchange(pieces, patterns, slots, axis, identity):
    remote = [([(a, b) for a, b in pairs if a != b], source, slot) for pairs, source, slot in patterns]
    remote = [entry for entry in remote if entry[0]]
    local = [(a, source, slot) for pairs, source, slot in patterns for a, b in pairs if a == b]
    shape = pieces.shape[1:]
    received = pl.pallas_call(
        lambda *refs: exchange_kernel(axis, remote, local, *refs),
        out_shape=jax.ShapeDtypeStruct((slots,) + shape, pieces.dtype),
        in_specs=[pl.BlockSpec(memory_space=pltpu.VMEM)],
        out_specs=pl.BlockSpec(memory_space=pltpu.VMEM),
        scratch_shapes=[
            pltpu.SemaphoreType.DMA((len(remote),)),
            pltpu.SemaphoreType.DMA((slots,)),
        ],
        compiler_params=pltpu.CompilerParams(collective_id=identity, has_side_effects=True),
    )(pieces)
    return [received[slot] for slot in range(slots)]


def gather_kernel(axis, count, source, target, send_sems, recv_sems):
    me = lax.axis_index(axis)
    barrier = pltpu.get_barrier_semaphore()
    for delta in range(1, count):
        pl.semaphore_signal(
            barrier, 1, device_id={axis: (me + delta) % count}, device_id_type=MESH
        )
    pl.semaphore_wait(barrier, count - 1)
    outgoing = []
    for delta in range(1, count):
        copy = pltpu.make_async_remote_copy(
            src_ref=source,
            dst_ref=target.at[me],
            send_sem=send_sems.at[delta - 1],
            recv_sem=recv_sems.at[delta - 1],
            device_id={axis: (me + delta) % count},
            device_id_type=MESH,
        )
        copy.start()
        outgoing.append(copy)
    target[me] = source[...]
    for delta, copy in zip(range(1, count), outgoing):
        copy.wait_send()
        incoming = pltpu.make_async_remote_copy(
            src_ref=source,
            dst_ref=target.at[(me + count - delta) % count],
            send_sem=send_sems.at[delta - 1],
            recv_sem=recv_sems.at[delta - 1],
            device_id={axis: (me + count - delta) % count},
            device_id_type=MESH,
        )
        incoming.wait_recv()


def gather(block, axis, identity):
    count = lax.axis_size(axis)
    return pl.pallas_call(
        lambda *refs: gather_kernel(axis, count, *refs),
        out_shape=jax.ShapeDtypeStruct((count,) + block.shape, block.dtype),
        in_specs=[pl.BlockSpec(memory_space=pltpu.VMEM)],
        out_specs=pl.BlockSpec(memory_space=pltpu.VMEM),
        scratch_shapes=[
            pltpu.SemaphoreType.DMA((count - 1,)),
            pltpu.SemaphoreType.DMA((count - 1,)),
        ],
        compiler_params=pltpu.CompilerParams(collective_id=identity, has_side_effects=True),
    )(block)


def stencil_kernel(relaxed, *refs):
    if relaxed:
        (values, velocity, mixing, western, eastern, southern, northern, forcing, weight) = refs[:9]
        out, last_row, first_row, last_col, first_col = refs[9:]
    else:
        (values, velocity, mixing, western, eastern, southern, northern, out) = refs
    levels, height, width = values.shape[1:]
    row = lax.broadcasted_iota(jnp.int32, (height, width), 0)
    col = lax.broadcasted_iota(jnp.int32, (height, width), 1)
    eye = (
        lax.broadcasted_iota(jnp.int32, (height, height), 0)
        == lax.broadcasted_iota(jnp.int32, (height, height), 1)
    ).astype(jnp.float32)
    first = pl.multiple_of(pl.program_id(0) * levels, levels)
    numbers = (((1,), (1,)), ((), ()))
    exact = lax.Precision.HIGHEST
    south_cols = lax.dot_general(
        eye, southern[pl.ds(first, levels), :], numbers, precision=exact,
        preferred_element_type=jnp.float32,
    )
    north_cols = lax.dot_general(
        eye, northern[pl.ds(first, levels), :], numbers, precision=exact,
        preferred_element_type=jnp.float32,
    )
    picks = lax.broadcasted_iota(jnp.int32, (8, width), 1)
    chosen = lax.broadcasted_iota(jnp.int32, (8, width), 0)
    ends = ((chosen == 0) & (picks == 0)) | ((chosen == 1) & (picks == width - 1))
    ends = ends.astype(jnp.float32)
    for level in range(levels):
        q = values[0, level]
        west_row = western[pl.ds(first + level, 1), :]
        east_row = eastern[pl.ds(first + level, 1), :]
        west = jnp.where(row == 0, west_row, pltpu.roll(q, 1, 0))
        east = jnp.where(row == height - 1, east_row, pltpu.roll(q, height - 1, 0))
        south = jnp.where(col == 0, south_cols[:, level:level + 1], pltpu.roll(q, 1, 1))
        north = jnp.where(
            col == width - 1, north_cols[:, level:level + 1], pltpu.roll(q, width - 1, 1)
        )
        along_rows = velocity[0, level]
        along_columns = velocity[1, level]
        upwind = (
            jnp.maximum(along_rows, 0.0) * (q - west)
            + jnp.minimum(along_rows, 0.0) * (east - q)
            + jnp.maximum(along_columns, 0.0) * (q - south)
            + jnp.minimum(along_columns, 0.0) * (north - q)
        )
        moved = q - upwind + mixing[level] * (east + west + north + south - 4.0 * q)
        if relaxed:
            moved = moved + weight[...] * (forcing[0, level] - moved)
            last_row[pl.ds(first + level, 1), :] = moved[height - 1:height, :]
            first_row[pl.ds(first + level, 1), :] = moved[0:1, :]
            sides = lax.dot_general(
                ends, moved, numbers, precision=exact, preferred_element_type=jnp.float32
            )
            first_col[pl.ds(first + level, 1), :] = sides[0:1, :]
            last_col[pl.ds(first + level, 1), :] = sides[1:2, :]
        out[0, level] = moved


def stencil(values, halo, velocity, mixing, forcing=None, weight=None):
    fields, levels, height, width = values.shape
    west_row, east_row, south_col, north_col = halo
    plane = pl.BlockSpec((1, levels, height, width), lambda f: (f, 0, 0, 0))
    edge_row = pl.BlockSpec((fields * levels, width), lambda f: (0, 0))
    edge_col = pl.BlockSpec((fields * levels, height), lambda f: (0, 0))
    operands = [values, velocity, mixing, west_row, east_row, south_col, north_col]
    specs = [
        plane,
        pl.BlockSpec(velocity.shape, lambda f: (0, 0, 0, 0)),
        pl.BlockSpec(mixing.shape, lambda f: (0, 0, 0)),
        edge_row,
        edge_row,
        edge_col,
        edge_col,
    ]
    relaxed = forcing is not None
    out_shape = jax.ShapeDtypeStruct(values.shape, values.dtype)
    out_specs = plane
    if relaxed:
        operands += [forcing, weight]
        specs += [plane, pl.BlockSpec(weight.shape, lambda f: (0, 0))]
        rows_shape = jax.ShapeDtypeStruct((fields * levels, width), values.dtype)
        cols_shape = jax.ShapeDtypeStruct((fields * levels, height), values.dtype)
        out_shape = (out_shape, rows_shape, rows_shape, cols_shape, cols_shape)
        out_specs = (plane, edge_row, edge_row, edge_col, edge_col)
    return pl.pallas_call(
        lambda *refs: stencil_kernel(relaxed, *refs),
        out_shape=out_shape,
        grid=(fields,),
        in_specs=specs,
        out_specs=out_specs,
    )(*operands)


def flat(block):
    size = block.size
    return block.reshape(size // 128, 128) if size % 128 == 0 else block.reshape(-1, block.shape[-1])


def per_device(
    parent_fields,
    parent_velocity,
    parent_mixing,
    nest_fields,
    nest_velocity,
    nest_mixing,
    nest_anchor,
):
    row_rank = lax.axis_index("gx")
    column_rank = lax.axis_index("gy")
    row_devices = lax.axis_size("gx")
    column_devices = lax.axis_size("gy")
    parent_rows = parent_fields.shape[2]
    parent_columns = parent_fields.shape[3]
    nest_rows = nest_fields.shape[2]
    nest_columns = nest_fields.shape[3]
    span_rows = nest_rows // 3
    span_columns = nest_columns // 3
    ratio = parent_columns // span_columns
    base = column_devices // 2
    base_column = base * parent_columns
    relay_rows = span_rows + 2
    relay_columns = span_columns + 2
    row_anchor = nest_anchor[0]
    column_anchor = nest_anchor[1]
    offset = column_anchor - 1 - base_column

    parent_next = stencil(
        parent_fields, neighbours(edges(parent_fields), 2), parent_velocity, parent_mixing
    )

    margin = parent_columns - span_columns
    wide = jnp.pad(parent_next, ((0, 0), (0, 0), (0, 0), (margin, margin)))
    straddle = (ratio - 1) * span_columns - 2
    regimes = (
        lambda k, extra: not (extra == 1 and k == ratio - 2),
        lambda k, extra: True,
        lambda k, extra: not (extra == 0 and k == ratio - 1),
    )
    regime = (offset > straddle - span_columns).astype(jnp.int32) + (
        offset > straddle - span_columns + 1
    ).astype(jnp.int32)
    pieces = []
    routes = []
    for extra in (0, 1):
        for k in range(ratio):
            if extra == 1 and k == 0:
                continue
            start = margin + span_columns * k + offset - extra * parent_columns
            piece = lax.dynamic_slice_in_dim(wide, start, relay_columns, axis=3)
            routes.append((k, extra, len(pieces)))
            pieces.append(flat(piece))
    stacked_pieces = jnp.stack(pieces)
    branches = []
    for number, active in enumerate(regimes):
        patterns = [
            (column_pairs(column_devices, base, ratio, k, extra), index, extra)
            for k, extra, index in routes
            if active(k, extra)
        ]
        identity = (0, 6, 7)[number]
        branches.append(
            lambda stacked, patterns=patterns, identity=identity: tuple(
                exchange(stacked, patterns, 2, "gy", identity)
            )
        )
    within_part, beyond_part = lax.switch(regime, branches, stacked_pieces)
    piece_shape = parent_next.shape[:3] + (relay_columns,)
    relay_cols = within_part.reshape(piece_shape) + beyond_part.reshape(piece_shape)

    padded = jnp.pad(relay_cols, ((0, 0), (0, 0), (relay_rows, relay_rows), (0, 0)))
    targets = jnp.arange(row_devices, dtype=jnp.int32)[:, None]
    first = row_anchor - 1 + span_rows * targets - parent_rows * row_rank
    first = jnp.clip(first, -relay_rows, parent_rows) + relay_rows
    picks = first + jnp.arange(relay_rows, dtype=jnp.int32)[None, :]
    stacked = jnp.take(padded, picks, axis=2, mode="clip")
    received = lax.all_to_all(stacked, "gx", split_axis=2, concat_axis=2, tiled=True)
    relay = jnp.sum(received, axis=2)

    forcing = refine(relay)
    row_global = row_rank * nest_rows + jnp.arange(nest_rows, dtype=jnp.int32)
    column_global = column_rank * nest_columns + jnp.arange(nest_columns, dtype=jnp.int32)
    weight = relax_weight(
        row_global, column_global, row_devices * nest_rows, column_devices * nest_columns
    )
    state = nest_fields
    sides = edges(state)
    for substep in range(SUBSTEPS):
        state, *sides = stencil(
            state, neighbours(sides, 3 + substep), nest_velocity, nest_mixing, forcing, weight
        )

    coarse = block_mean(state)
    fields_count, levels_count = coarse.shape[:2]
    collected = gather(coarse.reshape((-1,) + coarse.shape[2:]), "gx", 9)
    gathered = jnp.moveaxis(collected, 0, 1).reshape(
        fields_count, levels_count, row_devices * span_rows, coarse.shape[3]
    )
    total_span = row_devices * span_rows
    gathered = jnp.pad(gathered, ((0, 0), (0, 0), (parent_rows, parent_rows), (0, 0)))
    first = jnp.clip(parent_rows * row_rank - row_anchor, -parent_rows, total_span)
    strip = lax.dynamic_slice_in_dim(gathered, first + parent_rows, parent_rows, axis=2)

    routes = []
    for extra in (1, 0):
        for k in range(ratio):
            if extra == 1 and k == 0:
                continue
            pairs = [(j, p) for (p, j) in column_pairs(column_devices, base, ratio, k, extra)]
            routes.append((k, extra, pairs))
    back_branches = []
    for number, skipped in enumerate(((1, 1), (0, ratio - 1))):
        patterns = [
            (pairs, 0, slot) for slot, (k, extra, pairs) in enumerate(routes)
            if (k, extra) != (skipped[1], skipped[0])
        ]
        identity = (1, 8)[number]
        back_branches.append(
            lambda sent, patterns=patterns, identity=identity: tuple(
                exchange(sent, patterns, len(routes), "gy", identity)
            )
        )
    late = (offset > (ratio - 1) * span_columns - span_columns - 1).astype(jnp.int32)
    parts = lax.switch(late, back_branches, flat(strip)[None])
    joined = jnp.concatenate([part.reshape(strip.shape) for part in parts], axis=3)
    start = (ratio - 1) * span_columns - 1 - offset
    fed_back = lax.dynamic_slice_in_dim(joined, start, parent_columns, axis=3)

    relative_rows = row_rank * parent_rows + jnp.arange(parent_rows, dtype=jnp.int32) - row_anchor
    relative_columns = (
        column_rank * parent_columns + jnp.arange(parent_columns, dtype=jnp.int32) - column_anchor
    )
    rows_valid = within(relative_rows, total_span)
    columns_valid = within(relative_columns, column_devices * span_columns)
    covered = rows_valid[:, None] & columns_valid[None, :]
    parent_result = jnp.where(covered, fed_back, parent_next)
    return (parent_result, state)


def solution(mesh):
    placed = (
        P(None, None, "gx", "gy"),
        P(None, None, "gx", "gy"),
        P(None, "gx", "gy"),
        P(None, None, "gx", "gy"),
        P(None, None, "gx", "gy"),
        P(None, "gx", "gy"),
        P(),
    )
    return jax.shard_map(
        per_device,
        mesh=mesh,
        in_specs=placed,
        out_specs=(P(None, None, "gx", "gy"), P(None, None, "gx", "gy")),
        check_vma=False,
    )
```
